128 devices in a mesh: comp: 2 (over core), gx: 8 (over x_hi, z), gy: 8 (over x_lo, y).
Axes of the slice: x: 4 (x_hi: 2, x_lo: 2; x = x_hi * 2 + x_lo), y: 4, z: 4, core: 2. Of those that a mesh axis runs over, the one named last changes fastest.
Arguments:
- atmos_state: float32 [10, 20, 256, 1024], P(None, None, ('comp', 'gx'), 'gy'), may hold values from -6 to 6
- atmos_diffusion: float32 [10], replicated, may hold values from 0.03 to 0.12
- remap_atmos: float32 [2048, 128, 128], P(('comp', 'gx', 'gy')), may hold values from -0.1237436867076458 to 1.5237436867076457
- exchange_owner: int32 [2048, 1], P(('comp', 'gx', 'gy')), may hold values from 0 to 63; in each aligned block of 16 rows (0 to 15, 16 to 31, ...) at most 2 rows name the same one
- exchange_slot: int32 [2048], P(('comp', 'gx', 'gy')), may hold values from 0 to 15
- remap_ocean: float32 [2048, 128, 128], P(('comp', 'gx', 'gy')), may hold values from -0.1237436867076458 to 1.5237436867076457
- ocean_owner: int32 [2048, 1], P(('comp', 'gx', 'gy')), may hold values from 0 to 63; in each aligned block of 16 rows (0 to 15, 16 to 31, ...) at most 2 rows name the same one
- ocean_slot: int32 [2048], P(('comp', 'gx', 'gy')), may hold values from 0 to 63
- ocean_state: float32 [4, 8, 512, 1024], P(None, None, 'gx', 'gy'), may hold values from -6 to 6
- ocean_mixing: float32 [4], replicated, may hold values from 0.03 to 0.12
- wet_mask: int32 [512, 1024], P('gx', 'gy'), may hold values 0 or 1
Outputs:
- atmos_next: float32 [10, 20, 256, 1024], P(None, None, ('comp', 'gx'), 'gy')
- ocean_next: float32 [4, 8, 512, 1024], P(None, None, 'gx', 'gy')
- ocean_surface: float32 [4, 256, 1024], P(None, ('comp', 'gx'), 'gy')
The draws below stay inside these ranges and needn't reach their ends.
Inputs may be any that keep to these rules, and one draw needn't show every extreme that they name: `exchange_owner`: among the rows of one device, no owner appears more than 2 times, and one appears exactly 2 times. `ocean_owner`: among the rows of one device, no owner appears more than 2 times, and one appears exactly 2 times.
All inputs are finite; a program needn't handle non-finite values. No bound on the sum of `wet_mask` on one device may be relied on, other than what follows from the above.
Results may differ from the reference program's by a relative error of at most 0.000088.
Values sent between devices are 32-bit elements; how exact they have to be, the bound alone decides.
A program may use at most 128 MiB of HBM per device.

```python
import math
import jax
import jax.numpy as jnp
import numpy as np
from jax import lax

NF = 10
NO = 4
LEV = 20
OLEV = 8
TILE = 128
AX_DEV = 16
OX_DEV = 64
CAP = 2
NAX = 256
NAY = 1024
NOX = 512
NOY = 1024
NA_TILES = 2048
NO_TILES = 4096
N_GX = 8
N_GY = 8


def remap_tiles(key, count):
    diagonal_key, spread_key = jax.random.split(key)
    diagonal = jax.random.uniform(diagonal_key, (count, TILE), jnp.float32, 0.6, 1.4)
    spread = jax.random.truncated_normal(spread_key, -4.0, 4.0, (count, TILE, TILE), jnp.float32) * (0.35 / math.sqrt(TILE))
    return spread + diagonal[:, :, None] * jnp.eye(TILE, dtype=jnp.float32)[None]


def draw_remap_atmos(key, part):
    return remap_tiles(jax.random.fold_in(key, 11), NA_TILES)


def draw_remap_ocean(key, part):
    return remap_tiles(jax.random.fold_in(key, 23), NA_TILES)


def plant(drawn, stream_key, least, high):
    longest = drawn.shape.index(max(drawn.shape))
    spots = []
    for shift in (0, 1):
        where = [jax.random.randint(jax.random.fold_in(stream_key, axis), (), 0, length) for axis, length in enumerate(drawn.shape)]
        where[longest] = (where[longest] + shift) % drawn.shape[longest]
        spots.append(tuple(where))
    return drawn.at[spots[0]].set(least).at[spots[1]].set(high)


def block_levels(rng, shape, cuts, low, largest):
    level, own = 1.0, jax.random.fold_in(rng, 6)
    for axis_at, parts in cuts:
        steps = jnp.exp(jax.random.uniform(jax.random.fold_in(own, axis_at), (parts,), jnp.float32, low / len(cuts), largest / len(cuts)))
        level = level * jnp.repeat(steps, shape[axis_at] // parts).reshape([-1 if axis == axis_at else 1 for axis in range(len(shape))])
    return level


def deal_out(stream_key, own, number, rows, number_of, top, most, skew):
    ranking = jax.random.permutation(stream_key, number_of)
    crowded, ordinary = shares(number_of, rows * top, most, skew, True), shares(number_of, rows * top, most, skew, False)
    places = jnp.arange(number_of)

    def named(tallies, offset_by):
        used = int((tallies > 0).sum())
        fixed = max(1, used // 4)
        shifted = fixed + (places - fixed + offset_by * (used - fixed)) % max(1, number_of - fixed)
        return jnp.zeros((number_of,), jnp.int32).at[ranking[jnp.where(places < fixed, places, shifted)]].set(jnp.asarray(tallies, jnp.int32))

    tallies = jnp.where(number % 4 == 0, named(crowded, number // 4), named(ordinary, number - number // 4 - 1))
    mixed = jax.random.permutation(jax.random.fold_in(own, 3), number_of)
    giver, taker = mixed[0:number_of // 2 * 2:2], mixed[1:number_of // 2 * 2:2]
    slack = jnp.minimum(tallies[giver] - 1, most - tallies[taker]) // 2
    slack = jnp.where((giver == ranking[0]) | (taker == ranking[0]) | (tallies[taker] == 0), 0, jnp.maximum(slack, 0))
    shifted = jax.random.randint(jax.random.fold_in(own, 4), (number_of // 2,), 0, 1 << 20) % (slack + 1)
    tallies = tallies.at[giver].add(-shifted).at[taker].add(shifted)
    members = jnp.searchsorted(jnp.cumsum(tallies), jnp.arange(rows * top), side="right").astype(jnp.int32)
    table = members.reshape(top, rows).T
    table = table[jax.random.permutation(jax.random.fold_in(own, 1), rows)]
    offset_by = jax.random.randint(jax.random.fold_in(own, 2), (rows, 1), 0, top)
    return jnp.take_along_axis(table, (jnp.arange(top)[None, :] + offset_by) % top, axis=1)


def shares(amount, total, limit, lean, full):
    portions = [(1 << 20) // math.isqrt(standing ** lean) + 1 for standing in range(1, amount + 1)]
    largest = limit if full else min(limit, max(-(-total // amount), total * portions[0] // sum(portions)))
    least = 1 if total - largest >= amount - 1 else 0
    holding, rest = [largest] + [least] * (amount - 1), total - largest - least * (amount - 1)
    while rest > 0:
        candidates = [i for i in range(1, amount) if holding[i] < largest] or [i for i in range(1, amount) if holding[i] < limit]
        whole, left = sum([portions[i] for i in candidates]), rest
        for i in candidates:
            addition = min(limit - holding[i], max(1, left * portions[i] // whole), rest)
            holding[i] = holding[i] + addition
            rest = rest - addition
    return np.array(holding)


def centred(own_key, extent, deviation, reach, cuts=(), held_as=jnp.bfloat16):
    values = deviation * jax.random.normal(own_key, extent, jnp.float32)
    if cuts:
        values = values * block_levels(own_key, extent, cuts, -0.22, 0.18)
    return jnp.clip(values, -reach, reach).astype(held_as)


def setup_inputs(seed: int = 0) -> dict:
    seeds = jax.random.split(jax.random.key(seed), 12)
    atmos_state = centred(seeds[0], (NF, LEV, NAX, NAY), 1.0, 6.0, ((2, 16), (3, 8)), jnp.float32)
    atmos_diffusion = jnp.clip(jnp.exp(jax.random.uniform(seeds[1], (NF,), jnp.float32, math.log(0.03), math.log(0.12))), 0.03, 0.12)
    remap_atmos = draw_remap_atmos(jax.random.fold_in(seeds[11], 71), 0)
    exchange_owner_keys = jax.random.split(jax.random.fold_in(seeds[3], 1), NA_TILES // AX_DEV)
    exchange_owner_turns = jax.random.permutation(jax.random.fold_in(seeds[3], 3), NA_TILES // AX_DEV)
    exchange_owner = jax.vmap(lambda own, number: deal_out(jax.random.fold_in(seeds[3], 2), own, number, AX_DEV, N_GX * N_GY, 1, CAP, 2))(exchange_owner_keys, exchange_owner_turns).reshape((NA_TILES, 1))
    exchange_slot = plant(jax.random.randint(seeds[4], (NA_TILES,), 0, AX_DEV), jax.random.fold_in(seeds[4], 1), 0, AX_DEV - 1).astype(jnp.int32)
    remap_ocean = draw_remap_ocean(jax.random.fold_in(seeds[11], 71), 0)
    ocean_owner_keys = jax.random.split(jax.random.fold_in(seeds[6], 1), NA_TILES // AX_DEV)
    ocean_owner_turns = jax.random.permutation(jax.random.fold_in(seeds[6], 3), NA_TILES // AX_DEV)
    ocean_owner = jax.vmap(lambda own, number: deal_out(jax.random.fold_in(seeds[6], 2), own, number, AX_DEV, N_GX * N_GY, 1, CAP, 2))(ocean_owner_keys, ocean_owner_turns).reshape((NA_TILES, 1))
    ocean_slot = plant(jax.random.randint(seeds[7], (NA_TILES,), 0, OX_DEV), jax.random.fold_in(seeds[7], 1), 0, OX_DEV - 1).astype(jnp.int32)
    ocean_state = centred(seeds[8], (NO, OLEV, NOX, NOY), 1.0, 6.0, ((2, 8), (3, 8)), jnp.float32)
    ocean_mixing = jnp.clip(jnp.exp(jax.random.uniform(seeds[9], (NO,), jnp.float32, math.log(0.03), math.log(0.12))), 0.03, 0.12)
    wet_mask = plant((jax.random.randint(seeds[10], (NOX, NOY), 0, 4) < 3).astype(jnp.int32), jax.random.fold_in(seeds[10], 1), 0, 1)
    return dict(atmos_state=atmos_state, atmos_diffusion=atmos_diffusion, remap_atmos=remap_atmos, exchange_owner=exchange_owner, exchange_slot=exchange_slot, remap_ocean=remap_ocean, ocean_owner=ocean_owner, ocean_slot=ocean_slot, ocean_state=ocean_state, ocean_mixing=ocean_mixing, wet_mask=wet_mask)


HIGHEST = lax.Precision.HIGHEST
FORCING_SCALE = (0.1, -0.1, 0.1, 0.1)

def vertical_mix(state):
    upper = jnp.concatenate([state[:, :1], state[:, :-1]], axis=1)
    lower = jnp.concatenate([state[:, 1:], state[:, -1:]], axis=1)
    return upper + lower - 2.0 * state

def atmos_step(state, diffusion):
    beside = jnp.roll(state, 1, 2) + jnp.roll(state, -1, 2) + jnp.roll(state, 1, 3) + jnp.roll(state, -1, 3) - 4.0 * state
    return state + diffusion[:, None, None, None] * beside + 0.1 * vertical_mix(state)

def ocean_step(state, wet_cells, forcing, mixing):
    total = jnp.zeros_like(state)
    for axis_number, offset in ((2, 1), (2, -1), (3, 1), (3, -1)):
        nearby = jnp.roll(state, offset, axis_number)
        nearby_wet = jnp.roll(wet_cells, offset, axis_number - 2)
        total = total + nearby_wet * (nearby - state)
    tendency = mixing[:, None, None, None] * wet_cells * total + 0.1 * vertical_mix(state)
    scales = jnp.array(FORCING_SCALE, dtype=jnp.float32)
    top_level = tendency[:, :1] + scales[:, None, None, None] * forcing[:, None]
    tendency = jnp.concatenate([top_level, tendency[:, 1:]], axis=1)
    return state + wet_cells * tendency

def grid_to_tiles(grid, rows_each):
    channels, grid_rows, grid_cols = grid.shape
    blocks = grid.reshape(channels, grid_rows // rows_each, rows_each, grid_cols // TILE, TILE)
    return blocks.transpose(1, 3, 2, 0, 4).reshape(-1, channels, TILE)

def tiles_to_grid(tiles, rows_each, grid_rows, grid_cols):
    channels = tiles.shape[1]
    blocks = tiles.reshape(grid_rows // rows_each, grid_cols // TILE, rows_each, channels, TILE)
    return blocks.transpose(3, 0, 2, 1, 4).reshape(channels, grid_rows, grid_cols)

def surface_fluxes(fields):
    speed = jnp.sqrt(fields[:, 2] * fields[:, 2] + fields[:, 3] * fields[:, 3] + 0.5)
    heat_flux = speed * (fields[:, 0] - fields[:, 4]) + fields[:, 6] + fields[:, 7]
    fresh_flux = speed * fields[:, 1] + fields[:, 5] + fields[:, 8]
    east_stress = speed * fields[:, 2] * (1.0 + 0.2 * jnp.tanh(fields[:, 9]))
    north_stress = speed * fields[:, 3]
    return jnp.stack([heat_flux, fresh_flux, east_stress, north_stress], axis=1)

def reference(atmos_state, atmos_diffusion, remap_atmos, exchange_owner, exchange_slot, remap_ocean, ocean_owner, ocean_slot, ocean_state, ocean_mixing, wet_mask):
    after_first = atmos_step(atmos_state, atmos_diffusion)
    atmos_next = atmos_step(after_first, atmos_diffusion)
    surface_tiles = grid_to_tiles(after_first[:, LEV - 1], AX_DEV)
    pieces = jnp.einsum('tfc,tcd->tfd', surface_tiles, remap_atmos, precision=HIGHEST)
    section = jnp.arange(NA_TILES, dtype=jnp.int32) // (AX_DEV * N_GX * N_GY)
    exchange_index = ((section * (N_GX * N_GY) + exchange_owner[:, 0]) * AX_DEV + exchange_slot).astype(jnp.int32)
    exchange_fields = jax.ops.segment_sum(pieces, exchange_index, num_segments=NA_TILES)
    fluxes = surface_fluxes(exchange_fields)
    mapped = jnp.einsum('jgc,jcd->jgd', fluxes, remap_ocean, precision=HIGHEST)
    ocean_index = (ocean_owner[:, 0] * OX_DEV + ocean_slot).astype(jnp.int32)
    forcing_tiles = jax.ops.segment_sum(mapped, ocean_index, num_segments=NO_TILES)
    forcing = tiles_to_grid(forcing_tiles, OX_DEV, NOX, NOY)
    wet_cells = wet_mask.astype(jnp.float32)
    ocean_next = ocean_step(ocean_state, wet_cells, forcing, ocean_mixing)
    ocean_top = grid_to_tiles(ocean_next[:, 0], OX_DEV)
    on_exchange = jnp.einsum('jgc,jdc->jgd', ocean_top[ocean_index], remap_ocean, precision=HIGHEST)
    on_atmos = jnp.einsum('tgc,tdc->tgd', on_exchange[exchange_index], remap_atmos, precision=HIGHEST)
    ocean_surface = tiles_to_grid(on_atmos, AX_DEV, NAX, NAY)
    return (atmos_next, ocean_next, ocean_surface)
```

```python
import functools

import jax
import jax.numpy as jnp
from jax import lax
from jax.experimental import pallas as pl
from jax.experimental.pallas import tpu as pltpu
from jax.sharding import PartitionSpec as P

MESH = pl.DeviceIdType.MESH
F32 = jnp.float32
BF16 = jnp.bfloat16
FORCING_SCALE = (0.1, -0.1, 0.1, 0.1)

SURF, FULL, SECOND, OCEAN, COMP, A1, A2, A3, A4 = 0, 4, 8, 12, 16, 17, 18, 19, 20
SEMS = 21


def split_cat(x):
    hi = x.astype(BF16)
    lo = (x - hi.astype(F32)).astype(BF16)
    return jnp.concatenate([hi, lo], axis=1)


def split_stack(x):
    hi = x.astype(BF16).astype(F32)
    return jnp.concatenate([hi, x - hi], axis=0).astype(BF16)


def dot(a, b):
    return jnp.dot(a, b, preferred_element_type=F32)


def quad(lhs, cat):
    full = dot(lhs, cat)
    return (full[:8, :128] + full[8:, :128]) + (full[:8, 128:] + full[8:, 128:])


def halves(lhs, cat):
    full = dot(lhs, cat)
    return full[:, :128] + full[:, 128:]


def kernel(
    sizes,
    state, remap_a, remap_o, ocean, wet_in,
    diff, e_owner, e_slot, o_owner, o_slot, mixing,
    atmos_out, ocean_out, surf_out,
    S, A, N, MA, MO, MAC, MOC, MAT, MOT, O, ON, W, WN,
    rs_t, rs_b, ks, hs_a, hs_b, hs_l, hs_r,
    rf_t, rf_b, kf, hf_a, hf_b, hf_l, hf_r,
    r2_t, r2_b, k2, h2_a, h2_b, h2_l, h2_r,
    ro_t, ro_b, ko, ho_a, ho_b, ho_l, ho_r,
    X, pieces, MSG, R1, QM, PT, FL, mapped, MSG2, R2, FOR, FORIN,
    TOPC, ANS, B3, OE, OEC, REP, B4, OSV,
    tab_v, tab_s,
    in_sem, out_sem, tab_sem, send, recv,
):
    NC, NX, NY, NF, LEV, NO, OLEV = sizes
    peers = NX * NY
    comp, gx, gy = lax.axis_index("comp"), lax.axis_index("gx"), lax.axis_index("gy")
    me = gx * NY + gy
    pos = comp * NX + gx
    ring = NC * NX
    down, up = lax.rem(pos + 1, ring), lax.rem(pos + ring - 1, ring)
    dev_down = (down // NX, lax.rem(down, NX), gy)
    dev_up = (up // NX, lax.rem(up, NX), gy)
    dev_right = (comp, gx, lax.rem(gy + 1, NY))
    dev_left = (comp, gx, lax.rem(gy + NY - 1, NY))
    sea_down = (comp, lax.rem(gx + 1, NX), gy)
    sea_up = (comp, lax.rem(gx + NX - 1, NX), gy)
    twin = (lax.rem(comp + 1, NC), gx, gy)

    def peer(k):
        px = lax.rem(gx + k // NY, NX)
        py = lax.rem(gy + lax.rem(k, NY), NY)
        return px, py, px * NY + py

    barrier = pltpu.get_barrier_semaphore()

    def greet(k, carry):
        px, py, _ = peer(k)
        pl.semaphore_signal(barrier, inc=1, device_id=(comp, px, py), device_id_type=MESH)
        return carry

    lax.fori_loop(1, peers, greet, 0)
    for other in (dev_down, dev_up, twin):
        pl.semaphore_signal(barrier, inc=1, device_id=other, device_id_type=MESH)

    top_rows = 16 * (LEV - 2)
    loads = [
        pltpu.make_async_copy(state.at[:, pl.ds(top_rows, 32), :], S.at[:, pl.ds(top_rows, 32), :], in_sem.at[0]),
        pltpu.make_async_copy(state.at[:, pl.ds(0, top_rows), :], S.at[:, pl.ds(0, top_rows), :], in_sem.at[1]),
        pltpu.make_async_copy(ocean, O, in_sem.at[2]),
        pltpu.make_async_copy(wet_in, W, in_sem.at[3]),
        pltpu.make_async_copy(remap_a, MA, in_sem.at[4]),
        pltpu.make_async_copy(remap_o, MO, in_sem.at[5]),
    ]
    for load in loads:
        load.start()

    lane16 = lax.broadcasted_iota(jnp.int32, (16, 128), 1)
    row16 = lax.broadcasted_iota(jnp.int32, (16, 128), 0)
    pair16 = lane16 // 2
    even16 = lane16 == pair16 * 2
    sub8 = lax.broadcasted_iota(jnp.int32, (8, 128), 0)

    def places(owner):
        ranks, keys = [], []
        for i in range(16):
            rank = jnp.int32(0)
            for j in range(i):
                rank = rank + (owner[j, 0] == owner[i, 0]).astype(jnp.int32)
            ranks.append(rank)
            keys.append(2 * owner[i, 0] + rank)
        return ranks, keys

    e_rank, e_key = places(e_owner)
    o_rank, o_key = places(o_owner)
    lane8 = lax.broadcasted_iota(jnp.int32, (8, 128), 1)
    table = jnp.zeros((8, 128), jnp.int32)
    for i in range(16):
        table = jnp.where(lane8 == jnp.where(sub8 == 0, e_key[i], o_key[i]), i, table)
    tab_v[...] = table
    tab_copy = pltpu.make_async_copy(tab_v, tab_s, tab_sem.at[0])
    tab_copy.start()

    def remote(src, dst, number, device):
        copy = pltpu.make_async_remote_copy(
            src_ref=src, dst_ref=dst, send_sem=send.at[number], recv_sem=recv.at[number],
            device_id=device, device_id_type=MESH,
        )
        copy.start()
        return copy

    def halo(number, rows_t, rows_b, cols, from_a, from_b, from_l, from_r, below, above):
        return [
            remote(rows_b, from_a, number, below),
            remote(rows_t, from_b, number + 1, above),
            remote(cols, from_l, number + 2, dev_right),
            remote(cols, from_r, number + 3, dev_left),
        ]

    loads[0].wait()
    last = 16 * (LEV - 1)
    packed = jnp.zeros((16, 128), F32)
    for f in range(NF):
        v = S[f, pl.ds(last, 16), :]
        packed = jnp.where(pair16 == f, pltpu.roll(v, 2 * f + 1, 1), packed)
        rs_t[pl.ds(f, 1), :] = v[0:1]
        rs_b[pl.ds(f, 1), :] = v[15:16]
    ks[...] = packed
    pl.semaphore_wait(barrier, peers - 1 + 3)
    surface_halo = halo(SURF, rs_t, rs_b, ks, hs_a, hs_b, hs_l, hs_r, dev_down, dev_up)

    def pack_atmos(src, rows_t, rows_b, cols, f):
        kept = jnp.zeros((16, 128), F32)
        for lev in range(LEV):
            v = src[f, pl.ds(16 * lev, 16), :]
            kept = jnp.where(pair16 == lev, pltpu.roll(v, 2 * lev + 1, 1), kept)
        cols[f] = kept
        rows_t[f, pl.ds(0, LEV), :] = src[f, pl.ds(0, LEV, stride=16), :]
        rows_b[f, pl.ds(0, LEV), :] = src[f, pl.ds(15, LEV, stride=16), :]

    loads[1].wait()

    def pack_first(f, carry):
        pack_atmos(S, rf_t, rf_b, kf, f)
        return carry

    lax.fori_loop(0, NF, pack_first, 0)
    full_halo = halo(FULL, rf_t, rf_b, kf, hf_a, hf_b, hf_l, hf_r, dev_down, dev_up)

    loads[2].wait()
    loads[3].wait()
    planes = NO * OLEV
    lane64 = lax.broadcasted_iota(jnp.int32, (64, 128), 1)
    row64 = lax.broadcasted_iota(jnp.int32, (64, 128), 0)
    pair64 = lane64 // 2
    wet = W[...].astype(F32)
    WN[0] = wet
    kept = jnp.where(pair64 == planes, pltpu.roll(wet, 2 * planes + 1, 1), 0.0)
    ko[...] = kept
    ro_t[pl.ds(planes, 1), :] = wet[0:1]
    ro_b[pl.ds(planes, 1), :] = wet[63:64]

    def pack_ocean(f, carry):
        kept = ko[...]
        for lev in range(OLEV):
            q = f * OLEV + lev
            v = O[pl.ds(pl.multiple_of(q * 64, 64), 64), :]
            kept = jnp.where(pair64 == q, pltpu.roll(v, 2 * q + 1, 1), kept)
        ko[...] = kept
        return carry

    lax.fori_loop(0, NO, pack_ocean, 0)
    ro_t[pl.ds(0, planes), :] = O[pl.ds(0, planes, stride=64), :]
    ro_b[pl.ds(0, planes), :] = O[pl.ds(63, planes, stride=64), :]
    ocean_halo = halo(OCEAN, ro_t, ro_b, ko, ho_a, ho_b, ho_l, ho_r, sea_down, sea_up)

    r128 = lax.broadcasted_iota(jnp.int32, (128, 128), 0)
    lane128 = lax.broadcasted_iota(jnp.int32, (128, 128), 1)
    low128 = lane128 < 64
    labels = jnp.full((128, 128), -1, jnp.int32)
    for i in range(16):
        labels = jnp.where(
            r128 == jnp.where(low128, o_key[i], e_key[i]), jnp.where(low128, o_slot[i], e_slot[i]), labels
        )
    MSG[pl.ds(7, 128, stride=8), :] = labels.astype(F32)

    loads[4].wait()

    def split_a(i, carry):
        MAC[i] = split_cat(MA[i])
        return carry

    lax.fori_loop(0, 16, split_a, 0)

    tab_copy.wait()
    for copy in surface_halo:
        copy.wait_recv()
    kl, kr = hs_l[...], hs_r[...]
    cols = jnp.where(even16, kl, pltpu.roll(kr, 126, 1))
    after = []
    for f in range(NF):
        v = S[f, pl.ds(last, 16), :]
        edge = pltpu.roll(cols, (128 - 2 * f) % 128, 1)
        left = jnp.where(lane16 == 0, edge, pltpu.roll(v, 1, 1))
        right = jnp.where(lane16 == 127, edge, pltpu.roll(v, 127, 1))
        above = jnp.where(row16 == 0, hs_a[pl.ds(f, 1), :], pltpu.roll(v, 1, 0))
        below = jnp.where(row16 == 15, hs_b[pl.ds(f, 1), :], pltpu.roll(v, 15, 0))
        upper = S[f, pl.ds(last - 16, 16), :]
        after.append(v + diff[f] * (above + below + left + right - 4.0 * v) + 0.1 * (upper - v))
    combined = [after[0] - after[4], after[1], after[2], after[3], after[6] + after[7], after[5] + after[8], after[9], after[9]]
    for f in range(8):
        X[pl.ds(16 * f, 16), :] = combined[f]
    for i in range(16):
        pieces[i] = quad(split_stack(X[pl.ds(i, 8, stride=16), :]), MAC[i])

    def pack_pieces(n, carry):
        for m in range(8):
            r = n * 8 + m
            MSG[pl.ds(pl.multiple_of(r * 8, 8), 7), :] = pieces[tab_s[0, r]][0:7]
        return carry

    lax.fori_loop(0, 16, pack_pieces, 0)

    def exchange(number, rows, src, dst_of):
        def step(k, carry):
            px, py, target = peer(k)
            remote(src.at[pl.ds(pl.multiple_of(target * rows, 8), rows), :], dst_of(me), number, (comp, px, py))
            return carry

        lax.fori_loop(1, peers, step, 0)

    def arrived(number, count_ref):
        pltpu.make_async_copy(count_ref, count_ref, recv.at[number]).wait()

    def departed(number, count_ref):
        pltpu.make_async_copy(count_ref, count_ref, send.at[number]).wait()

    mine16 = pl.ds(pl.multiple_of(me * 16, 16), 16)
    mine8 = pl.ds(pl.multiple_of(me * 8, 8), 8)
    exchange(A1, 16, MSG, lambda m: R1.at[pl.ds(pl.multiple_of(m * 16, 16), 16), :])
    R1[mine16, :] = MSG[mine16, :]

    for copy in ocean_halo:
        copy.wait_recv()
    ol, orr = ho_l[...], ho_r[...]
    even64 = lane64 == pair64 * 2
    ho_l[...] = jnp.where(even64, ol, pltpu.roll(orr, 126, 1))

    def around(v, q, edges):
        edge = pltpu.roll(edges, 128 - 2 * q, 1)
        left = jnp.where(lane64 == 0, edge, pltpu.roll(v, 1, 1))
        right = jnp.where(lane64 == 127, edge, pltpu.roll(v, 127, 1))
        above = jnp.where(row64 == 0, ho_a[pl.ds(q, 1), :], pltpu.roll(v, 1, 0))
        below = jnp.where(row64 == 63, ho_b[pl.ds(q, 1), :], pltpu.roll(v, 63, 0))
        return above, below, left, right

    for n, w in enumerate(around(wet, planes, ho_l[...])):
        WN[1 + n] = w

    def sea(f, carry):
        mix = mixing[f]
        base = f * OLEV
        for lev in range(OLEV):
            q = base + lev
            v = O[pl.ds(pl.multiple_of(q * 64, 64), 64), :]
            total = jnp.zeros((64, 128), F32)
            edges = pltpu.roll(ho_l[...], 128 - 2 * q, 1)
            left = jnp.where(lane64 == 0, edges, pltpu.roll(v, 1, 1))
            right = jnp.where(lane64 == 127, edges, pltpu.roll(v, 127, 1))
            above = jnp.where(row64 == 0, ho_a[pl.ds(q, 1), :], pltpu.roll(v, 1, 0))
            below = jnp.where(row64 == 63, ho_b[pl.ds(q, 1), :], pltpu.roll(v, 63, 0))
            total = WN[1] * (above - v) + WN[2] * (below - v) + WN[3] * (left - v) + WN[4] * (right - v)
            upper = v if lev == 0 else O[pl.ds(pl.multiple_of(q * 64 - 64, 64), 64), :]
            lower = v if lev == OLEV - 1 else O[pl.ds(pl.multiple_of(q * 64 + 64, 64), 64), :]
            w = WN[0]
            ON[pl.ds(pl.multiple_of(q * 64, 64), 64), :] = v + w * (
                mix * w * total + 0.1 * (upper + lower - 2.0 * v)
            )
        return carry

    lax.fori_loop(0, NO, sea, 0)

    loads[5].wait()

    def split_o(i, carry):
        MOC[i] = split_cat(MO[i])
        MOT[i] = split_cat(jnp.transpose(MO[i]))
        MAT[i] = split_cat(jnp.transpose(MA[i]))
        return carry

    lax.fori_loop(0, 16, split_o, 0)

    arrived(A1, R1.at[pl.ds(0, 16 * (peers - 1)), :])
    chosen = (R1[pl.ds(7, 128, stride=8), :] == (lane128 - jnp.where(low128, 0, 64)).astype(F32)).astype(F32)
    QM[...] = chosen.astype(BF16)
    PT[...] = jnp.transpose(chosen).astype(BF16)
    fields = [halves(PT[pl.ds(64, 16), :], split_cat(R1[pl.ds(f, 128, stride=8), :])) for f in range(7)]
    heat, salt, east, north, gain, fresh, shape = fields
    speed = jnp.sqrt(east * east + north * north + 0.5)
    flux = [
        speed * heat + gain,
        speed * salt + fresh,
        speed * east * (1.0 + 0.2 * jnp.tanh(shape)),
        speed * north,
    ]
    for g in range(8):
        FL[pl.ds(16 * g, 16), :] = flux[g % 4]
    for j in range(16):
        mapped[j] = quad(split_stack(FL[pl.ds(j, 8, stride=16), :]), MOC[j])

    def pack_mapped(n, carry):
        for m in range(8):
            t = n * 8 + m
            MSG2[pl.ds(pl.multiple_of(t * 8, 8), 8), :] = jnp.where(
                sub8 < 4, mapped[tab_s[1, 2 * t]], mapped[tab_s[1, 2 * t + 1]]
            )
        return carry

    lax.fori_loop(0, peers // 8, pack_mapped, 0)
    exchange(A2, 8, MSG2, lambda m: R2.at[pl.ds(pl.multiple_of(m * 8, 8), 8), :])
    R2[mine8, :] = MSG2[mine8, :]

    for copy in full_halo:
        copy.wait_recv()

    def atmos_field(src, dst, from_a, from_b, from_l, from_r, f):
        d = diff[f]
        both = jnp.where(even16, from_l[f], pltpu.roll(from_r[f], 126, 1))
        for lev in range(LEV):
            v = src[f, pl.ds(16 * lev, 16), :]
            edge = pltpu.roll(both, (128 - 2 * lev) % 128, 1)
            left = jnp.where(lane16 == 0, edge, pltpu.roll(v, 1, 1))
            right = jnp.where(lane16 == 127, edge, pltpu.roll(v, 127, 1))
            above = jnp.where(row16 == 0, from_a[f, pl.ds(lev, 1), :], pltpu.roll(v, 1, 0))
            below = jnp.where(row16 == 15, from_b[f, pl.ds(lev, 1), :], pltpu.roll(v, 15, 0))
            upper = v if lev == 0 else src[f, pl.ds(16 * lev - 16, 16), :]
            lower = v if lev == LEV - 1 else src[f, pl.ds(16 * lev + 16, 16), :]
            dst[f, pl.ds(16 * lev, 16), :] = (
                v + d * (above + below + left + right - 4.0 * v) + 0.1 * (upper + lower - 2.0 * v)
            )

    def first_step(f, carry):
        atmos_field(S, A, hf_a, hf_b, hf_l, hf_r, f)
        pack_atmos(A, r2_t, r2_b, k2, f)
        return carry

    lax.fori_loop(0, NF, first_step, 0)
    second_halo = halo(SECOND, r2_t, r2_b, k2, h2_a, h2_b, h2_l, h2_r, dev_down, dev_up)

    arrived(A2, R2.at[pl.ds(0, 8 * (peers - 1)), :])
    for g in range(NO):
        FOR[pl.ds(64 * g, 64), :] = halves(PT[pl.ds(0, 64), :], split_cat(R2[pl.ds(g, 128, stride=4), :]))
    twin_copy = remote(FOR, FORIN, COMP, twin)
    zero64 = jnp.zeros((64, 256), BF16)
    for g in range(NO):
        TOPC[g, pl.ds(64, 64), :] = zero64
        OEC[g, pl.ds(0, 64), :] = zero64
        OEC[g, pl.ds(64, 64), :] = zero64
    twin_copy.wait_recv()
    for g in range(NO):
        rows = pl.ds(64 * OLEV * g, 64)
        plane = pl.ds(64 * g, 64)
        top = ON[rows, :] + WN[0] * (FORCING_SCALE[g] * (FOR[plane, :] + FORIN[plane, :]))
        ON[rows, :] = top
        TOPC[g, pl.ds(0, 64), :] = split_cat(top)
    for g in range(NO):
        ANS[pl.ds(g, 128, stride=4), :] = halves(QM[...], TOPC[g])
    exchange(A3, 8, ANS, lambda m: B3.at[m])
    B3[me] = ANS[mine8, :]
    ocean_store = pltpu.make_async_copy(ON, ocean_out, out_sem.at[0])
    ocean_store.start()

    for copy in second_halo:
        copy.wait_recv()

    def second_step(f, carry):
        atmos_field(A, N, h2_a, h2_b, h2_l, h2_r, f)
        return carry

    lax.fori_loop(0, NF, second_step, 0)
    atmos_store = pltpu.make_async_copy(N, atmos_out, out_sem.at[1])
    atmos_store.start()

    b3_all = B3.at[pl.ds(0, peers - 1)]
    arrived(A3, b3_all)
    for j in range(16):
        both = quad(split_stack(B3[o_owner[j, 0]]), MOT[j])
        picked = jnp.where(o_rank[j] == 0, both, pltpu.roll(both, 4, 0))
        OE[pl.ds(j, 4, stride=16), :] = picked[0:4]
    for g in range(NO):
        OEC[g, pl.ds(64, 16), :] = split_cat(OE[pl.ds(16 * g, 16), :])
    for g in range(NO):
        REP[pl.ds(g, 128, stride=4), :] = halves(QM[...], OEC[g])
    exchange(A4, 8, REP, lambda m: B4.at[m])
    B4[me] = REP[mine8, :]

    arrived(A4, B4.at[pl.ds(0, peers - 1)])
    for i in range(16):
        both = quad(split_stack(B4[e_owner[i, 0]]), MAT[i])
        picked = jnp.where(e_rank[i] == 0, both, pltpu.roll(both, 4, 0))
        OSV[pl.ds(i, 4, stride=16), :] = picked[0:4]
    surf_store = pltpu.make_async_copy(OSV, surf_out, out_sem.at[2])
    surf_store.start()

    for copy in surface_halo + full_halo + ocean_halo + second_halo + [twin_copy]:
        copy.wait_send()
    departed(A1, MSG.at[pl.ds(0, 16 * (peers - 1)), :])
    departed(A2, MSG2.at[pl.ds(0, 8 * (peers - 1)), :])
    departed(A3, ANS.at[pl.ds(0, 8 * (peers - 1)), :])
    departed(A4, REP.at[pl.ds(0, 8 * (peers - 1)), :])
    ocean_store.wait()
    atmos_store.wait()
    surf_store.wait()


def on_device(
    sizes,
    atmos_state, atmos_diffusion, remap_atmos, exchange_owner, exchange_slot,
    remap_ocean, ocean_owner, ocean_slot, ocean_state, ocean_mixing, wet_mask,
):
    NC, NX, NY, NF, LEV, NO, OLEV = sizes
    peers = NX * NY
    any_ = pl.BlockSpec(memory_space=pl.ANY)
    smem = pl.BlockSpec(memory_space=pltpu.SMEM)

    def vm(*shape, dtype=F32):
        return pltpu.VMEM(shape, dtype)

    halo_atmos = [vm(NF, 24, 128), vm(NF, 24, 128), vm(NF, 16, 128), vm(NF, 24, 128), vm(NF, 24, 128), vm(NF, 16, 128), vm(NF, 16, 128)]
    scratch = (
        [vm(NF, 16 * LEV, 128) for _ in range(3)]
        + [vm(16, 128, 128), vm(16, 128, 128)]
        + [vm(16, 128, 256, dtype=BF16) for _ in range(4)]
        + [vm(NO * OLEV * 64, 128), vm(NO * OLEV * 64, 128), vm(64, 128, dtype=jnp.int32), vm(5, 64, 128)]
        + [vm(16, 128) for _ in range(7)]
        + halo_atmos
        + halo_atmos
        + [vm(40, 128), vm(40, 128), vm(64, 128), vm(40, 128), vm(40, 128), vm(64, 128), vm(64, 128)]
        + [vm(128, 128), vm(16, 8, 128), vm(16 * peers, 128), vm(16 * peers, 128)]
        + [vm(128, 128, dtype=BF16), vm(128, 128, dtype=BF16), vm(128, 128), vm(16, 8, 128)]
        + [vm(8 * peers, 128), vm(8 * peers, 128), vm(256, 128), vm(256, 128)]
        + [vm(NO, 128, 256, dtype=BF16), vm(8 * peers, 128), vm(peers, 8, 128), vm(64, 128)]
        + [vm(NO, 128, 256, dtype=BF16), vm(8 * peers, 128), vm(peers, 8, 128), vm(64, 128)]
        + [vm(8, 128, dtype=jnp.int32), pltpu.SMEM((8, 128), jnp.int32)]
        + [
            pltpu.SemaphoreType.DMA((6,)),
            pltpu.SemaphoreType.DMA((3,)),
            pltpu.SemaphoreType.DMA((1,)),
            pltpu.SemaphoreType.DMA((SEMS,)),
            pltpu.SemaphoreType.DMA((SEMS,)),
        ]
    )
    atmos_next, ocean_next, surface = pl.pallas_call(
        functools.partial(kernel, sizes),
        out_shape=(
            jax.ShapeDtypeStruct((NF, 16 * LEV, 128), F32),
            jax.ShapeDtypeStruct((NO * OLEV * 64, 128), F32),
            jax.ShapeDtypeStruct((64, 128), F32),
        ),
        in_specs=[any_] * 5 + [smem] * 6,
        out_specs=(any_, any_, any_),
        scratch_shapes=scratch,
        compiler_params=pltpu.CompilerParams(
            collective_id=0, has_side_effects=True, vmem_limit_bytes=40 * 1024 * 1024
        ),
    )(
        atmos_state.reshape(NF, 16 * LEV, 128),
        remap_atmos,
        remap_ocean,
        ocean_state.reshape(NO * OLEV * 64, 128),
        wet_mask,
        atmos_diffusion, exchange_owner, exchange_slot, ocean_owner, ocean_slot, ocean_mixing,
    )
    return (
        atmos_next.reshape(NF, LEV, 16, 128),
        ocean_next.reshape(NO, OLEV, 64, 128),
        surface.reshape(NO, 16, 128),
    )


def solution(mesh):
    sizes = (mesh.shape["comp"], mesh.shape["gx"], mesh.shape["gy"], 10, 20, 4, 8)
    in_specs = (
        P(None, None, ("comp", "gx"), "gy"),
        P(),
        P(("comp", "gx", "gy"), None, None),
        P(("comp", "gx", "gy"), None),
        P(("comp", "gx", "gy")),
        P(("comp", "gx", "gy"), None, None),
        P(("comp", "gx", "gy"), None),
        P(("comp", "gx", "gy")),
        P(None, None, "gx", "gy"),
        P(),
        P("gx", "gy"),
    )
    out_specs = (
        P(None, None, ("comp", "gx"), "gy"),
        P(None, None, "gx", "gy"),
        P(None, ("comp", "gx"), "gy"),
    )
    return jax.shard_map(
        functools.partial(on_device, sizes), mesh=mesh, in_specs=in_specs, out_specs=out_specs, check_vma=False
    )
```

```python
import functools

import jax
import jax.numpy as jnp
from jax import lax
from jax.experimental import pallas as pl
from jax.experimental.pallas import tpu as pltpu
from jax.sharding import PartitionSpec as P

MESH = pl.DeviceIdType.MESH
F32 = jnp.float32
BF16 = jnp.bfloat16
FORCING_SCALE = (0.1, -0.1, 0.1, 0.1)

SURF, FULL, SECOND, OCEAN, COMP, A1, A2, A3, A4 = 0, 4, 8, 12, 16, 17, 18, 19, 20
SEMS = 21


def split_cat(x):
    hi = x.astype(BF16)
    lo = (x - hi.astype(F32)).astype(BF16)
    return jnp.concatenate([hi, lo], axis=1)


def split_stack(x):
    hi = x.astype(BF16).astype(F32)
    return jnp.concatenate([hi, x - hi], axis=0).astype(BF16)


def dot(a, b):
    return jnp.dot(a, b, preferred_element_type=F32)


def quad(lhs, cat):
    full = dot(lhs, cat)
    return (full[:8, :128] + full[8:, :128]) + (full[:8, 128:] + full[8:, 128:])


def halves(lhs, cat):
    full = dot(lhs, cat)
    return full[:, :128] + full[:, 128:]


def kernel(
    sizes,
    state, remap_a, remap_o, ocean, wet_in,
    diff_in, e_owner_in, e_slot_in, o_owner_in, o_slot_in, mixing_in,
    atmos_out, ocean_out, surf_out,
    S, A, N, MA, MO, MAC, MOC, MAT, MOT, O, ON, W, WN,
    rs_t, rs_b, ks, hs_a, hs_b, hs_l, hs_r,
    rf_t, rf_b, kf, hf_a, hf_b, hf_l, hf_r,
    r2_t, r2_b, k2, h2_a, h2_b, h2_l, h2_r,
    ro_t, ro_b, ko, ho_a, ho_b, ho_l, ho_r,
    X, pieces, MSG, R1, QM, PT, FL, mapped, MSG2, R2, FOR, FORIN,
    TOPC, ANS, B3, OE, OEC, REP, B4, OSV,
    diff, e_owner, e_slot, o_owner, o_slot, mixing,
    tab_v, tab_s,
    in_sem, out_sem, tab_sem, send, recv,
):
    NC, NX, NY, NF, LEV, NO, OLEV = sizes
    peers = NX * NY
    comp, gx, gy = lax.axis_index("comp"), lax.axis_index("gx"), lax.axis_index("gy")
    me = gx * NY + gy
    pos = comp * NX + gx
    ring = NC * NX
    down, up = lax.rem(pos + 1, ring), lax.rem(pos + ring - 1, ring)
    dev_down = (down // NX, lax.rem(down, NX), gy)
    dev_up = (up // NX, lax.rem(up, NX), gy)
    dev_right = (comp, gx, lax.rem(gy + 1, NY))
    dev_left = (comp, gx, lax.rem(gy + NY - 1, NY))
    sea_down = (comp, lax.rem(gx + 1, NX), gy)
    sea_up = (comp, lax.rem(gx + NX - 1, NX), gy)
    twin = (lax.rem(comp + 1, NC), gx, gy)

    def peer(k):
        px = lax.rem(gx + k // NY, NX)
        py = lax.rem(gy + lax.rem(k, NY), NY)
        return px, py, px * NY + py

    barrier = pltpu.get_barrier_semaphore()

    def greet(k, carry):
        px, py, _ = peer(k)
        pl.semaphore_signal(barrier, inc=1, device_id=(comp, px, py), device_id_type=MESH)
        return carry

    lax.fori_loop(1, peers, greet, 0)
    for other in (dev_down, dev_up, twin):
        pl.semaphore_signal(barrier, inc=1, device_id=other, device_id_type=MESH)

    top_rows = 16 * (LEV - 2)
    loads = [
        pltpu.make_async_copy(state.at[:, pl.ds(top_rows, 32), :], S.at[:, pl.ds(top_rows, 32), :], in_sem.at[0]),
        pltpu.make_async_copy(state.at[:, pl.ds(0, top_rows), :], S.at[:, pl.ds(0, top_rows), :], in_sem.at[1]),
        pltpu.make_async_copy(ocean, O, in_sem.at[2]),
        pltpu.make_async_copy(wet_in, W, in_sem.at[3]),
        pltpu.make_async_copy(remap_a, MA, in_sem.at[4]),
        pltpu.make_async_copy(remap_o, MO, in_sem.at[5]),
    ]
    small = [
        pltpu.make_async_copy(src, dst, in_sem.at[6 + n])
        for n, (src, dst) in enumerate([
            (e_owner_in, e_owner), (o_owner_in, o_owner), (e_slot_in, e_slot), (o_slot_in, o_slot),
            (diff_in, diff), (mixing_in, mixing),
        ])
    ]
    for load in small + loads:
        load.start()

    lane16 = lax.broadcasted_iota(jnp.int32, (16, 128), 1)
    row16 = lax.broadcasted_iota(jnp.int32, (16, 128), 0)
    pair16 = lane16 // 2
    even16 = lane16 == pair16 * 2
    sub8 = lax.broadcasted_iota(jnp.int32, (8, 128), 0)

    def remote(src, dst, number, device):
        copy = pltpu.make_async_remote_copy(
            src_ref=src, dst_ref=dst, send_sem=send.at[number], recv_sem=recv.at[number],
            device_id=device, device_id_type=MESH,
        )
        copy.start()
        return copy

    def halo(number, rows_t, rows_b, cols, from_a, from_b, from_l, from_r, below, above):
        return [
            remote(rows_b, from_a, number, below),
            remote(rows_t, from_b, number + 1, above),
            remote(cols, from_l, number + 2, dev_right),
            remote(cols, from_r, number + 3, dev_left),
        ]

    loads[0].wait()
    last = 16 * (LEV - 1)
    packed = jnp.zeros((16, 128), F32)
    for f in range(NF):
        v = S[f, pl.ds(last, 16), :]
        packed = jnp.where(pair16 == f, pltpu.roll(v, 2 * f + 1, 1), packed)
        rs_t[pl.ds(f, 1), :] = v[0:1]
        rs_b[pl.ds(f, 1), :] = v[15:16]
    ks[...] = packed
    pl.semaphore_wait(barrier, peers - 1 + 3)
    surface_halo = halo(SURF, rs_t, rs_b, ks, hs_a, hs_b, hs_l, hs_r, dev_down, dev_up)

    def places(owner):
        ranks, keys = [], []
        for i in range(16):
            rank = jnp.int32(0)
            for j in range(i):
                rank = rank + (owner[j] == owner[i]).astype(jnp.int32)
            ranks.append(rank)
            keys.append(2 * owner[i] + rank)
        return ranks, keys

    for load in small:
        load.wait()
    e_rank, e_key = places(e_owner)
    o_rank, o_key = places(o_owner)
    lane8 = lax.broadcasted_iota(jnp.int32, (8, 128), 1)
    table = jnp.zeros((8, 128), jnp.int32)
    for i in range(16):
        table = jnp.where(lane8 == jnp.where(sub8 == 0, e_key[i], o_key[i]), i, table)
    tab_v[...] = table
    tab_copy = pltpu.make_async_copy(tab_v, tab_s, tab_sem.at[0])
    tab_copy.start()

    def pack_atmos(src, rows_t, rows_b, cols, f):
        kept = jnp.zeros((16, 128), F32)
        for lev in range(LEV):
            v = src[f, pl.ds(16 * lev, 16), :]
            kept = jnp.where(pair16 == lev, pltpu.roll(v, 2 * lev + 1, 1), kept)
        cols[f] = kept
        rows_t[f, pl.ds(0, LEV), :] = src[f, pl.ds(0, LEV, stride=16), :]
        rows_b[f, pl.ds(0, LEV), :] = src[f, pl.ds(15, LEV, stride=16), :]

    loads[1].wait()

    def pack_first(f, carry):
        pack_atmos(S, rf_t, rf_b, kf, f)
        return carry

    lax.fori_loop(0, NF, pack_first, 0)
    full_halo = halo(FULL, rf_t, rf_b, kf, hf_a, hf_b, hf_l, hf_r, dev_down, dev_up)

    loads[2].wait()
    loads[3].wait()
    planes = NO * OLEV
    lane64 = lax.broadcasted_iota(jnp.int32, (64, 128), 1)
    row64 = lax.broadcasted_iota(jnp.int32, (64, 128), 0)
    pair64 = lane64 // 2
    wet = W[...].astype(F32)
    WN[0] = wet
    kept = jnp.where(pair64 == planes, pltpu.roll(wet, 2 * planes + 1, 1), 0.0)
    ko[...] = kept
    ro_t[pl.ds(planes, 1), :] = wet[0:1]
    ro_b[pl.ds(planes, 1), :] = wet[63:64]

    def pack_ocean(f, carry):
        kept = ko[...]
        for lev in range(OLEV):
            q = f * OLEV + lev
            v = O[pl.ds(pl.multiple_of(q * 64, 64), 64), :]
            kept = jnp.where(pair64 == q, pltpu.roll(v, 2 * q + 1, 1), kept)
        ko[...] = kept
        return carry

    lax.fori_loop(0, NO, pack_ocean, 0)
    ro_t[pl.ds(0, planes), :] = O[pl.ds(0, planes, stride=64), :]
    ro_b[pl.ds(0, planes), :] = O[pl.ds(63, planes, stride=64), :]
    ocean_halo = halo(OCEAN, ro_t, ro_b, ko, ho_a, ho_b, ho_l, ho_r, sea_down, sea_up)

    r128 = lax.broadcasted_iota(jnp.int32, (128, 128), 0)
    lane128 = lax.broadcasted_iota(jnp.int32, (128, 128), 1)
    low128 = lane128 < 64
    labels = jnp.full((128, 128), -1, jnp.int32)
    for i in range(16):
        labels = jnp.where(
            r128 == jnp.where(low128, o_key[i], e_key[i]), jnp.where(low128, o_slot[i], e_slot[i]), labels
        )
    MSG[pl.ds(7, 128, stride=8), :] = labels.astype(F32)

    loads[4].wait()

    def split_a(i, carry):
        MAC[i] = split_cat(MA[i])
        return carry

    lax.fori_loop(0, 16, split_a, 0)

    tab_copy.wait()
    for copy in surface_halo:
        copy.wait_recv()
    kl, kr = hs_l[...], hs_r[...]
    cols = jnp.where(even16, kl, pltpu.roll(kr, 126, 1))
    after = []
    for f in range(NF):
        v = S[f, pl.ds(last, 16), :]
        edge = pltpu.roll(cols, (128 - 2 * f) % 128, 1)
        left = jnp.where(lane16 == 0, edge, pltpu.roll(v, 1, 1))
        right = jnp.where(lane16 == 127, edge, pltpu.roll(v, 127, 1))
        above = jnp.where(row16 == 0, hs_a[pl.ds(f, 1), :], pltpu.roll(v, 1, 0))
        below = jnp.where(row16 == 15, hs_b[pl.ds(f, 1), :], pltpu.roll(v, 15, 0))
        upper = S[f, pl.ds(last - 16, 16), :]
        after.append(v + diff[f] * (above + below + left + right - 4.0 * v) + 0.1 * (upper - v))
    combined = [after[0] - after[4], after[1], after[2], after[3], after[6] + after[7], after[5] + after[8], after[9], after[9]]
    for f in range(8):
        X[pl.ds(16 * f, 16), :] = combined[f]
    for i in range(16):
        pieces[i] = quad(split_stack(X[pl.ds(i, 8, stride=16), :]), MAC[i])

    def pack_pieces(n, carry):
        for m in range(8):
            r = n * 8 + m
            MSG[pl.ds(pl.multiple_of(r * 8, 8), 7), :] = pieces[tab_s[0, r]][0:7]
        return carry

    lax.fori_loop(0, 16, pack_pieces, 0)

    def exchange(number, rows, src, dst_of):
        def step(k, carry):
            px, py, target = peer(k)
            remote(src.at[pl.ds(pl.multiple_of(target * rows, 8), rows), :], dst_of(me), number, (comp, px, py))
            return carry

        lax.fori_loop(1, peers, step, 0)

    def arrived(number, count_ref):
        pltpu.make_async_copy(count_ref, count_ref, recv.at[number]).wait()

    def departed(number, count_ref):
        pltpu.make_async_copy(count_ref, count_ref, send.at[number]).wait()

    mine16 = pl.ds(pl.multiple_of(me * 16, 16), 16)
    mine8 = pl.ds(pl.multiple_of(me * 8, 8), 8)
    exchange(A1, 16, MSG, lambda m: R1.at[pl.ds(pl.multiple_of(m * 16, 16), 16), :])
    R1[mine16, :] = MSG[mine16, :]

    for copy in ocean_halo:
        copy.wait_recv()
    ol, orr = ho_l[...], ho_r[...]
    even64 = lane64 == pair64 * 2
    ho_l[...] = jnp.where(even64, ol, pltpu.roll(orr, 126, 1))

    def around(v, q, edges):
        edge = pltpu.roll(edges, 128 - 2 * q, 1)
        left = jnp.where(lane64 == 0, edge, pltpu.roll(v, 1, 1))
        right = jnp.where(lane64 == 127, edge, pltpu.roll(v, 127, 1))
        above = jnp.where(row64 == 0, ho_a[pl.ds(q, 1), :], pltpu.roll(v, 1, 0))
        below = jnp.where(row64 == 63, ho_b[pl.ds(q, 1), :], pltpu.roll(v, 63, 0))
        return above, below, left, right

    for n, w in enumerate(around(wet, planes, ho_l[...])):
        WN[1 + n] = w

    def sea(f, carry):
        mix = mixing[f]
        base = f * OLEV
        for lev in range(OLEV):
            q = base + lev
            v = O[pl.ds(pl.multiple_of(q * 64, 64), 64), :]
            total = jnp.zeros((64, 128), F32)
            edges = pltpu.roll(ho_l[...], 128 - 2 * q, 1)
            left = jnp.where(lane64 == 0, edges, pltpu.roll(v, 1, 1))
            right = jnp.where(lane64 == 127, edges, pltpu.roll(v, 127, 1))
            above = jnp.where(row64 == 0, ho_a[pl.ds(q, 1), :], pltpu.roll(v, 1, 0))
            below = jnp.where(row64 == 63, ho_b[pl.ds(q, 1), :], pltpu.roll(v, 63, 0))
            total = WN[1] * (above - v) + WN[2] * (below - v) + WN[3] * (left - v) + WN[4] * (right - v)
            upper = v if lev == 0 else O[pl.ds(pl.multiple_of(q * 64 - 64, 64), 64), :]
            lower = v if lev == OLEV - 1 else O[pl.ds(pl.multiple_of(q * 64 + 64, 64), 64), :]
            w = WN[0]
            ON[pl.ds(pl.multiple_of(q * 64, 64), 64), :] = v + w * (
                mix * w * total + 0.1 * (upper + lower - 2.0 * v)
            )
        return carry

    lax.fori_loop(0, NO, sea, 0)

    loads[5].wait()

    def split_o(i, carry):
        MOC[i] = split_cat(MO[i])
        MOT[i] = split_cat(jnp.transpose(MO[i]))
        MAT[i] = split_cat(jnp.transpose(MA[i]))
        return carry

    lax.fori_loop(0, 16, split_o, 0)

    arrived(A1, R1.at[pl.ds(0, 16 * (peers - 1)), :])
    chosen = (R1[pl.ds(7, 128, stride=8), :] == (lane128 - jnp.where(low128, 0, 64)).astype(F32)).astype(F32)
    QM[...] = chosen.astype(BF16)
    PT[...] = jnp.transpose(chosen).astype(BF16)
    fields = [halves(PT[pl.ds(64, 16), :], split_cat(R1[pl.ds(f, 128, stride=8), :])) for f in range(7)]
    heat, salt, east, north, gain, fresh, shape = fields
    speed = jnp.sqrt(east * east + north * north + 0.5)
    flux = [
        speed * heat + gain,
        speed * salt + fresh,
        speed * east * (1.0 + 0.2 * jnp.tanh(shape)),
        speed * north,
    ]
    for g in range(8):
        FL[pl.ds(16 * g, 16), :] = flux[g % 4]
    for j in range(16):
        mapped[j] = quad(split_stack(FL[pl.ds(j, 8, stride=16), :]), MOC[j])

    def pack_mapped(n, carry):
        for m in range(8):
            t = n * 8 + m
            MSG2[pl.ds(pl.multiple_of(t * 8, 8), 8), :] = jnp.where(
                sub8 < 4, mapped[tab_s[1, 2 * t]], mapped[tab_s[1, 2 * t + 1]]
            )
        return carry

    lax.fori_loop(0, peers // 8, pack_mapped, 0)
    exchange(A2, 8, MSG2, lambda m: R2.at[pl.ds(pl.multiple_of(m * 8, 8), 8), :])
    R2[mine8, :] = MSG2[mine8, :]

    for copy in full_halo:
        copy.wait_recv()

    def atmos_field(src, dst, from_a, from_b, from_l, from_r, f):
        d = diff[f]
        both = jnp.where(even16, from_l[f], pltpu.roll(from_r[f], 126, 1))
        for lev in range(LEV):
            v = src[f, pl.ds(16 * lev, 16), :]
            edge = pltpu.roll(both, (128 - 2 * lev) % 128, 1)
            left = jnp.where(lane16 == 0, edge, pltpu.roll(v, 1, 1))
            right = jnp.where(lane16 == 127, edge, pltpu.roll(v, 127, 1))
            above = jnp.where(row16 == 0, from_a[f, pl.ds(lev, 1), :], pltpu.roll(v, 1, 0))
            below = jnp.where(row16 == 15, from_b[f, pl.ds(lev, 1), :], pltpu.roll(v, 15, 0))
            upper = v if lev == 0 else src[f, pl.ds(16 * lev - 16, 16), :]
            lower = v if lev == LEV - 1 else src[f, pl.ds(16 * lev + 16, 16), :]
            dst[f, pl.ds(16 * lev, 16), :] = (
                v + d * (above + below + left + right - 4.0 * v) + 0.1 * (upper + lower - 2.0 * v)
            )

    def first_step(f, carry):
        atmos_field(S, A, hf_a, hf_b, hf_l, hf_r, f)
        pack_atmos(A, r2_t, r2_b, k2, f)
        return carry

    lax.fori_loop(0, NF, first_step, 0)
    second_halo = halo(SECOND, r2_t, r2_b, k2, h2_a, h2_b, h2_l, h2_r, dev_down, dev_up)

    arrived(A2, R2.at[pl.ds(0, 8 * (peers - 1)), :])
    for g in range(NO):
        FOR[pl.ds(64 * g, 64), :] = halves(PT[pl.ds(0, 64), :], split_cat(R2[pl.ds(g, 128, stride=4), :]))
    twin_copy = remote(FOR, FORIN, COMP, twin)
    zero64 = jnp.zeros((64, 256), BF16)
    for g in range(NO):
        TOPC[g, pl.ds(64, 64), :] = zero64
        OEC[g, pl.ds(0, 64), :] = zero64
        OEC[g, pl.ds(64, 64), :] = zero64
    twin_copy.wait_recv()
    for g in range(NO):
        rows = pl.ds(64 * OLEV * g, 64)
        plane = pl.ds(64 * g, 64)
        top = ON[rows, :] + WN[0] * (FORCING_SCALE[g] * (FOR[plane, :] + FORIN[plane, :]))
        ON[rows, :] = top
        TOPC[g, pl.ds(0, 64), :] = split_cat(top)
    for g in range(NO):
        ANS[pl.ds(g, 128, stride=4), :] = halves(QM[...], TOPC[g])
    exchange(A3, 8, ANS, lambda m: B3.at[m])
    B3[me] = ANS[mine8, :]
    ocean_store = pltpu.make_async_copy(ON, ocean_out, out_sem.at[0])
    ocean_store.start()

    for copy in second_halo:
        copy.wait_recv()

    def second_step(f, carry):
        atmos_field(A, N, h2_a, h2_b, h2_l, h2_r, f)
        return carry

    lax.fori_loop(0, NF, second_step, 0)
    atmos_store = pltpu.make_async_copy(N, atmos_out, out_sem.at[1])
    atmos_store.start()

    b3_all = B3.at[pl.ds(0, peers - 1)]
    arrived(A3, b3_all)
    for j in range(16):
        both = quad(split_stack(B3[o_owner[j]]), MOT[j])
        picked = jnp.where(o_rank[j] == 0, both, pltpu.roll(both, 4, 0))
        OE[pl.ds(j, 4, stride=16), :] = picked[0:4]
    for g in range(NO):
        OEC[g, pl.ds(64, 16), :] = split_cat(OE[pl.ds(16 * g, 16), :])
    for g in range(NO):
        REP[pl.ds(g, 128, stride=4), :] = halves(QM[...], OEC[g])
    exchange(A4, 8, REP, lambda m: B4.at[m])
    B4[me] = REP[mine8, :]

    arrived(A4, B4.at[pl.ds(0, peers - 1)])
    for i in range(16):
        both = quad(split_stack(B4[e_owner[i]]), MAT[i])
        picked = jnp.where(e_rank[i] == 0, both, pltpu.roll(both, 4, 0))
        OSV[pl.ds(i, 4, stride=16), :] = picked[0:4]
    surf_store = pltpu.make_async_copy(OSV, surf_out, out_sem.at[2])
    surf_store.start()

    for copy in surface_halo + full_halo + ocean_halo + second_halo + [twin_copy]:
        copy.wait_send()
    departed(A1, MSG.at[pl.ds(0, 16 * (peers - 1)), :])
    departed(A2, MSG2.at[pl.ds(0, 8 * (peers - 1)), :])
    departed(A3, ANS.at[pl.ds(0, 8 * (peers - 1)), :])
    departed(A4, REP.at[pl.ds(0, 8 * (peers - 1)), :])
    ocean_store.wait()
    atmos_store.wait()
    surf_store.wait()


def on_device(
    sizes,
    atmos_state, atmos_diffusion, remap_atmos, exchange_owner, exchange_slot,
    remap_ocean, ocean_owner, ocean_slot, ocean_state, ocean_mixing, wet_mask,
):
    NC, NX, NY, NF, LEV, NO, OLEV = sizes
    peers = NX * NY
    hbm = pl.BlockSpec(memory_space=pltpu.HBM)

    def vm(*shape, dtype=F32):
        return pltpu.VMEM(shape, dtype)

    halo_atmos = [vm(NF, 24, 128), vm(NF, 24, 128), vm(NF, 16, 128), vm(NF, 24, 128), vm(NF, 24, 128), vm(NF, 16, 128), vm(NF, 16, 128)]
    scratch = (
        [vm(NF, 16 * LEV, 128) for _ in range(3)]
        + [vm(16, 128, 128), vm(16, 128, 128)]
        + [vm(16, 128, 256, dtype=BF16) for _ in range(4)]
        + [vm(NO * OLEV * 64, 128), vm(NO * OLEV * 64, 128), vm(64, 128, dtype=jnp.int32), vm(5, 64, 128)]
        + [vm(16, 128) for _ in range(7)]
        + halo_atmos
        + halo_atmos
        + [vm(40, 128), vm(40, 128), vm(64, 128), vm(40, 128), vm(40, 128), vm(64, 128), vm(64, 128)]
        + [vm(128, 128), vm(16, 8, 128), vm(16 * peers, 128), vm(16 * peers, 128)]
        + [vm(128, 128, dtype=BF16), vm(128, 128, dtype=BF16), vm(128, 128), vm(16, 8, 128)]
        + [vm(8 * peers, 128), vm(8 * peers, 128), vm(256, 128), vm(256, 128)]
        + [vm(NO, 128, 256, dtype=BF16), vm(8 * peers, 128), vm(peers, 8, 128), vm(64, 128)]
        + [vm(NO, 128, 256, dtype=BF16), vm(8 * peers, 128), vm(peers, 8, 128), vm(64, 128)]
        + [pltpu.SMEM((NF,), F32)] + [pltpu.SMEM((16,), jnp.int32) for _ in range(4)] + [pltpu.SMEM((NO,), F32)]
        + [vm(8, 128, dtype=jnp.int32), pltpu.SMEM((8, 128), jnp.int32)]
        + [
            pltpu.SemaphoreType.DMA((12,)),
            pltpu.SemaphoreType.DMA((3,)),
            pltpu.SemaphoreType.DMA((1,)),
            pltpu.SemaphoreType.DMA((SEMS,)),
            pltpu.SemaphoreType.DMA((SEMS,)),
        ]
    )
    atmos_next, ocean_next, surface = pl.pallas_call(
        functools.partial(kernel, sizes),
        out_shape=(
            jax.ShapeDtypeStruct((NF, 16 * LEV, 128), F32),
            jax.ShapeDtypeStruct((NO * OLEV * 64, 128), F32),
            jax.ShapeDtypeStruct((64, 128), F32),
        ),
        in_specs=[hbm] * 11,
        out_specs=(hbm, hbm, hbm),
        scratch_shapes=scratch,
        compiler_params=pltpu.CompilerParams(
            collective_id=0, has_side_effects=True, vmem_limit_bytes=62 * 1024 * 1024
        ),
    )(
        atmos_state.reshape(NF, 16 * LEV, 128),
        remap_atmos,
        remap_ocean,
        ocean_state.reshape(NO * OLEV * 64, 128),
        wet_mask,
        atmos_diffusion, exchange_owner.reshape(16), exchange_slot, ocean_owner.reshape(16), ocean_slot, ocean_mixing,
    )
    return (
        atmos_next.reshape(NF, LEV, 16, 128),
        ocean_next.reshape(NO, OLEV, 64, 128),
        surface.reshape(NO, 16, 128),
    )


def solution(mesh):
    sizes = (mesh.shape["comp"], mesh.shape["gx"], mesh.shape["gy"], 10, 20, 4, 8)
    in_specs = (
        P(None, None, ("comp", "gx"), "gy"),
        P(),
        P(("comp", "gx", "gy"), None, None),
        P(("comp", "gx", "gy"), None),
        P(("comp", "gx", "gy")),
        P(("comp", "gx", "gy"), None, None),
        P(("comp", "gx", "gy"), None),
        P(("comp", "gx", "gy")),
        P(None, None, "gx", "gy"),
        P(),
        P("gx", "gy"),
    )
    out_specs = (
        P(None, None, ("comp", "gx"), "gy"),
        P(None, None, "gx", "gy"),
        P(None, ("comp", "gx"), "gy"),
    )
    return jax.shard_map(
        functools.partial(on_device, sizes), mesh=mesh, in_specs=in_specs, out_specs=out_specs, check_vma=False
    )
```

```python
import functools

import jax
import jax.numpy as jnp
from jax import lax
from jax.experimental import pallas as pl
from jax.experimental.pallas import tpu as pltpu
from jax.sharding import PartitionSpec as P

MESH = pl.DeviceIdType.MESH
F32 = jnp.float32
BF16 = jnp.bfloat16
FORCING_SCALE = (0.1, -0.1, 0.1, 0.1)

SURF, FULL, SECOND, OCEAN, COMP, A1, A2, A3, A4 = 0, 4, 8, 12, 16, 17, 18, 19, 20
SEMS = 21


def far_first(nx, ny):
    def way(n, offset, flip):
        total = 0
        for at in range(n):
            to = (at + offset) % n
            ahead = (to - at) % 4
            total += min(ahead, 4 - ahead) + flip * (to // 4 != at // 4)
        return total / n

    return sorted(range(1, nx * ny), key=lambda k: (-way(nx, k // ny, 2) - way(ny, k % ny, 1), k))


def split_cat(x):
    hi = x.astype(BF16)
    lo = (x - hi.astype(F32)).astype(BF16)
    return jnp.concatenate([hi, lo], axis=1)


def split_stack(x):
    hi = x.astype(BF16).astype(F32)
    return jnp.concatenate([hi, x - hi], axis=0).astype(BF16)


def dot(a, b):
    return jnp.dot(a, b, preferred_element_type=F32)


def quad(lhs, cat):
    full = dot(lhs, cat)
    return (full[:8, :128] + full[8:, :128]) + (full[:8, 128:] + full[8:, 128:])


def halves(lhs, cat):
    full = dot(lhs, cat)
    return full[:, :128] + full[:, 128:]


def kernel(
    sizes,
    state, remap_a, remap_o, ocean, wet_in,
    diff_in, e_owner_in, e_slot_in, o_owner_in, o_slot_in, mixing_in,
    atmos_out, ocean_out, surf_out,
    S, A, N, MA, MO, MAC, MOC, MAT, MOT, O, ON, W, WN,
    rs_t, rs_b, ks, hs_a, hs_b, hs_l, hs_r,
    rf_t, rf_b, kf, hf_a, hf_b, hf_l, hf_r,
    r2_t, r2_b, k2, h2_a, h2_b, h2_l, h2_r,
    ro_t, ro_b, ko, ho_a, ho_b, ho_l, ho_r,
    X, pieces, MSG, R1, QM, PT, FL, mapped, MSG2, R2, FOR, FORIN,
    TOPC, ANS, B3, OE, OEC, REP, B4, OSV,
    diff, e_owner, e_slot, o_owner, o_slot, mixing,
    tab_v, tab_s,
    in_sem, out_sem, tab_sem, send, recv,
):
    NC, NX, NY, NF, LEV, NO, OLEV = sizes
    peers = NX * NY
    comp, gx, gy = lax.axis_index("comp"), lax.axis_index("gx"), lax.axis_index("gy")
    me = gx * NY + gy
    pos = comp * NX + gx
    ring = NC * NX
    down, up = lax.rem(pos + 1, ring), lax.rem(pos + ring - 1, ring)
    dev_down = (down // NX, lax.rem(down, NX), gy)
    dev_up = (up // NX, lax.rem(up, NX), gy)
    dev_right = (comp, gx, lax.rem(gy + 1, NY))
    dev_left = (comp, gx, lax.rem(gy + NY - 1, NY))
    sea_down = (comp, lax.rem(gx + 1, NX), gy)
    sea_up = (comp, lax.rem(gx + NX - 1, NX), gy)
    twin = (lax.rem(comp + 1, NC), gx, gy)

    def peer(k):
        px = lax.rem(gx + k // NY, NX)
        py = lax.rem(gy + lax.rem(k, NY), NY)
        return px, py, px * NY + py

    barrier = pltpu.get_barrier_semaphore()

    def greet(k, carry):
        px, py, _ = peer(k)
        pl.semaphore_signal(barrier, inc=1, device_id=(comp, px, py), device_id_type=MESH)
        return carry

    lax.fori_loop(1, peers, greet, 0)
    for other in (dev_down, dev_up, twin):
        pl.semaphore_signal(barrier, inc=1, device_id=other, device_id_type=MESH)

    top_rows = 16 * (LEV - 2)
    loads = [
        pltpu.make_async_copy(state.at[:, pl.ds(top_rows, 32), :], S.at[:, pl.ds(top_rows, 32), :], in_sem.at[0]),
        pltpu.make_async_copy(state.at[:, pl.ds(0, top_rows), :], S.at[:, pl.ds(0, top_rows), :], in_sem.at[1]),
        pltpu.make_async_copy(ocean, O, in_sem.at[2]),
        pltpu.make_async_copy(wet_in, W, in_sem.at[3]),
        pltpu.make_async_copy(remap_a, MA, in_sem.at[4]),
        pltpu.make_async_copy(remap_o, MO, in_sem.at[5]),
    ]
    small = [
        pltpu.make_async_copy(src, dst, in_sem.at[6 + n])
        for n, (src, dst) in enumerate([
            (e_owner_in, e_owner), (o_owner_in, o_owner), (e_slot_in, e_slot), (o_slot_in, o_slot),
            (diff_in, diff), (mixing_in, mixing),
        ])
    ]
    for load in small + loads:
        load.start()

    lane16 = lax.broadcasted_iota(jnp.int32, (16, 128), 1)
    row16 = lax.broadcasted_iota(jnp.int32, (16, 128), 0)
    pair16 = lane16 // 2
    even16 = lane16 == pair16 * 2
    sub8 = lax.broadcasted_iota(jnp.int32, (8, 128), 0)

    def remote(src, dst, number, device):
        copy = pltpu.make_async_remote_copy(
            src_ref=src, dst_ref=dst, send_sem=send.at[number], recv_sem=recv.at[number],
            device_id=device, device_id_type=MESH,
        )
        copy.start()
        return copy

    def halo(number, rows_t, rows_b, cols, from_a, from_b, from_l, from_r, below, above):
        return [
            remote(rows_b, from_a, number, below),
            remote(rows_t, from_b, number + 1, above),
            remote(cols, from_l, number + 2, dev_right),
            remote(cols, from_r, number + 3, dev_left),
        ]

    loads[0].wait()
    last = 16 * (LEV - 1)
    packed = jnp.zeros((16, 128), F32)
    for f in range(NF):
        v = S[f, pl.ds(last, 16), :]
        packed = jnp.where(pair16 == f, pltpu.roll(v, 2 * f + 1, 1), packed)
        rs_t[pl.ds(f, 1), :] = v[0:1]
        rs_b[pl.ds(f, 1), :] = v[15:16]
    ks[...] = packed
    pl.semaphore_wait(barrier, peers - 1 + 3)
    surface_halo = halo(SURF, rs_t, rs_b, ks, hs_a, hs_b, hs_l, hs_r, dev_down, dev_up)

    def places(owner):
        ranks, keys = [], []
        for i in range(16):
            rank = jnp.int32(0)
            for j in range(i):
                rank = rank + (owner[j] == owner[i]).astype(jnp.int32)
            ranks.append(rank)
            keys.append(2 * owner[i] + rank)
        return ranks, keys

    for load in small:
        load.wait()
    e_rank, e_key = places(e_owner)
    o_rank, o_key = places(o_owner)
    lane8 = lax.broadcasted_iota(jnp.int32, (8, 128), 1)
    table = jnp.zeros((8, 128), jnp.int32)
    for i in range(16):
        table = jnp.where(lane8 == jnp.where(sub8 == 0, e_key[i], o_key[i]), i, table)
    tab_v[...] = table
    tab_copy = pltpu.make_async_copy(tab_v, tab_s, tab_sem.at[0])
    tab_copy.start()

    def pack_atmos(src, rows_t, rows_b, cols, f):
        kept = jnp.zeros((16, 128), F32)
        for lev in range(LEV):
            v = src[f, pl.ds(16 * lev, 16), :]
            kept = jnp.where(pair16 == lev, pltpu.roll(v, 2 * lev + 1, 1), kept)
        cols[f] = kept
        rows_t[f, pl.ds(0, LEV), :] = src[f, pl.ds(0, LEV, stride=16), :]
        rows_b[f, pl.ds(0, LEV), :] = src[f, pl.ds(15, LEV, stride=16), :]

    loads[2].wait()
    loads[3].wait()
    planes = NO * OLEV
    lane64 = lax.broadcasted_iota(jnp.int32, (64, 128), 1)
    row64 = lax.broadcasted_iota(jnp.int32, (64, 128), 0)
    pair64 = lane64 // 2
    wet = W[...].astype(F32)
    WN[0] = wet
    kept = jnp.where(pair64 == planes, pltpu.roll(wet, 2 * planes + 1, 1), 0.0)
    ko[...] = kept
    ro_t[pl.ds(planes, 1), :] = wet[0:1]
    ro_b[pl.ds(planes, 1), :] = wet[63:64]

    def pack_ocean(f, carry):
        kept = ko[...]
        for lev in range(OLEV):
            q = f * OLEV + lev
            v = O[pl.ds(pl.multiple_of(q * 64, 64), 64), :]
            kept = jnp.where(pair64 == q, pltpu.roll(v, 2 * q + 1, 1), kept)
        ko[...] = kept
        return carry

    lax.fori_loop(0, NO, pack_ocean, 0)
    ro_t[pl.ds(0, planes), :] = O[pl.ds(0, planes, stride=64), :]
    ro_b[pl.ds(0, planes), :] = O[pl.ds(63, planes, stride=64), :]
    ocean_halo = halo(OCEAN, ro_t, ro_b, ko, ho_a, ho_b, ho_l, ho_r, sea_down, sea_up)

    r128 = lax.broadcasted_iota(jnp.int32, (128, 128), 0)
    lane128 = lax.broadcasted_iota(jnp.int32, (128, 128), 1)
    low128 = lane128 < 64
    labels = jnp.full((128, 128), -1, jnp.int32)
    for i in range(16):
        labels = jnp.where(
            r128 == jnp.where(low128, o_key[i], e_key[i]), jnp.where(low128, o_slot[i], e_slot[i]), labels
        )
    MSG[pl.ds(7, 128, stride=8), :] = labels.astype(F32)

    loads[4].wait()

    def split_a(i, carry):
        MAC[i] = split_cat(MA[i])
        return carry

    lax.fori_loop(0, 16, split_a, 0)

    tab_copy.wait()
    for copy in surface_halo:
        copy.wait_recv()
    kl, kr = hs_l[...], hs_r[...]
    cols = jnp.where(even16, kl, pltpu.roll(kr, 126, 1))
    after = []
    for f in range(NF):
        v = S[f, pl.ds(last, 16), :]
        edge = pltpu.roll(cols, (128 - 2 * f) % 128, 1)
        left = jnp.where(lane16 == 0, edge, pltpu.roll(v, 1, 1))
        right = jnp.where(lane16 == 127, edge, pltpu.roll(v, 127, 1))
        above = jnp.where(row16 == 0, hs_a[pl.ds(f, 1), :], pltpu.roll(v, 1, 0))
        below = jnp.where(row16 == 15, hs_b[pl.ds(f, 1), :], pltpu.roll(v, 15, 0))
        upper = S[f, pl.ds(last - 16, 16), :]
        after.append(v + diff[f] * (above + below + left + right - 4.0 * v) + 0.1 * (upper - v))
    combined = [after[0] - after[4], after[1], after[2], after[3], after[6] + after[7], after[5] + after[8], after[9], after[9]]
    for f in range(8):
        X[pl.ds(16 * f, 16), :] = combined[f]
    for i in range(16):
        pieces[i] = quad(split_stack(X[pl.ds(i, 8, stride=16), :]), MAC[i])

    def pack_pieces(n, carry):
        for m in range(8):
            r = n * 8 + m
            MSG[pl.ds(pl.multiple_of(r * 8, 8), 7), :] = pieces[tab_s[0, r]][0:7]
        return carry

    lax.fori_loop(0, 16, pack_pieces, 0)

    def exchange(number, rows, src, dst_of):
        def step(k, carry):
            px, py, target = peer(k)
            remote(src.at[pl.ds(pl.multiple_of(target * rows, 8), rows), :], dst_of(me), number, (comp, px, py))
            return carry

        for k in far_first(NX, NY):
            step(k, 0)

    def arrived(number, count_ref):
        pltpu.make_async_copy(count_ref, count_ref, recv.at[number]).wait()

    def departed(number, count_ref):
        pltpu.make_async_copy(count_ref, count_ref, send.at[number]).wait()

    mine16 = pl.ds(pl.multiple_of(me * 16, 16), 16)
    mine8 = pl.ds(pl.multiple_of(me * 8, 8), 8)
    exchange(A1, 16, MSG, lambda m: R1.at[pl.ds(pl.multiple_of(m * 16, 16), 16), :])
    R1[mine16, :] = MSG[mine16, :]

    loads[1].wait()

    def pack_first(f, carry):
        pack_atmos(S, rf_t, rf_b, kf, f)
        return carry

    lax.fori_loop(0, NF, pack_first, 0)
    full_halo = halo(FULL, rf_t, rf_b, kf, hf_a, hf_b, hf_l, hf_r, dev_down, dev_up)

    for copy in ocean_halo:
        copy.wait_recv()
    ol, orr = ho_l[...], ho_r[...]
    even64 = lane64 == pair64 * 2
    ho_l[...] = jnp.where(even64, ol, pltpu.roll(orr, 126, 1))

    def around(v, q, edges):
        edge = pltpu.roll(edges, 128 - 2 * q, 1)
        left = jnp.where(lane64 == 0, edge, pltpu.roll(v, 1, 1))
        right = jnp.where(lane64 == 127, edge, pltpu.roll(v, 127, 1))
        above = jnp.where(row64 == 0, ho_a[pl.ds(q, 1), :], pltpu.roll(v, 1, 0))
        below = jnp.where(row64 == 63, ho_b[pl.ds(q, 1), :], pltpu.roll(v, 63, 0))
        return above, below, left, right

    for n, w in enumerate(around(wet, planes, ho_l[...])):
        WN[1 + n] = w

    def sea(f, carry):
        mix = mixing[f]
        base = f * OLEV
        for lev in range(OLEV):
            q = base + lev
            v = O[pl.ds(pl.multiple_of(q * 64, 64), 64), :]
            total = jnp.zeros((64, 128), F32)
            edges = pltpu.roll(ho_l[...], 128 - 2 * q, 1)
            left = jnp.where(lane64 == 0, edges, pltpu.roll(v, 1, 1))
            right = jnp.where(lane64 == 127, edges, pltpu.roll(v, 127, 1))
            above = jnp.where(row64 == 0, ho_a[pl.ds(q, 1), :], pltpu.roll(v, 1, 0))
            below = jnp.where(row64 == 63, ho_b[pl.ds(q, 1), :], pltpu.roll(v, 63, 0))
            total = WN[1] * (above - v) + WN[2] * (below - v) + WN[3] * (left - v) + WN[4] * (right - v)
            upper = v if lev == 0 else O[pl.ds(pl.multiple_of(q * 64 - 64, 64), 64), :]
            lower = v if lev == OLEV - 1 else O[pl.ds(pl.multiple_of(q * 64 + 64, 64), 64), :]
            w = WN[0]
            ON[pl.ds(pl.multiple_of(q * 64, 64), 64), :] = v + w * (
                mix * w * total + 0.1 * (upper + lower - 2.0 * v)
            )
        return carry

    lax.fori_loop(0, NO, sea, 0)

    loads[5].wait()

    def split_o(i, carry):
        MOC[i] = split_cat(MO[i])
        MOT[i] = split_cat(jnp.transpose(MO[i]))
        MAT[i] = split_cat(jnp.transpose(MA[i]))
        return carry

    lax.fori_loop(0, 16, split_o, 0)

    arrived(A1, R1.at[pl.ds(0, 16 * (peers - 1)), :])
    chosen = (R1[pl.ds(7, 128, stride=8), :] == (lane128 - jnp.where(low128, 0, 64)).astype(F32)).astype(F32)
    QM[...] = chosen.astype(BF16)
    PT[...] = jnp.transpose(chosen).astype(BF16)
    fields = [halves(PT[pl.ds(64, 16), :], split_cat(R1[pl.ds(f, 128, stride=8), :])) for f in range(7)]
    heat, salt, east, north, gain, fresh, shape = fields
    speed = jnp.sqrt(east * east + north * north + 0.5)
    flux = [
        speed * heat + gain,
        speed * salt + fresh,
        speed * east * (1.0 + 0.2 * jnp.tanh(shape)),
        speed * north,
    ]
    for g in range(8):
        FL[pl.ds(16 * g, 16), :] = flux[g % 4]
    for j in range(16):
        mapped[j] = quad(split_stack(FL[pl.ds(j, 8, stride=16), :]), MOC[j])

    def pack_mapped(n, carry):
        for m in range(8):
            t = n * 8 + m
            MSG2[pl.ds(pl.multiple_of(t * 8, 8), 8), :] = jnp.where(
                sub8 < 4, mapped[tab_s[1, 2 * t]], mapped[tab_s[1, 2 * t + 1]]
            )
        return carry

    lax.fori_loop(0, peers // 8, pack_mapped, 0)
    exchange(A2, 8, MSG2, lambda m: R2.at[pl.ds(pl.multiple_of(m * 8, 8), 8), :])
    R2[mine8, :] = MSG2[mine8, :]

    for copy in full_halo:
        copy.wait_recv()

    def atmos_field(src, dst, from_a, from_b, from_l, from_r, f):
        d = diff[f]
        both = jnp.where(even16, from_l[f], pltpu.roll(from_r[f], 126, 1))
        for lev in range(LEV):
            v = src[f, pl.ds(16 * lev, 16), :]
            edge = pltpu.roll(both, (128 - 2 * lev) % 128, 1)
            left = jnp.where(lane16 == 0, edge, pltpu.roll(v, 1, 1))
            right = jnp.where(lane16 == 127, edge, pltpu.roll(v, 127, 1))
            above = jnp.where(row16 == 0, from_a[f, pl.ds(lev, 1), :], pltpu.roll(v, 1, 0))
            below = jnp.where(row16 == 15, from_b[f, pl.ds(lev, 1), :], pltpu.roll(v, 15, 0))
            upper = v if lev == 0 else src[f, pl.ds(16 * lev - 16, 16), :]
            lower = v if lev == LEV - 1 else src[f, pl.ds(16 * lev + 16, 16), :]
            dst[f, pl.ds(16 * lev, 16), :] = (
                v + d * (above + below + left + right - 4.0 * v) + 0.1 * (upper + lower - 2.0 * v)
            )

    def first_step(f, carry):
        atmos_field(S, A, hf_a, hf_b, hf_l, hf_r, f)
        pack_atmos(A, r2_t, r2_b, k2, f)
        return carry

    lax.fori_loop(0, NF, first_step, 0)

    arrived(A2, R2.at[pl.ds(0, 8 * (peers - 1)), :])
    for g in range(NO):
        FOR[pl.ds(64 * g, 64), :] = halves(PT[pl.ds(0, 64), :], split_cat(R2[pl.ds(g, 128, stride=4), :]))
    twin_copy = remote(FOR, FORIN, COMP, twin)
    zero64 = jnp.zeros((64, 256), BF16)
    for g in range(NO):
        TOPC[g, pl.ds(64, 64), :] = zero64
        OEC[g, pl.ds(0, 64), :] = zero64
        OEC[g, pl.ds(64, 64), :] = zero64
    twin_copy.wait_recv()
    for g in range(NO):
        rows = pl.ds(64 * OLEV * g, 64)
        plane = pl.ds(64 * g, 64)
        top = ON[rows, :] + WN[0] * (FORCING_SCALE[g] * (FOR[plane, :] + FORIN[plane, :]))
        ON[rows, :] = top
        TOPC[g, pl.ds(0, 64), :] = split_cat(top)
    for g in range(NO):
        ANS[pl.ds(g, 128, stride=4), :] = halves(QM[...], TOPC[g])
    exchange(A3, 8, ANS, lambda m: B3.at[m])
    B3[me] = ANS[mine8, :]
    second_halo = halo(SECOND, r2_t, r2_b, k2, h2_a, h2_b, h2_l, h2_r, dev_down, dev_up)
    ocean_store = pltpu.make_async_copy(ON, ocean_out, out_sem.at[0])
    ocean_store.start()

    b3_all = B3.at[pl.ds(0, peers - 1)]
    arrived(A3, b3_all)
    for j in range(16):
        both = quad(split_stack(B3[o_owner[j]]), MOT[j])
        picked = jnp.where(o_rank[j] == 0, both, pltpu.roll(both, 4, 0))
        OE[pl.ds(j, 4, stride=16), :] = picked[0:4]
    for g in range(NO):
        OEC[g, pl.ds(64, 16), :] = split_cat(OE[pl.ds(16 * g, 16), :])
    for g in range(NO):
        REP[pl.ds(g, 128, stride=4), :] = halves(QM[...], OEC[g])
    exchange(A4, 8, REP, lambda m: B4.at[m])
    B4[me] = REP[mine8, :]

    for copy in second_halo:
        copy.wait_recv()

    def second_step(f, carry):
        atmos_field(A, N, h2_a, h2_b, h2_l, h2_r, f)
        return carry

    lax.fori_loop(0, NF, second_step, 0)
    atmos_store = pltpu.make_async_copy(N, atmos_out, out_sem.at[1])
    atmos_store.start()

    arrived(A4, B4.at[pl.ds(0, peers - 1)])
    for i in range(16):
        both = quad(split_stack(B4[e_owner[i]]), MAT[i])
        picked = jnp.where(e_rank[i] == 0, both, pltpu.roll(both, 4, 0))
        OSV[pl.ds(i, 4, stride=16), :] = picked[0:4]
    surf_store = pltpu.make_async_copy(OSV, surf_out, out_sem.at[2])
    surf_store.start()

    for copy in surface_halo + full_halo + ocean_halo + second_halo + [twin_copy]:
        copy.wait_send()
    departed(A1, MSG.at[pl.ds(0, 16 * (peers - 1)), :])
    departed(A2, MSG2.at[pl.ds(0, 8 * (peers - 1)), :])
    departed(A3, ANS.at[pl.ds(0, 8 * (peers - 1)), :])
    departed(A4, REP.at[pl.ds(0, 8 * (peers - 1)), :])
    ocean_store.wait()
    atmos_store.wait()
    surf_store.wait()


def hand_out(a, b, c, a_out, b_out, c_out, sem):
    copies = [pltpu.make_async_copy(x, y, sem.at[n]) for n, (x, y) in enumerate([(a, a_out), (b, b_out), (c, c_out)])]
    for copy in copies:
        copy.start()
    for copy in copies:
        copy.wait()


def on_device(
    sizes,
    atmos_state, atmos_diffusion, remap_atmos, exchange_owner, exchange_slot,
    remap_ocean, ocean_owner, ocean_slot, ocean_state, ocean_mixing, wet_mask,
):
    NC, NX, NY, NF, LEV, NO, OLEV = sizes
    peers = NX * NY
    hbm = pl.BlockSpec(memory_space=pltpu.HBM)
    any_ = pl.BlockSpec(memory_space=pl.ANY)

    def vm(*shape, dtype=F32):
        return pltpu.VMEM(shape, dtype)

    halo_atmos = [vm(NF, 24, 128), vm(NF, 24, 128), vm(NF, 16, 128), vm(NF, 24, 128), vm(NF, 24, 128), vm(NF, 16, 128), vm(NF, 16, 128)]
    scratch = (
        [vm(NF, 16 * LEV, 128) for _ in range(3)]
        + [vm(16, 128, 128), vm(16, 128, 128)]
        + [vm(16, 128, 256, dtype=BF16) for _ in range(4)]
        + [vm(NO * OLEV * 64, 128), vm(NO * OLEV * 64, 128), vm(64, 128, dtype=jnp.int32), vm(5, 64, 128)]
        + [vm(16, 128) for _ in range(7)]
        + halo_atmos
        + halo_atmos
        + [vm(40, 128), vm(40, 128), vm(64, 128), vm(40, 128), vm(40, 128), vm(64, 128), vm(64, 128)]
        + [vm(128, 128), vm(16, 8, 128), vm(16 * peers, 128), vm(16 * peers, 128)]
        + [vm(128, 128, dtype=BF16), vm(128, 128, dtype=BF16), vm(128, 128), vm(16, 8, 128)]
        + [vm(8 * peers, 128), vm(8 * peers, 128), vm(256, 128), vm(256, 128)]
        + [vm(NO, 128, 256, dtype=BF16), vm(8 * peers, 128), vm(peers, 8, 128), vm(64, 128)]
        + [vm(NO, 128, 256, dtype=BF16), vm(8 * peers, 128), vm(peers, 8, 128), vm(64, 128)]
        + [pltpu.SMEM((NF,), F32)] + [pltpu.SMEM((16,), jnp.int32) for _ in range(4)] + [pltpu.SMEM((NO,), F32)]
        + [vm(8, 128, dtype=jnp.int32), pltpu.SMEM((8, 128), jnp.int32)]
        + [
            pltpu.SemaphoreType.DMA((12,)),
            pltpu.SemaphoreType.DMA((3,)),
            pltpu.SemaphoreType.DMA((1,)),
            pltpu.SemaphoreType.DMA((SEMS,)),
            pltpu.SemaphoreType.DMA((SEMS,)),
        ]
    )
    atmos_next, ocean_next, surface = pl.pallas_call(
        functools.partial(kernel, sizes),
        out_shape=(
            jax.ShapeDtypeStruct((NF, 16 * LEV, 128), F32),
            jax.ShapeDtypeStruct((NO * OLEV * 64, 128), F32),
            jax.ShapeDtypeStruct((64, 128), F32),
        ),
        in_specs=[hbm] * 11,
        out_specs=(any_, any_, any_),
        scratch_shapes=scratch,
        compiler_params=pltpu.CompilerParams(
            collective_id=0, has_side_effects=True, vmem_limit_bytes=40 * 1024 * 1024
        ),
    )(*(pltpu.with_memory_space_constraint(x, pltpu.HBM) for x in (
        atmos_state.reshape(NF, 16 * LEV, 128),
        remap_atmos,
        remap_ocean,
        ocean_state.reshape(NO * OLEV * 64, 128),
        wet_mask,
        atmos_diffusion, exchange_owner.reshape(16), exchange_slot, ocean_owner.reshape(16), ocean_slot, ocean_mixing,
    )))
    results = (atmos_next, ocean_next, surface)
    atmos_next, ocean_next, surface = pl.pallas_call(
        hand_out,
        out_shape=tuple(jax.ShapeDtypeStruct(x.shape, x.dtype) for x in results),
        in_specs=[any_] * 3,
        out_specs=(hbm, hbm, hbm),
        scratch_shapes=[pltpu.SemaphoreType.DMA((3,))],
        compiler_params=pltpu.CompilerParams(vmem_limit_bytes=1024 * 1024),
    )(*results)
    return (
        atmos_next.reshape(NF, LEV, 16, 128),
        ocean_next.reshape(NO, OLEV, 64, 128),
        surface.reshape(NO, 16, 128),
    )


def solution(mesh):
    sizes = (mesh.shape["comp"], mesh.shape["gx"], mesh.shape["gy"], 10, 20, 4, 8)
    in_specs = (
        P(None, None, ("comp", "gx"), "gy"),
        P(),
        P(("comp", "gx", "gy"), None, None),
        P(("comp", "gx", "gy"), None),
        P(("comp", "gx", "gy")),
        P(("comp", "gx", "gy"), None, None),
        P(("comp", "gx", "gy"), None),
        P(("comp", "gx", "gy")),
        P(None, None, "gx", "gy"),
        P(),
        P("gx", "gy"),
    )
    out_specs = (
        P(None, None, ("comp", "gx"), "gy"),
        P(None, None, "gx", "gy"),
        P(None, ("comp", "gx"), "gy"),
    )
    return jax.shard_map(
        functools.partial(on_device, sizes), mesh=mesh, in_specs=in_specs, out_specs=out_specs, check_vma=False
    )
```

```python
import functools

import jax
import jax.numpy as jnp
from jax import lax
from jax.experimental import pallas as pl
from jax.experimental.pallas import tpu as pltpu
from jax.sharding import PartitionSpec as P

MESH = pl.DeviceIdType.MESH
F32 = jnp.float32
BF16 = jnp.bfloat16
FORCING_SCALE = (0.1, -0.1, 0.1, 0.1)

SURF, FULL, SECOND, OCEAN, COMP, A1, A2, A3, A4 = 0, 4, 8, 12, 16, 17, 18, 19, 20
SEMS = 21


def far_first(nx, ny):
    def way(n, offset, flip):
        total = 0
        for at in range(n):
            to = (at + offset) % n
            ahead = (to - at) % 4
            total += min(ahead, 4 - ahead) + flip * (to // 4 != at // 4)
        return total / n

    return sorted(range(1, nx * ny), key=lambda k: (-way(nx, k // ny, 2) - way(ny, k % ny, 1), k))


def split_cat(x):
    hi = x.astype(BF16)
    lo = (x - hi.astype(F32)).astype(BF16)
    return jnp.concatenate([hi, lo], axis=1)


def split_stack(x):
    hi = x.astype(BF16).astype(F32)
    return jnp.concatenate([hi, x - hi], axis=0).astype(BF16)


def dot(a, b):
    return jnp.dot(a, b, preferred_element_type=F32)


def quad(lhs, cat):
    full = dot(lhs, cat)
    return (full[:8, :128] + full[8:, :128]) + (full[:8, 128:] + full[8:, 128:])


def halves(lhs, cat):
    full = dot(lhs, cat)
    return full[:, :128] + full[:, 128:]


def kernel(
    sizes,
    state, remap_a, remap_o, ocean, wet_in,
    diff_in, e_owner_in, e_slot_in, o_owner_in, o_slot_in, mixing_in,
    atmos_out, ocean_out, surf_out,
    S, A, N, MA, MO, MAC, MOC, MAT, MOT, O, ON, W, WN,
    rs_t, rs_b, ks, hs_a, hs_b, hs_l, hs_r,
    rf_t, rf_b, kf, hf_a, hf_b, hf_l, hf_r,
    r2_t, r2_b, k2, h2_a, h2_b, h2_l, h2_r,
    ro_t, ro_b, ko, ho_a, ho_b, ho_l, ho_r,
    X, pieces, MSG, R1, QM, PT, FL, mapped, MSG2, R2, FOR, FORIN,
    TOPC, ANS, B3, OE, OEC, REP, B4, OSV,
    diff, e_owner, e_slot, o_owner, o_slot, mixing,
    tab_v, tab_s,
    in_sem, out_sem, tab_sem, send, recv, row_here,
):
    NC, NX, NY, NF, LEV, NO, OLEV = sizes
    peers = NX * NY
    comp, gx, gy = lax.axis_index("comp"), lax.axis_index("gx"), lax.axis_index("gy")
    me = gx * NY + gy
    pos = comp * NX + gx
    ring = NC * NX
    down, up = lax.rem(pos + 1, ring), lax.rem(pos + ring - 1, ring)
    dev_down = (down // NX, lax.rem(down, NX), gy)
    dev_up = (up // NX, lax.rem(up, NX), gy)
    dev_right = (comp, gx, lax.rem(gy + 1, NY))
    dev_left = (comp, gx, lax.rem(gy + NY - 1, NY))
    sea_down = (comp, lax.rem(gx + 1, NX), gy)
    sea_up = (comp, lax.rem(gx + NX - 1, NX), gy)
    twin = (lax.rem(comp + 1, NC), gx, gy)

    def peer(k):
        px = lax.rem(gx + k // NY, NX)
        py = lax.rem(gy + lax.rem(k, NY), NY)
        return px, py, px * NY + py

    barrier = pltpu.get_barrier_semaphore()

    row_peers = [(comp, gx, lax.rem(gy + b, NY)) for b in range(1, NY)]
    column_peers = [(comp, lax.rem(gx + a, NX), gy) for a in range(1, NX)]
    greeted = row_peers + column_peers + [dev_down, dev_up, twin]
    for other in greeted:
        pl.semaphore_signal(barrier, inc=1, device_id=other, device_id_type=MESH)

    top_rows = 16 * (LEV - 2)
    loads = [
        pltpu.make_async_copy(state.at[:, pl.ds(top_rows, 32), :], S.at[:, pl.ds(top_rows, 32), :], in_sem.at[0]),
        pltpu.make_async_copy(state.at[:, pl.ds(0, top_rows), :], S.at[:, pl.ds(0, top_rows), :], in_sem.at[1]),
        pltpu.make_async_copy(ocean, O, in_sem.at[2]),
        pltpu.make_async_copy(wet_in, W, in_sem.at[3]),
        pltpu.make_async_copy(remap_a, MA, in_sem.at[4]),
        pltpu.make_async_copy(remap_o, MO, in_sem.at[5]),
    ]
    small = [
        pltpu.make_async_copy(src, dst, in_sem.at[6 + n])
        for n, (src, dst) in enumerate([
            (e_owner_in, e_owner), (o_owner_in, o_owner), (e_slot_in, e_slot), (o_slot_in, o_slot),
            (diff_in, diff), (mixing_in, mixing),
        ])
    ]
    for load in small + loads:
        load.start()

    lane16 = lax.broadcasted_iota(jnp.int32, (16, 128), 1)
    row16 = lax.broadcasted_iota(jnp.int32, (16, 128), 0)
    pair16 = lane16 // 2
    even16 = lane16 == pair16 * 2
    sub8 = lax.broadcasted_iota(jnp.int32, (8, 128), 0)

    def remote(src, dst, number, device):
        copy = pltpu.make_async_remote_copy(
            src_ref=src, dst_ref=dst, send_sem=send.at[number], recv_sem=recv.at[number],
            device_id=device, device_id_type=MESH,
        )
        copy.start()
        return copy

    def halo(number, rows_t, rows_b, cols, from_a, from_b, from_l, from_r, below, above):
        return [
            remote(rows_b, from_a, number, below),
            remote(rows_t, from_b, number + 1, above),
            remote(cols, from_l, number + 2, dev_right),
            remote(cols, from_r, number + 3, dev_left),
        ]

    loads[0].wait()
    last = 16 * (LEV - 1)
    packed = jnp.zeros((16, 128), F32)
    for f in range(NF):
        v = S[f, pl.ds(last, 16), :]
        packed = jnp.where(pair16 == f, pltpu.roll(v, 2 * f + 1, 1), packed)
        rs_t[pl.ds(f, 1), :] = v[0:1]
        rs_b[pl.ds(f, 1), :] = v[15:16]
    ks[...] = packed
    pl.semaphore_wait(barrier, len(greeted))
    surface_halo = halo(SURF, rs_t, rs_b, ks, hs_a, hs_b, hs_l, hs_r, dev_down, dev_up)
    for other in column_peers:
        pl.semaphore_signal(row_here.at[0], inc=1, device_id=other, device_id_type=MESH)

    def places(owner):
        ranks, keys = [], []
        for i in range(16):
            rank = jnp.int32(0)
            for j in range(i):
                rank = rank + (owner[j] == owner[i]).astype(jnp.int32)
            ranks.append(rank)
            keys.append(2 * owner[i] + rank)
        return ranks, keys

    for load in small:
        load.wait()
    e_rank, e_key = places(e_owner)
    o_rank, o_key = places(o_owner)
    lane8 = lax.broadcasted_iota(jnp.int32, (8, 128), 1)
    table = jnp.zeros((8, 128), jnp.int32)
    for i in range(16):
        table = jnp.where(lane8 == jnp.where(sub8 == 0, e_key[i], o_key[i]), i, table)
    tab_v[...] = table
    tab_copy = pltpu.make_async_copy(tab_v, tab_s, tab_sem.at[0])
    tab_copy.start()

    def pack_atmos(src, rows_t, rows_b, cols, f):
        kept = jnp.zeros((16, 128), F32)
        for lev in range(LEV):
            v = src[f, pl.ds(16 * lev, 16), :]
            kept = jnp.where(pair16 == lev, pltpu.roll(v, 2 * lev + 1, 1), kept)
        cols[f] = kept
        rows_t[f, pl.ds(0, LEV), :] = src[f, pl.ds(0, LEV, stride=16), :]
        rows_b[f, pl.ds(0, LEV), :] = src[f, pl.ds(15, LEV, stride=16), :]

    loads[2].wait()
    loads[3].wait()
    planes = NO * OLEV
    lane64 = lax.broadcasted_iota(jnp.int32, (64, 128), 1)
    row64 = lax.broadcasted_iota(jnp.int32, (64, 128), 0)
    pair64 = lane64 // 2
    wet = W[...].astype(F32)
    WN[0] = wet
    kept = jnp.where(pair64 == planes, pltpu.roll(wet, 2 * planes + 1, 1), 0.0)
    ko[...] = kept
    ro_t[pl.ds(planes, 1), :] = wet[0:1]
    ro_b[pl.ds(planes, 1), :] = wet[63:64]

    def pack_ocean(f, carry):
        kept = ko[...]
        for lev in range(OLEV):
            q = f * OLEV + lev
            v = O[pl.ds(pl.multiple_of(q * 64, 64), 64), :]
            kept = jnp.where(pair64 == q, pltpu.roll(v, 2 * q + 1, 1), kept)
        ko[...] = kept
        return carry

    lax.fori_loop(0, NO, pack_ocean, 0)
    ro_t[pl.ds(0, planes), :] = O[pl.ds(0, planes, stride=64), :]
    ro_b[pl.ds(0, planes), :] = O[pl.ds(63, planes, stride=64), :]
    ocean_halo = halo(OCEAN, ro_t, ro_b, ko, ho_a, ho_b, ho_l, ho_r, sea_down, sea_up)

    r128 = lax.broadcasted_iota(jnp.int32, (128, 128), 0)
    lane128 = lax.broadcasted_iota(jnp.int32, (128, 128), 1)
    low128 = lane128 < 64
    labels = jnp.full((128, 128), -1, jnp.int32)
    for i in range(16):
        labels = jnp.where(
            r128 == jnp.where(low128, o_key[i], e_key[i]), jnp.where(low128, o_slot[i], e_slot[i]), labels
        )
    MSG[pl.ds(7, 128, stride=8), :] = labels.astype(F32)

    loads[4].wait()

    def split_a(i, carry):
        MAC[i] = split_cat(MA[i])
        return carry

    lax.fori_loop(0, 16, split_a, 0)

    tab_copy.wait()
    for copy in surface_halo:
        copy.wait_recv()
    kl, kr = hs_l[...], hs_r[...]
    cols = jnp.where(even16, kl, pltpu.roll(kr, 126, 1))
    after = []
    for f in range(NF):
        v = S[f, pl.ds(last, 16), :]
        edge = pltpu.roll(cols, (128 - 2 * f) % 128, 1)
        left = jnp.where(lane16 == 0, edge, pltpu.roll(v, 1, 1))
        right = jnp.where(lane16 == 127, edge, pltpu.roll(v, 127, 1))
        above = jnp.where(row16 == 0, hs_a[pl.ds(f, 1), :], pltpu.roll(v, 1, 0))
        below = jnp.where(row16 == 15, hs_b[pl.ds(f, 1), :], pltpu.roll(v, 15, 0))
        upper = S[f, pl.ds(last - 16, 16), :]
        after.append(v + diff[f] * (above + below + left + right - 4.0 * v) + 0.1 * (upper - v))
    combined = [after[0] - after[4], after[1], after[2], after[3], after[6] + after[7], after[5] + after[8], after[9], after[9]]
    for f in range(8):
        X[pl.ds(16 * f, 16), :] = combined[f]
    for i in range(16):
        pieces[i] = quad(split_stack(X[pl.ds(i, 8, stride=16), :]), MAC[i])

    def pack_pieces(n, carry):
        for m in range(8):
            r = n * 8 + m
            MSG[pl.ds(pl.multiple_of(r * 8, 8), 7), :] = pieces[tab_s[0, r]][0:7]
        return carry

    lax.fori_loop(0, 16, pack_pieces, 0)

    def exchange(number, rows, src, dst_of):
        def step(k, carry):
            px, py, target = peer(k)
            remote(src.at[pl.ds(pl.multiple_of(target * rows, 8), rows), :], dst_of(me), number, (comp, px, py))
            return carry

        for k in far_first(NX, NY):
            step(k, 0)

    def arrived(number, count_ref):
        pltpu.make_async_copy(count_ref, count_ref, recv.at[number]).wait()

    def departed(number, count_ref):
        pltpu.make_async_copy(count_ref, count_ref, send.at[number]).wait()

    mine16 = pl.ds(pl.multiple_of(me * 16, 16), 16)
    mine8 = pl.ds(pl.multiple_of(me * 8, 8), 8)
    pl.semaphore_wait(row_here.at[0], NX - 1)
    exchange(A1, 16, MSG, lambda m: R1.at[pl.ds(pl.multiple_of(m * 16, 16), 16), :])
    R1[mine16, :] = MSG[mine16, :]

    loads[1].wait()

    def pack_first(f, carry):
        pack_atmos(S, rf_t, rf_b, kf, f)
        return carry

    lax.fori_loop(0, NF, pack_first, 0)
    full_halo = halo(FULL, rf_t, rf_b, kf, hf_a, hf_b, hf_l, hf_r, dev_down, dev_up)

    for copy in ocean_halo:
        copy.wait_recv()
    ol, orr = ho_l[...], ho_r[...]
    even64 = lane64 == pair64 * 2
    ho_l[...] = jnp.where(even64, ol, pltpu.roll(orr, 126, 1))

    def around(v, q, edges):
        edge = pltpu.roll(edges, 128 - 2 * q, 1)
        left = jnp.where(lane64 == 0, edge, pltpu.roll(v, 1, 1))
        right = jnp.where(lane64 == 127, edge, pltpu.roll(v, 127, 1))
        above = jnp.where(row64 == 0, ho_a[pl.ds(q, 1), :], pltpu.roll(v, 1, 0))
        below = jnp.where(row64 == 63, ho_b[pl.ds(q, 1), :], pltpu.roll(v, 63, 0))
        return above, below, left, right

    for n, w in enumerate(around(wet, planes, ho_l[...])):
        WN[1 + n] = w

    def sea(f, carry):
        mix = mixing[f]
        base = f * OLEV
        for lev in range(OLEV):
            q = base + lev
            v = O[pl.ds(pl.multiple_of(q * 64, 64), 64), :]
            total = jnp.zeros((64, 128), F32)
            edges = pltpu.roll(ho_l[...], 128 - 2 * q, 1)
            left = jnp.where(lane64 == 0, edges, pltpu.roll(v, 1, 1))
            right = jnp.where(lane64 == 127, edges, pltpu.roll(v, 127, 1))
            above = jnp.where(row64 == 0, ho_a[pl.ds(q, 1), :], pltpu.roll(v, 1, 0))
            below = jnp.where(row64 == 63, ho_b[pl.ds(q, 1), :], pltpu.roll(v, 63, 0))
            total = WN[1] * (above - v) + WN[2] * (below - v) + WN[3] * (left - v) + WN[4] * (right - v)
            upper = v if lev == 0 else O[pl.ds(pl.multiple_of(q * 64 - 64, 64), 64), :]
            lower = v if lev == OLEV - 1 else O[pl.ds(pl.multiple_of(q * 64 + 64, 64), 64), :]
            w = WN[0]
            ON[pl.ds(pl.multiple_of(q * 64, 64), 64), :] = v + w * (
                mix * w * total + 0.1 * (upper + lower - 2.0 * v)
            )
        return carry

    lax.fori_loop(0, NO, sea, 0)

    loads[5].wait()

    def split_o(i, carry):
        MOC[i] = split_cat(MO[i])
        MOT[i] = split_cat(jnp.transpose(MO[i]))
        MAT[i] = split_cat(jnp.transpose(MA[i]))
        return carry

    lax.fori_loop(0, 16, split_o, 0)

    arrived(A1, R1.at[pl.ds(0, 16 * (peers - 1)), :])
    chosen = (R1[pl.ds(7, 128, stride=8), :] == (lane128 - jnp.where(low128, 0, 64)).astype(F32)).astype(F32)
    QM[...] = chosen.astype(BF16)
    PT[...] = jnp.transpose(chosen).astype(BF16)
    fields = [halves(PT[pl.ds(64, 16), :], split_cat(R1[pl.ds(f, 128, stride=8), :])) for f in range(7)]
    heat, salt, east, north, gain, fresh, shape = fields
    speed = jnp.sqrt(east * east + north * north + 0.5)
    flux = [
        speed * heat + gain,
        speed * salt + fresh,
        speed * east * (1.0 + 0.2 * jnp.tanh(shape)),
        speed * north,
    ]
    for g in range(8):
        FL[pl.ds(16 * g, 16), :] = flux[g % 4]
    for j in range(16):
        mapped[j] = quad(split_stack(FL[pl.ds(j, 8, stride=16), :]), MOC[j])

    def pack_mapped(n, carry):
        for m in range(8):
            t = n * 8 + m
            MSG2[pl.ds(pl.multiple_of(t * 8, 8), 8), :] = jnp.where(
                sub8 < 4, mapped[tab_s[1, 2 * t]], mapped[tab_s[1, 2 * t + 1]]
            )
        return carry

    lax.fori_loop(0, peers // 8, pack_mapped, 0)
    exchange(A2, 8, MSG2, lambda m: R2.at[pl.ds(pl.multiple_of(m * 8, 8), 8), :])
    R2[mine8, :] = MSG2[mine8, :]

    for copy in full_halo:
        copy.wait_recv()

    def atmos_field(src, dst, from_a, from_b, from_l, from_r, f):
        d = diff[f]
        both = jnp.where(even16, from_l[f], pltpu.roll(from_r[f], 126, 1))
        for lev in range(LEV):
            v = src[f, pl.ds(16 * lev, 16), :]
            edge = pltpu.roll(both, (128 - 2 * lev) % 128, 1)
            left = jnp.where(lane16 == 0, edge, pltpu.roll(v, 1, 1))
            right = jnp.where(lane16 == 127, edge, pltpu.roll(v, 127, 1))
            above = jnp.where(row16 == 0, from_a[f, pl.ds(lev, 1), :], pltpu.roll(v, 1, 0))
            below = jnp.where(row16 == 15, from_b[f, pl.ds(lev, 1), :], pltpu.roll(v, 15, 0))
            upper = v if lev == 0 else src[f, pl.ds(16 * lev - 16, 16), :]
            lower = v if lev == LEV - 1 else src[f, pl.ds(16 * lev + 16, 16), :]
            dst[f, pl.ds(16 * lev, 16), :] = (
                v + d * (above + below + left + right - 4.0 * v) + 0.1 * (upper + lower - 2.0 * v)
            )

    def first_step(f, carry):
        atmos_field(S, A, hf_a, hf_b, hf_l, hf_r, f)
        pack_atmos(A, r2_t, r2_b, k2, f)
        return carry

    lax.fori_loop(0, NF, first_step, 0)

    arrived(A2, R2.at[pl.ds(0, 8 * (peers - 1)), :])
    for g in range(NO):
        FOR[pl.ds(64 * g, 64), :] = halves(PT[pl.ds(0, 64), :], split_cat(R2[pl.ds(g, 128, stride=4), :]))
    twin_copy = remote(FOR, FORIN, COMP, twin)
    zero64 = jnp.zeros((64, 256), BF16)
    for g in range(NO):
        TOPC[g, pl.ds(64, 64), :] = zero64
        OEC[g, pl.ds(0, 64), :] = zero64
        OEC[g, pl.ds(64, 64), :] = zero64
    twin_copy.wait_recv()
    for g in range(NO):
        rows = pl.ds(64 * OLEV * g, 64)
        plane = pl.ds(64 * g, 64)
        top = ON[rows, :] + WN[0] * (FORCING_SCALE[g] * (FOR[plane, :] + FORIN[plane, :]))
        ON[rows, :] = top
        TOPC[g, pl.ds(0, 64), :] = split_cat(top)
    for g in range(NO):
        ANS[pl.ds(g, 128, stride=4), :] = halves(QM[...], TOPC[g])
    exchange(A3, 8, ANS, lambda m: B3.at[m])
    B3[me] = ANS[mine8, :]
    second_halo = halo(SECOND, r2_t, r2_b, k2, h2_a, h2_b, h2_l, h2_r, dev_down, dev_up)
    ocean_store = pltpu.make_async_copy(ON, ocean_out, out_sem.at[0])
    ocean_store.start()

    b3_all = B3.at[pl.ds(0, peers - 1)]
    arrived(A3, b3_all)
    for j in range(16):
        both = quad(split_stack(B3[o_owner[j]]), MOT[j])
        picked = jnp.where(o_rank[j] == 0, both, pltpu.roll(both, 4, 0))
        OE[pl.ds(j, 4, stride=16), :] = picked[0:4]
    for g in range(NO):
        OEC[g, pl.ds(64, 16), :] = split_cat(OE[pl.ds(16 * g, 16), :])
    for g in range(NO):
        REP[pl.ds(g, 128, stride=4), :] = halves(QM[...], OEC[g])
    exchange(A4, 8, REP, lambda m: B4.at[m])
    B4[me] = REP[mine8, :]

    for copy in second_halo:
        copy.wait_recv()

    def second_step(f, carry):
        atmos_field(A, N, h2_a, h2_b, h2_l, h2_r, f)
        return carry

    lax.fori_loop(0, NF, second_step, 0)
    atmos_store = pltpu.make_async_copy(N, atmos_out, out_sem.at[1])
    atmos_store.start()

    arrived(A4, B4.at[pl.ds(0, peers - 1)])
    for i in range(16):
        both = quad(split_stack(B4[e_owner[i]]), MAT[i])
        picked = jnp.where(e_rank[i] == 0, both, pltpu.roll(both, 4, 0))
        OSV[pl.ds(i, 4, stride=16), :] = picked[0:4]
    surf_store = pltpu.make_async_copy(OSV, surf_out, out_sem.at[2])
    surf_store.start()

    for copy in surface_halo + full_halo + ocean_halo + second_halo + [twin_copy]:
        copy.wait_send()
    departed(A1, MSG.at[pl.ds(0, 16 * (peers - 1)), :])
    departed(A2, MSG2.at[pl.ds(0, 8 * (peers - 1)), :])
    departed(A3, ANS.at[pl.ds(0, 8 * (peers - 1)), :])
    departed(A4, REP.at[pl.ds(0, 8 * (peers - 1)), :])
    ocean_store.wait()
    atmos_store.wait()
    surf_store.wait()


def hand_out(a, b, c, a_out, b_out, c_out, sem):
    copies = [pltpu.make_async_copy(x, y, sem.at[n]) for n, (x, y) in enumerate([(a, a_out), (b, b_out), (c, c_out)])]
    for copy in copies:
        copy.start()
    for copy in copies:
        copy.wait()


def on_device(
    sizes,
    atmos_state, atmos_diffusion, remap_atmos, exchange_owner, exchange_slot,
    remap_ocean, ocean_owner, ocean_slot, ocean_state, ocean_mixing, wet_mask,
):
    NC, NX, NY, NF, LEV, NO, OLEV = sizes
    peers = NX * NY
    hbm = pl.BlockSpec(memory_space=pltpu.HBM)
    any_ = pl.BlockSpec(memory_space=pl.ANY)

    def vm(*shape, dtype=F32):
        return pltpu.VMEM(shape, dtype)

    halo_atmos = [vm(NF, 24, 128), vm(NF, 24, 128), vm(NF, 16, 128), vm(NF, 24, 128), vm(NF, 24, 128), vm(NF, 16, 128), vm(NF, 16, 128)]
    scratch = (
        [vm(NF, 16 * LEV, 128) for _ in range(3)]
        + [vm(16, 128, 128), vm(16, 128, 128)]
        + [vm(16, 128, 256, dtype=BF16) for _ in range(4)]
        + [vm(NO * OLEV * 64, 128), vm(NO * OLEV * 64, 128), vm(64, 128, dtype=jnp.int32), vm(5, 64, 128)]
        + [vm(16, 128) for _ in range(7)]
        + halo_atmos
        + halo_atmos
        + [vm(40, 128), vm(40, 128), vm(64, 128), vm(40, 128), vm(40, 128), vm(64, 128), vm(64, 128)]
        + [vm(128, 128), vm(16, 8, 128), vm(16 * peers, 128), vm(16 * peers, 128)]
        + [vm(128, 128, dtype=BF16), vm(128, 128, dtype=BF16), vm(128, 128), vm(16, 8, 128)]
        + [vm(8 * peers, 128), vm(8 * peers, 128), vm(256, 128), vm(256, 128)]
        + [vm(NO, 128, 256, dtype=BF16), vm(8 * peers, 128), vm(peers, 8, 128), vm(64, 128)]
        + [vm(NO, 128, 256, dtype=BF16), vm(8 * peers, 128), vm(peers, 8, 128), vm(64, 128)]
        + [pltpu.SMEM((NF,), F32)] + [pltpu.SMEM((16,), jnp.int32) for _ in range(4)] + [pltpu.SMEM((NO,), F32)]
        + [vm(8, 128, dtype=jnp.int32), pltpu.SMEM((8, 128), jnp.int32)]
        + [
            pltpu.SemaphoreType.DMA((12,)),
            pltpu.SemaphoreType.DMA((3,)),
            pltpu.SemaphoreType.DMA((1,)),
            pltpu.SemaphoreType.DMA((SEMS,)),
            pltpu.SemaphoreType.DMA((SEMS,)),
            pltpu.SemaphoreType.REGULAR((1,)),
        ]
    )
    atmos_next, ocean_next, surface = pl.pallas_call(
        functools.partial(kernel, sizes),
        out_shape=(
            jax.ShapeDtypeStruct((NF, 16 * LEV, 128), F32),
            jax.ShapeDtypeStruct((NO * OLEV * 64, 128), F32),
            jax.ShapeDtypeStruct((64, 128), F32),
        ),
        in_specs=[hbm] * 11,
        out_specs=(any_, any_, any_),
        scratch_shapes=scratch,
        compiler_params=pltpu.CompilerParams(
            collective_id=0, has_side_effects=True, vmem_limit_bytes=40 * 1024 * 1024
        ),
    )(*(pltpu.with_memory_space_constraint(x, pltpu.HBM) for x in (
        atmos_state.reshape(NF, 16 * LEV, 128),
        remap_atmos,
        remap_ocean,
        ocean_state.reshape(NO * OLEV * 64, 128),
        wet_mask,
        atmos_diffusion, exchange_owner.reshape(16), exchange_slot, ocean_owner.reshape(16), ocean_slot, ocean_mixing,
    )))
    results = (atmos_next, ocean_next, surface)
    atmos_next, ocean_next, surface = pl.pallas_call(
        hand_out,
        out_shape=tuple(jax.ShapeDtypeStruct(x.shape, x.dtype) for x in results),
        in_specs=[any_] * 3,
        out_specs=(hbm, hbm, hbm),
        scratch_shapes=[pltpu.SemaphoreType.DMA((3,))],
        compiler_params=pltpu.CompilerParams(vmem_limit_bytes=1024 * 1024),
    )(*results)
    return (
        atmos_next.reshape(NF, LEV, 16, 128),
        ocean_next.reshape(NO, OLEV, 64, 128),
        surface.reshape(NO, 16, 128),
    )


def solution(mesh):
    sizes = (mesh.shape["comp"], mesh.shape["gx"], mesh.shape["gy"], 10, 20, 4, 8)
    in_specs = (
        P(None, None, ("comp", "gx"), "gy"),
        P(),
        P(("comp", "gx", "gy"), None, None),
        P(("comp", "gx", "gy"), None),
        P(("comp", "gx", "gy")),
        P(("comp", "gx", "gy"), None, None),
        P(("comp", "gx", "gy"), None),
        P(("comp", "gx", "gy")),
        P(None, None, "gx", "gy"),
        P(),
        P("gx", "gy"),
    )
    out_specs = (
        P(None, None, ("comp", "gx"), "gy"),
        P(None, None, "gx", "gy"),
        P(None, ("comp", "gx"), "gy"),
    )
    return jax.shard_map(
        functools.partial(on_device, sizes), mesh=mesh, in_specs=in_specs, out_specs=out_specs, check_vma=False
    )
```

```python
import functools

import jax
import jax.numpy as jnp
from jax import lax
from jax.experimental import pallas as pl
from jax.experimental.pallas import tpu as pltpu
from jax.sharding import PartitionSpec as P

MESH = pl.DeviceIdType.MESH
F32 = jnp.float32
BF16 = jnp.bfloat16
FORCING_SCALE = (0.1, -0.1, 0.1, 0.1)

SURF, FULL, SECOND, OCEAN, COMP, A1, A2, A3, A4, LABELS = 0, 4, 8, 12, 16, 17, 18, 19, 20, 21
SEMS = 22


def far_first(nx, ny):
    def way(n, offset, flip):
        total = 0
        for at in range(n):
            to = (at + offset) % n
            ahead = (to - at) % 4
            total += min(ahead, 4 - ahead) + flip * (to // 4 != at // 4)
        return total / n

    return sorted(range(1, nx * ny), key=lambda k: (-way(nx, k // ny, 2) - way(ny, k % ny, 1), k))


def split_cat(x):
    hi = x.astype(BF16)
    lo = (x - hi.astype(F32)).astype(BF16)
    return jnp.concatenate([hi, lo], axis=1)


def split_stack(x):
    hi = x.astype(BF16).astype(F32)
    return jnp.concatenate([hi, x - hi], axis=0).astype(BF16)


def dot(a, b):
    return jnp.dot(a, b, preferred_element_type=F32)


def quad(lhs, cat):
    full = dot(lhs, cat)
    return (full[:8, :128] + full[8:, :128]) + (full[:8, 128:] + full[8:, 128:])


def both_ranks(ref, first, apart, stride):
    return jnp.concatenate([ref[pl.ds(first + apart * c, 64, stride=stride), :] for c in range(2)], axis=0)


def put_ranks(ref, g, rows):
    for c in range(2):
        ref[pl.ds(g + 4 * c, 64, stride=8), :] = rows[64 * c : 64 * c + 64]


def halves(lhs, cat):
    full = dot(lhs, cat)
    return full[:, :128] + full[:, 128:]


def kernel(
    sizes,
    state, remap_a, remap_o, ocean, wet_in,
    diff_in, e_owner_in, e_slot_in, o_owner_in, o_slot_in, mixing_in,
    atmos_out, ocean_out, surf_out,
    S, A, N, MA, MO, MAC, MOC, MAT, MOT, O, ON, W, WN,
    rs_t, rs_b, ks, hs_a, hs_b, hs_l, hs_r,
    rf_t, rf_b, kf, hf_a, hf_b, hf_l, hf_r,
    r2_t, r2_b, k2, h2_a, h2_b, h2_l, h2_r,
    ro_t, ro_b, ko, ho_a, ho_b, ho_l, ho_r,
    NOTE, NOTES, X, pieces, shifted, MSG, R1, QM, PT, FL, mapped, MSG2, R2, FOR, FORIN,
    TOPC, ANS, B3, OE, OEC, REP, B4, OSV,
    diff, e_owner, e_slot, o_owner, o_slot, mixing,
    tab_v, tab_s,
    in_sem, out_sem, tab_sem, send, recv, row_here,
):
    NC, NX, NY, NF, LEV, NO, OLEV = sizes
    peers = NX * NY
    comp, gx, gy = lax.axis_index("comp"), lax.axis_index("gx"), lax.axis_index("gy")
    me = gx * NY + gy
    pos = comp * NX + gx
    ring = NC * NX
    down, up = lax.rem(pos + 1, ring), lax.rem(pos + ring - 1, ring)
    dev_down = (down // NX, lax.rem(down, NX), gy)
    dev_up = (up // NX, lax.rem(up, NX), gy)
    dev_right = (comp, gx, lax.rem(gy + 1, NY))
    dev_left = (comp, gx, lax.rem(gy + NY - 1, NY))
    sea_down = (comp, lax.rem(gx + 1, NX), gy)
    sea_up = (comp, lax.rem(gx + NX - 1, NX), gy)
    twin = (lax.rem(comp + 1, NC), gx, gy)

    def peer(k):
        px = lax.rem(gx + k // NY, NX)
        py = lax.rem(gy + lax.rem(k, NY), NY)
        return px, py, px * NY + py

    barrier = pltpu.get_barrier_semaphore()

    row_peers = [(comp, gx, lax.rem(gy + b, NY)) for b in range(1, NY)]
    column_peers = [(comp, lax.rem(gx + a, NX), gy) for a in range(1, NX)]
    greeted = row_peers + column_peers + [dev_down, dev_up, twin]
    for other in greeted:
        pl.semaphore_signal(barrier, inc=1, device_id=other, device_id_type=MESH)

    top_rows = 16 * (LEV - 2)
    loads = [
        pltpu.make_async_copy(state.at[:, pl.ds(top_rows, 32), :], S.at[:, pl.ds(top_rows, 32), :], in_sem.at[0]),
        pltpu.make_async_copy(state.at[:, pl.ds(0, top_rows), :], S.at[:, pl.ds(0, top_rows), :], in_sem.at[1]),
        pltpu.make_async_copy(ocean, O, in_sem.at[2]),
        pltpu.make_async_copy(wet_in, W, in_sem.at[3]),
        pltpu.make_async_copy(remap_a, MA, in_sem.at[4]),
        pltpu.make_async_copy(remap_o, MO, in_sem.at[5]),
    ]
    small = [
        pltpu.make_async_copy(src, dst, in_sem.at[6 + n])
        for n, (src, dst) in enumerate([
            (e_owner_in, e_owner), (o_owner_in, o_owner), (e_slot_in, e_slot), (o_slot_in, o_slot),
            (diff_in, diff), (mixing_in, mixing),
        ])
    ]
    for load in small + loads:
        load.start()

    lane16 = lax.broadcasted_iota(jnp.int32, (16, 128), 1)
    row16 = lax.broadcasted_iota(jnp.int32, (16, 128), 0)
    pair16 = lane16 // 2
    even16 = lane16 == pair16 * 2
    sub8 = lax.broadcasted_iota(jnp.int32, (8, 128), 0)

    def remote(src, dst, number, device):
        copy = pltpu.make_async_remote_copy(
            src_ref=src, dst_ref=dst, send_sem=send.at[number], recv_sem=recv.at[number],
            device_id=device, device_id_type=MESH,
        )
        copy.start()
        return copy

    def halo(number, rows_t, rows_b, cols, from_a, from_b, from_l, from_r, below, above):
        if len(rows_b.shape) == 3:
            used = pl.ds(0, LEV)
            rows_t, rows_b, from_a, from_b = (ref.at[:, used, :] for ref in (rows_t, rows_b, from_a, from_b))
        return [
            remote(rows_b, from_a, number, below),
            remote(rows_t, from_b, number + 1, above),
            remote(cols, from_l, number + 2, dev_right),
            remote(cols, from_r, number + 3, dev_left),
        ]

    loads[0].wait()
    last = 16 * (LEV - 1)
    packed = jnp.zeros((16, 128), F32)
    for f in range(NF):
        v = S[f, pl.ds(last, 16), :]
        packed = jnp.where(pair16 == f, pltpu.roll(v, 2 * f + 1, 1), packed)
        rs_t[pl.ds(f, 1), :] = v[0:1]
        rs_b[pl.ds(f, 1), :] = v[15:16]
    ks[...] = packed
    pl.semaphore_wait(barrier, len(greeted))
    surface_halo = halo(SURF, rs_t, rs_b, ks, hs_a, hs_b, hs_l, hs_r, dev_down, dev_up)
    for other in column_peers:
        pl.semaphore_signal(row_here.at[0], inc=1, device_id=other, device_id_type=MESH)

    def places(owner):
        ranks, keys = [], []
        for i in range(16):
            rank = jnp.int32(0)
            for j in range(i):
                rank = rank + (owner[j] == owner[i]).astype(jnp.int32)
            ranks.append(rank)
            keys.append(2 * owner[i] + rank)
        return ranks, keys

    for load in small:
        load.wait()
    e_rank, e_key = places(e_owner)
    o_rank, o_key = places(o_owner)
    lane8 = lax.broadcasted_iota(jnp.int32, (8, 128), 1)
    table = jnp.zeros((8, 128), jnp.int32)
    for i in range(16):
        table = jnp.where(lane8 == jnp.where(sub8 == 0, e_key[i], o_key[i]), i, table)
    tab_v[...] = table
    tab_copy = pltpu.make_async_copy(tab_v, tab_s, tab_sem.at[0])
    tab_copy.start()

    def pack_atmos(src, rows_t, rows_b, cols, f):
        kept = jnp.zeros((16, 128), F32)
        for lev in range(LEV):
            v = src[f, pl.ds(16 * lev, 16), :]
            kept = jnp.where(pair16 == lev, pltpu.roll(v, 2 * lev + 1, 1), kept)
        cols[f] = kept
        rows_t[f, pl.ds(0, LEV), :] = src[f, pl.ds(0, LEV, stride=16), :]
        rows_b[f, pl.ds(0, LEV), :] = src[f, pl.ds(15, LEV, stride=16), :]

    loads[2].wait()
    loads[3].wait()
    planes = NO * OLEV
    lane64 = lax.broadcasted_iota(jnp.int32, (64, 128), 1)
    row64 = lax.broadcasted_iota(jnp.int32, (64, 128), 0)
    pair64 = lane64 // 2
    wet = W[...].astype(F32)
    WN[0] = wet
    kept = jnp.where(pair64 == planes, pltpu.roll(wet, 2 * planes + 1, 1), 0.0)
    ko[...] = kept
    ro_t[pl.ds(planes, 1), :] = wet[0:1]
    ro_b[pl.ds(planes, 1), :] = wet[63:64]

    def pack_ocean(f, carry):
        kept = ko[...]
        for lev in range(OLEV):
            q = f * OLEV + lev
            v = O[pl.ds(pl.multiple_of(q * 64, 64), 64), :]
            kept = jnp.where(pair64 == q, pltpu.roll(v, 2 * q + 1, 1), kept)
        ko[...] = kept
        return carry

    lax.fori_loop(0, NO, pack_ocean, 0)
    ro_t[pl.ds(0, planes), :] = O[pl.ds(0, planes, stride=64), :]
    ro_b[pl.ds(0, planes), :] = O[pl.ds(63, planes, stride=64), :]
    ocean_halo = halo(OCEAN, ro_t, ro_b, ko, ho_a, ho_b, ho_l, ho_r, sea_down, sea_up)

    loads[4].wait()

    def split_a(i, carry):
        MAC[i] = split_cat(MA[i])
        return carry

    lax.fori_loop(0, 16, split_a, 0)

    lane1 = lax.broadcasted_iota(jnp.int32, (1, 128), 1)
    row = jnp.zeros((1, 128), jnp.int32)
    for i in range(16):
        for at, value in ((0, e_key[i]), (16, e_slot[i] + 1), (32, o_key[i]), (48, o_slot[i] + 1)):
            row = jnp.where(lane1 == at + i, value, row)
    NOTE[0] = row.astype(F32)
    NOTES[me] = row.astype(F32)
    pl.semaphore_wait(row_here.at[0], NX - 1)
    for k in far_first(NX, NY):
        px, py, _ = peer(k)
        remote(NOTE.at[0], NOTES.at[me], LABELS, (comp, px, py))

    tab_copy.wait()
    for copy in surface_halo:
        copy.wait_recv()
    kl, kr = hs_l[...], hs_r[...]
    cols = jnp.where(even16, kl, pltpu.roll(kr, 126, 1))
    after = []
    for f in range(NF):
        v = S[f, pl.ds(last, 16), :]
        edge = pltpu.roll(cols, (128 - 2 * f) % 128, 1)
        left = jnp.where(lane16 == 0, edge, pltpu.roll(v, 1, 1))
        right = jnp.where(lane16 == 127, edge, pltpu.roll(v, 127, 1))
        above = jnp.where(row16 == 0, hs_a[pl.ds(f, 1), :], pltpu.roll(v, 1, 0))
        below = jnp.where(row16 == 15, hs_b[pl.ds(f, 1), :], pltpu.roll(v, 15, 0))
        upper = S[f, pl.ds(last - 16, 16), :]
        after.append(v + diff[f] * (above + below + left + right - 4.0 * v) + 0.1 * (upper - v))
    combined = [after[0] - after[4], after[1], after[2], after[3], after[6] + after[7], after[5] + after[8], after[9], after[9]]
    for f in range(8):
        X[pl.ds(16 * f, 16), :] = combined[f]
    for i in range(16):
        piece = quad(split_stack(X[pl.ds(i, 8, stride=16), :]), MAC[i])
        pieces[i] = piece
        shifted[i] = pltpu.roll(piece, 7, 0)

    def pack_pieces(n, carry):
        for m in range(4):
            t = n * 4 + m
            one, two = pieces[tab_s[0, 2 * t]], shifted[tab_s[0, 2 * t + 1]]
            MSG[pl.ds(pl.multiple_of(t * 16, 16), 8), :] = jnp.where(sub8 < 7, one, two)
            MSG[pl.ds(pl.multiple_of(t * 16 + 8, 8), 8), :] = two
        return carry

    lax.fori_loop(0, 16, pack_pieces, 0)

    def exchange(number, rows, sent, src, dst_of):
        def step(k, carry):
            px, py, target = peer(k)
            remote(src.at[pl.ds(pl.multiple_of(target * rows, 8), sent), :], dst_of(me), number, (comp, px, py))
            return carry

        for k in far_first(NX, NY):
            step(k, 0)

    def arrived(number, count_ref):
        pltpu.make_async_copy(count_ref, count_ref, recv.at[number]).wait()

    def departed(number, count_ref):
        pltpu.make_async_copy(count_ref, count_ref, send.at[number]).wait()

    mine16 = pl.ds(pl.multiple_of(me * 16, 16), 16)
    mine8 = pl.ds(pl.multiple_of(me * 8, 8), 8)
    exchange(A1, 16, 14, MSG, lambda m: R1.at[pl.ds(pl.multiple_of(m * 16, 16), 14), :])
    R1[mine16, :] = MSG[mine16, :]

    for copy in ocean_halo:
        copy.wait_recv()
    ol, orr = ho_l[...], ho_r[...]
    even64 = lane64 == pair64 * 2
    ho_l[...] = jnp.where(even64, ol, pltpu.roll(orr, 126, 1))

    def around(v, q, edges):
        edge = pltpu.roll(edges, 128 - 2 * q, 1)
        left = jnp.where(lane64 == 0, edge, pltpu.roll(v, 1, 1))
        right = jnp.where(lane64 == 127, edge, pltpu.roll(v, 127, 1))
        above = jnp.where(row64 == 0, ho_a[pl.ds(q, 1), :], pltpu.roll(v, 1, 0))
        below = jnp.where(row64 == 63, ho_b[pl.ds(q, 1), :], pltpu.roll(v, 63, 0))
        return above, below, left, right

    for n, w in enumerate(around(wet, planes, ho_l[...])):
        WN[1 + n] = w

    def sea(f, carry):
        mix = mixing[f]
        base = f * OLEV
        for lev in range(OLEV):
            q = base + lev
            v = O[pl.ds(pl.multiple_of(q * 64, 64), 64), :]
            total = jnp.zeros((64, 128), F32)
            edges = pltpu.roll(ho_l[...], 128 - 2 * q, 1)
            left = jnp.where(lane64 == 0, edges, pltpu.roll(v, 1, 1))
            right = jnp.where(lane64 == 127, edges, pltpu.roll(v, 127, 1))
            above = jnp.where(row64 == 0, ho_a[pl.ds(q, 1), :], pltpu.roll(v, 1, 0))
            below = jnp.where(row64 == 63, ho_b[pl.ds(q, 1), :], pltpu.roll(v, 63, 0))
            total = WN[1] * (above - v) + WN[2] * (below - v) + WN[3] * (left - v) + WN[4] * (right - v)
            upper = v if lev == 0 else O[pl.ds(pl.multiple_of(q * 64 - 64, 64), 64), :]
            lower = v if lev == OLEV - 1 else O[pl.ds(pl.multiple_of(q * 64 + 64, 64), 64), :]
            w = WN[0]
            ON[pl.ds(pl.multiple_of(q * 64, 64), 64), :] = v + w * (
                mix * w * total + 0.1 * (upper + lower - 2.0 * v)
            )
        return carry

    lax.fori_loop(0, NO, sea, 0)

    loads[5].wait()

    def split_o(i, carry):
        MOC[i] = split_cat(MO[i])
        MOT[i] = split_cat(jnp.transpose(MO[i]))
        MAT[i] = split_cat(jnp.transpose(MA[i]))
        return carry

    lax.fori_loop(0, 16, split_o, 0)

    loads[1].wait()

    def pack_first(f, carry):
        pack_atmos(S, rf_t, rf_b, kf, f)
        return carry

    lax.fori_loop(0, NF, pack_first, 0)
    full_halo = halo(FULL, rf_t, rf_b, kf, hf_a, hf_b, hf_l, hf_r, dev_down, dev_up)

    arrived(LABELS, NOTES.at[pl.ds(0, peers - 1)])
    notes = NOTES[:, 0, :]
    slots = pltpu.roll(notes, 112, 1)
    labels = []
    for c in range(2):
        hit = notes == (2 * me + c).astype(F32)
        of_e = jnp.sum(jnp.where(hit & (lane64 < 16), slots, 0.0), axis=1, keepdims=True) - 1.0
        of_o = jnp.sum(jnp.where(hit & (lane64 >= 32) & (lane64 < 48), slots, 0.0), axis=1, keepdims=True) - 1.0
        labels.append(jnp.where(lane64 < 64, of_o, of_e))
    lane128 = lax.broadcasted_iota(jnp.int32, (128, 128), 1)
    place = (lane128 - jnp.where(lane128 < 64, 0, 64)).astype(F32)
    chosen = (jnp.concatenate(labels, axis=0) == place).astype(F32)
    QM[...] = chosen.astype(BF16)
    PT[...] = jnp.transpose(chosen).astype(BF16)

    arrived(A1, R1.at[pl.ds(0, 14 * (peers - 1)), :])
    fields = [halves(PT[pl.ds(64, 16), :], split_cat(both_ranks(R1, f, 7, 16))) for f in range(7)]
    heat, salt, east, north, gain, fresh, shape = fields
    speed = jnp.sqrt(east * east + north * north + 0.5)
    flux = [
        speed * heat + gain,
        speed * salt + fresh,
        speed * east * (1.0 + 0.2 * jnp.tanh(shape)),
        speed * north,
    ]
    for g in range(8):
        FL[pl.ds(16 * g, 16), :] = flux[g % 4]
    for j in range(16):
        mapped[j] = quad(split_stack(FL[pl.ds(j, 8, stride=16), :]), MOC[j])

    def pack_mapped(n, carry):
        for m in range(8):
            t = n * 8 + m
            MSG2[pl.ds(pl.multiple_of(t * 8, 8), 8), :] = jnp.where(
                sub8 < 4, mapped[tab_s[1, 2 * t]], mapped[tab_s[1, 2 * t + 1]]
            )
        return carry

    lax.fori_loop(0, peers // 8, pack_mapped, 0)
    exchange(A2, 8, 8, MSG2, lambda m: R2.at[pl.ds(pl.multiple_of(m * 8, 8), 8), :])
    R2[mine8, :] = MSG2[mine8, :]

    for copy in full_halo:
        copy.wait_recv()

    def atmos_field(src, dst, from_a, from_b, from_l, from_r, f):
        d = diff[f]
        both = jnp.where(even16, from_l[f], pltpu.roll(from_r[f], 126, 1))
        for lev in range(LEV):
            v = src[f, pl.ds(16 * lev, 16), :]
            edge = pltpu.roll(both, (128 - 2 * lev) % 128, 1)
            left = jnp.where(lane16 == 0, edge, pltpu.roll(v, 1, 1))
            right = jnp.where(lane16 == 127, edge, pltpu.roll(v, 127, 1))
            above = jnp.where(row16 == 0, from_a[f, pl.ds(lev, 1), :], pltpu.roll(v, 1, 0))
            below = jnp.where(row16 == 15, from_b[f, pl.ds(lev, 1), :], pltpu.roll(v, 15, 0))
            upper = v if lev == 0 else src[f, pl.ds(16 * lev - 16, 16), :]
            lower = v if lev == LEV - 1 else src[f, pl.ds(16 * lev + 16, 16), :]
            dst[f, pl.ds(16 * lev, 16), :] = (
                v + d * (above + below + left + right - 4.0 * v) + 0.1 * (upper + lower - 2.0 * v)
            )

    def first_step(f, carry):
        atmos_field(S, A, hf_a, hf_b, hf_l, hf_r, f)
        pack_atmos(A, r2_t, r2_b, k2, f)
        return carry

    lax.fori_loop(0, NF, first_step, 0)

    arrived(A2, R2.at[pl.ds(0, 8 * (peers - 1)), :])
    for g in range(NO):
        FOR[pl.ds(64 * g, 64), :] = halves(PT[pl.ds(0, 64), :], split_cat(both_ranks(R2, g, 4, 8)))
    twin_copy = remote(FOR, FORIN, COMP, twin)
    zero64 = jnp.zeros((64, 256), BF16)
    for g in range(NO):
        TOPC[g, pl.ds(64, 64), :] = zero64
        OEC[g, pl.ds(0, 64), :] = zero64
        OEC[g, pl.ds(64, 64), :] = zero64
    twin_copy.wait_recv()
    for g in range(NO):
        rows = pl.ds(64 * OLEV * g, 64)
        plane = pl.ds(64 * g, 64)
        top = ON[rows, :] + WN[0] * (FORCING_SCALE[g] * (FOR[plane, :] + FORIN[plane, :]))
        ON[rows, :] = top
        TOPC[g, pl.ds(0, 64), :] = split_cat(top)
    for g in range(NO):
        put_ranks(ANS, g, halves(QM[...], TOPC[g]))
    exchange(A3, 8, 8, ANS, lambda m: B3.at[m])
    B3[me] = ANS[mine8, :]
    second_halo = halo(SECOND, r2_t, r2_b, k2, h2_a, h2_b, h2_l, h2_r, dev_down, dev_up)
    ocean_store = pltpu.make_async_copy(ON, ocean_out, out_sem.at[0])
    ocean_store.start()

    b3_all = B3.at[pl.ds(0, peers - 1)]
    arrived(A3, b3_all)
    for j in range(16):
        both = quad(split_stack(B3[o_owner[j]]), MOT[j])
        picked = jnp.where(o_rank[j] == 0, both, pltpu.roll(both, 4, 0))
        OE[pl.ds(j, 4, stride=16), :] = picked[0:4]
    for g in range(NO):
        OEC[g, pl.ds(64, 16), :] = split_cat(OE[pl.ds(16 * g, 16), :])
    for g in range(NO):
        put_ranks(REP, g, halves(QM[...], OEC[g]))
    exchange(A4, 8, 8, REP, lambda m: B4.at[m])
    B4[me] = REP[mine8, :]

    for copy in second_halo:
        copy.wait_recv()

    def second_step(f, carry):
        atmos_field(A, N, h2_a, h2_b, h2_l, h2_r, f)
        return carry

    lax.fori_loop(0, NF, second_step, 0)
    atmos_store = pltpu.make_async_copy(N, atmos_out, out_sem.at[1])
    atmos_store.start()

    arrived(A4, B4.at[pl.ds(0, peers - 1)])
    for i in range(16):
        both = quad(split_stack(B4[e_owner[i]]), MAT[i])
        picked = jnp.where(e_rank[i] == 0, both, pltpu.roll(both, 4, 0))
        OSV[pl.ds(i, 4, stride=16), :] = picked[0:4]
    surf_store = pltpu.make_async_copy(OSV, surf_out, out_sem.at[2])
    surf_store.start()

    for copy in surface_halo + full_halo + ocean_halo + second_halo + [twin_copy]:
        copy.wait_send()
    departed(A1, MSG.at[pl.ds(0, 14 * (peers - 1)), :])
    departed(LABELS, NOTES.at[pl.ds(0, peers - 1)])
    departed(A2, MSG2.at[pl.ds(0, 8 * (peers - 1)), :])
    departed(A3, ANS.at[pl.ds(0, 8 * (peers - 1)), :])
    departed(A4, REP.at[pl.ds(0, 8 * (peers - 1)), :])
    ocean_store.wait()
    atmos_store.wait()
    surf_store.wait()


def hand_out(a, b, c, a_out, b_out, c_out, sem):
    copies = [pltpu.make_async_copy(x, y, sem.at[n]) for n, (x, y) in enumerate([(a, a_out), (b, b_out), (c, c_out)])]
    for copy in copies:
        copy.start()
    for copy in copies:
        copy.wait()


def on_device(
    sizes,
    atmos_state, atmos_diffusion, remap_atmos, exchange_owner, exchange_slot,
    remap_ocean, ocean_owner, ocean_slot, ocean_state, ocean_mixing, wet_mask,
):
    NC, NX, NY, NF, LEV, NO, OLEV = sizes
    peers = NX * NY
    hbm = pl.BlockSpec(memory_space=pltpu.HBM)
    any_ = pl.BlockSpec(memory_space=pl.ANY)

    def vm(*shape, dtype=F32):
        return pltpu.VMEM(shape, dtype)

    halo_atmos = [vm(NF, 24, 128), vm(NF, 24, 128), vm(NF, 16, 128), vm(NF, 24, 128), vm(NF, 24, 128), vm(NF, 16, 128), vm(NF, 16, 128)]
    scratch = (
        [vm(NF, 16 * LEV, 128) for _ in range(3)]
        + [vm(16, 128, 128), vm(16, 128, 128)]
        + [vm(16, 128, 256, dtype=BF16) for _ in range(4)]
        + [vm(NO * OLEV * 64, 128), vm(NO * OLEV * 64, 128), vm(64, 128, dtype=jnp.int32), vm(5, 64, 128)]
        + [vm(16, 128) for _ in range(7)]
        + halo_atmos
        + halo_atmos
        + [vm(40, 128), vm(40, 128), vm(64, 128), vm(40, 128), vm(40, 128), vm(64, 128), vm(64, 128)]
        + [vm(1, 1, 128), vm(peers, 1, 128), vm(128, 128), vm(16, 8, 128), vm(16, 8, 128), vm(16 * peers, 128), vm(16 * peers, 128)]
        + [vm(128, 128, dtype=BF16), vm(128, 128, dtype=BF16), vm(128, 128), vm(16, 8, 128)]
        + [vm(8 * peers, 128), vm(8 * peers, 128), vm(256, 128), vm(256, 128)]
        + [vm(NO, 128, 256, dtype=BF16), vm(8 * peers, 128), vm(peers, 8, 128), vm(64, 128)]
        + [vm(NO, 128, 256, dtype=BF16), vm(8 * peers, 128), vm(peers, 8, 128), vm(64, 128)]
        + [pltpu.SMEM((NF,), F32)] + [pltpu.SMEM((16,), jnp.int32) for _ in range(4)] + [pltpu.SMEM((NO,), F32)]
        + [vm(8, 128, dtype=jnp.int32), pltpu.SMEM((8, 128), jnp.int32)]
        + [
            pltpu.SemaphoreType.DMA((12,)),
            pltpu.SemaphoreType.DMA((3,)),
            pltpu.SemaphoreType.DMA((1,)),
            pltpu.SemaphoreType.DMA((SEMS,)),
            pltpu.SemaphoreType.DMA((SEMS,)),
            pltpu.SemaphoreType.REGULAR((1,)),
        ]
    )
    atmos_next, ocean_next, surface = pl.pallas_call(
        functools.partial(kernel, sizes),
        out_shape=(
            jax.ShapeDtypeStruct((NF, 16 * LEV, 128), F32),
            jax.ShapeDtypeStruct((NO * OLEV * 64, 128), F32),
            jax.ShapeDtypeStruct((64, 128), F32),
        ),
        in_specs=[hbm] * 11,
        out_specs=(any_, any_, any_),
        scratch_shapes=scratch,
        compiler_params=pltpu.CompilerParams(
            collective_id=0, has_side_effects=True, vmem_limit_bytes=40 * 1024 * 1024
        ),
    )(*(pltpu.with_memory_space_constraint(x, pltpu.HBM) for x in (
        atmos_state.reshape(NF, 16 * LEV, 128),
        remap_atmos,
        remap_ocean,
        ocean_state.reshape(NO * OLEV * 64, 128),
        wet_mask,
        atmos_diffusion, exchange_owner.reshape(16), exchange_slot, ocean_owner.reshape(16), ocean_slot, ocean_mixing,
    )))
    results = (atmos_next, ocean_next, surface)
    atmos_next, ocean_next, surface = pl.pallas_call(
        hand_out,
        out_shape=tuple(jax.ShapeDtypeStruct(x.shape, x.dtype) for x in results),
        in_specs=[any_] * 3,
        out_specs=(hbm, hbm, hbm),
        scratch_shapes=[pltpu.SemaphoreType.DMA((3,))],
        compiler_params=pltpu.CompilerParams(vmem_limit_bytes=1024 * 1024),
    )(*results)
    return (
        atmos_next.reshape(NF, LEV, 16, 128),
        ocean_next.reshape(NO, OLEV, 64, 128),
        surface.reshape(NO, 16, 128),
    )


def solution(mesh):
    sizes = (mesh.shape["comp"], mesh.shape["gx"], mesh.shape["gy"], 10, 20, 4, 8)
    in_specs = (
        P(None, None, ("comp", "gx"), "gy"),
        P(),
        P(("comp", "gx", "gy"), None, None),
        P(("comp", "gx", "gy"), None),
        P(("comp", "gx", "gy")),
        P(("comp", "gx", "gy"), None, None),
        P(("comp", "gx", "gy"), None),
        P(("comp", "gx", "gy")),
        P(None, None, "gx", "gy"),
        P(),
        P("gx", "gy"),
    )
    out_specs = (
        P(None, None, ("comp", "gx"), "gy"),
        P(None, None, "gx", "gy"),
        P(None, ("comp", "gx"), "gy"),
    )
    return jax.shard_map(
        functools.partial(on_device, sizes), mesh=mesh, in_specs=in_specs, out_specs=out_specs, check_vma=False
    )
```

```python
import functools

import jax
import jax.numpy as jnp
from jax import lax
from jax.experimental import pallas as pl
from jax.experimental.pallas import tpu as pltpu
from jax.sharding import PartitionSpec as P

MESH = pl.DeviceIdType.MESH
F32 = jnp.float32
BF16 = jnp.bfloat16
FORCING_SCALE = (0.1, -0.1, 0.1, 0.1)

SURF, FULL, SECOND, OCEAN, COMP, A1, A2, A3, A4, LABELS = 0, 4, 8, 12, 16, 17, 18, 19, 20, 21
SEMS = 22


def far_first(nx, ny):
    def way(n, offset, flip):
        total = 0
        for at in range(n):
            to = (at + offset) % n
            ahead = (to - at) % 4
            total = max(total, min(ahead, 4 - ahead) + flip * (to // 4 != at // 4))
        return total

    return sorted(range(1, nx * ny), key=lambda k: (-way(nx, k // ny, 2) - way(ny, k % ny, 1), k))


def split_cat(x):
    hi = x.astype(BF16)
    lo = (x - hi.astype(F32)).astype(BF16)
    return jnp.concatenate([hi, lo], axis=1)


def split_stack(x):
    hi = x.astype(BF16).astype(F32)
    return jnp.concatenate([hi, x - hi], axis=0).astype(BF16)


def dot(a, b):
    return jnp.dot(a, b, preferred_element_type=F32)


def quad(lhs, cat):
    full = dot(lhs, cat)
    return (full[:8, :128] + full[8:, :128]) + (full[:8, 128:] + full[8:, 128:])


def both_ranks(ref, first, apart, stride):
    return jnp.concatenate([ref[pl.ds(first + apart * c, 64, stride=stride), :] for c in range(2)], axis=0)


def put_ranks(ref, g, rows):
    for c in range(2):
        ref[pl.ds(g + 4 * c, 64, stride=8), :] = rows[64 * c : 64 * c + 64]


def halves(lhs, cat):
    full = dot(lhs, cat)
    return full[:, :128] + full[:, 128:]


def kernel(
    sizes,
    state, remap_a, remap_o, ocean, wet_in,
    diff_in, e_owner_in, e_slot_in, o_owner_in, o_slot_in, mixing_in,
    atmos_out, ocean_out, surf_out,
    S, A, N, MA, MO, MAC, MOC, MAT, MOT, O, ON, W, WN,
    rs_t, rs_b, ks, hs_a, hs_b, hs_l, hs_r,
    rf_t, rf_b, kf, hf_a, hf_b, hf_l, hf_r,
    r2_t, r2_b, k2, h2_a, h2_b, h2_l, h2_r,
    ro_t, ro_b, ko, ho_a, ho_b, ho_l, ho_r,
    NOTE, NOTES, X, pieces, shifted, MSG, R1, QM, PT, FL, mapped, MSG2, R2, FOR, FORIN,
    TOPC, ANS, B3, OE, OEC, REP, B4, OSV,
    diff, e_owner, e_slot, o_owner, o_slot, mixing,
    tab_v, tab_s,
    in_sem, out_sem, tab_sem, send, recv, row_here,
):
    NC, NX, NY, NF, LEV, NO, OLEV = sizes
    peers = NX * NY
    comp, gx, gy = lax.axis_index("comp"), lax.axis_index("gx"), lax.axis_index("gy")
    me = gx * NY + gy
    pos = comp * NX + gx
    ring = NC * NX
    down, up = lax.rem(pos + 1, ring), lax.rem(pos + ring - 1, ring)
    dev_down = (down // NX, lax.rem(down, NX), gy)
    dev_up = (up // NX, lax.rem(up, NX), gy)
    dev_right = (comp, gx, lax.rem(gy + 1, NY))
    dev_left = (comp, gx, lax.rem(gy + NY - 1, NY))
    sea_down = (comp, lax.rem(gx + 1, NX), gy)
    sea_up = (comp, lax.rem(gx + NX - 1, NX), gy)
    twin = (lax.rem(comp + 1, NC), gx, gy)

    def peer(k):
        px = lax.rem(gx + k // NY, NX)
        py = lax.rem(gy + lax.rem(k, NY), NY)
        return px, py, px * NY + py

    barrier = pltpu.get_barrier_semaphore()

    row_peers = [(comp, gx, lax.rem(gy + b, NY)) for b in range(1, NY)]
    column_peers = [(comp, lax.rem(gx + a, NX), gy) for a in range(1, NX)]
    greeted = row_peers + column_peers + [dev_down, dev_up, twin]
    for other in greeted:
        pl.semaphore_signal(barrier, inc=1, device_id=other, device_id_type=MESH)

    top_rows = 16 * (LEV - 2)
    loads = [
        pltpu.make_async_copy(state.at[:, pl.ds(top_rows, 32), :], S.at[:, pl.ds(top_rows, 32), :], in_sem.at[0]),
        pltpu.make_async_copy(state.at[:, pl.ds(0, top_rows), :], S.at[:, pl.ds(0, top_rows), :], in_sem.at[1]),
        pltpu.make_async_copy(ocean, O, in_sem.at[2]),
        pltpu.make_async_copy(wet_in, W, in_sem.at[3]),
        pltpu.make_async_copy(remap_a, MA, in_sem.at[4]),
        pltpu.make_async_copy(remap_o, MO, in_sem.at[5]),
    ]
    small = [
        pltpu.make_async_copy(src, dst, in_sem.at[6 + n])
        for n, (src, dst) in enumerate([
            (e_owner_in, e_owner), (o_owner_in, o_owner), (e_slot_in, e_slot), (o_slot_in, o_slot),
            (diff_in, diff), (mixing_in, mixing),
        ])
    ]
    for load in small + loads:
        load.start()

    lane16 = lax.broadcasted_iota(jnp.int32, (16, 128), 1)
    row16 = lax.broadcasted_iota(jnp.int32, (16, 128), 0)
    pair16 = lane16 // 2
    even16 = lane16 == pair16 * 2
    sub8 = lax.broadcasted_iota(jnp.int32, (8, 128), 0)

    def remote(src, dst, number, device):
        copy = pltpu.make_async_remote_copy(
            src_ref=src, dst_ref=dst, send_sem=send.at[number], recv_sem=recv.at[number],
            device_id=device, device_id_type=MESH,
        )
        copy.start()
        return copy

    def halo(number, rows_t, rows_b, cols, from_a, from_b, from_l, from_r, below, above):
        if len(rows_b.shape) == 3:
            used = pl.ds(0, LEV)
            rows_t, rows_b, from_a, from_b = (ref.at[:, used, :] for ref in (rows_t, rows_b, from_a, from_b))
        return [
            remote(rows_b, from_a, number, below),
            remote(rows_t, from_b, number + 1, above),
            remote(cols, from_l, number + 2, dev_right),
            remote(cols, from_r, number + 3, dev_left),
        ]

    loads[0].wait()
    last = 16 * (LEV - 1)
    packed = jnp.zeros((16, 128), F32)
    for f in range(NF):
        v = S[f, pl.ds(last, 16), :]
        packed = jnp.where(pair16 == f, pltpu.roll(v, 2 * f + 1, 1), packed)
        rs_t[pl.ds(f, 1), :] = v[0:1]
        rs_b[pl.ds(f, 1), :] = v[15:16]
    ks[...] = packed
    pl.semaphore_wait(barrier, len(greeted))
    surface_halo = halo(SURF, rs_t, rs_b, ks, hs_a, hs_b, hs_l, hs_r, dev_down, dev_up)
    for other in column_peers:
        pl.semaphore_signal(row_here.at[0], inc=1, device_id=other, device_id_type=MESH)

    def places(owner):
        ranks, keys = [], []
        for i in range(16):
            rank = jnp.int32(0)
            for j in range(i):
                rank = rank + (owner[j] == owner[i]).astype(jnp.int32)
            ranks.append(rank)
            keys.append(2 * owner[i] + rank)
        return ranks, keys

    for load in small:
        load.wait()
    e_rank, e_key = places(e_owner)
    o_rank, o_key = places(o_owner)
    lane8 = lax.broadcasted_iota(jnp.int32, (8, 128), 1)
    table = jnp.zeros((8, 128), jnp.int32)
    for i in range(16):
        table = jnp.where(lane8 == jnp.where(sub8 == 0, e_key[i], o_key[i]), i, table)
    tab_v[...] = table
    tab_copy = pltpu.make_async_copy(tab_v, tab_s, tab_sem.at[0])
    tab_copy.start()

    def pack_atmos(src, rows_t, rows_b, cols, f):
        kept = jnp.zeros((16, 128), F32)
        for lev in range(LEV):
            v = src[f, pl.ds(16 * lev, 16), :]
            kept = jnp.where(pair16 == lev, pltpu.roll(v, 2 * lev + 1, 1), kept)
        cols[f] = kept
        rows_t[f, pl.ds(0, LEV), :] = src[f, pl.ds(0, LEV, stride=16), :]
        rows_b[f, pl.ds(0, LEV), :] = src[f, pl.ds(15, LEV, stride=16), :]

    loads[2].wait()
    loads[3].wait()
    planes = NO * OLEV
    lane64 = lax.broadcasted_iota(jnp.int32, (64, 128), 1)
    row64 = lax.broadcasted_iota(jnp.int32, (64, 128), 0)
    pair64 = lane64 // 2
    wet = W[...].astype(F32)
    WN[0] = wet
    kept = jnp.where(pair64 == planes, pltpu.roll(wet, 2 * planes + 1, 1), 0.0)
    ko[...] = kept
    ro_t[pl.ds(planes, 1), :] = wet[0:1]
    ro_b[pl.ds(planes, 1), :] = wet[63:64]

    def pack_ocean(f, carry):
        kept = ko[...]
        for lev in range(OLEV):
            q = f * OLEV + lev
            v = O[pl.ds(pl.multiple_of(q * 64, 64), 64), :]
            kept = jnp.where(pair64 == q, pltpu.roll(v, 2 * q + 1, 1), kept)
        ko[...] = kept
        return carry

    lax.fori_loop(0, NO, pack_ocean, 0)
    ro_t[pl.ds(0, planes), :] = O[pl.ds(0, planes, stride=64), :]
    ro_b[pl.ds(0, planes), :] = O[pl.ds(63, planes, stride=64), :]
    ocean_halo = halo(OCEAN, ro_t, ro_b, ko, ho_a, ho_b, ho_l, ho_r, sea_down, sea_up)

    loads[4].wait()

    def split_a(i, carry):
        MAC[i] = split_cat(MA[i])
        return carry

    lax.fori_loop(0, 16, split_a, 0)

    lane1 = lax.broadcasted_iota(jnp.int32, (1, 128), 1)
    row = jnp.zeros((1, 128), jnp.int32)
    for i in range(16):
        for at, value in ((0, e_key[i]), (16, e_slot[i] + 1), (32, o_key[i]), (48, o_slot[i] + 1)):
            row = jnp.where(lane1 == at + i, value, row)
    NOTE[0] = row.astype(F32)
    NOTES[me] = row.astype(F32)
    pl.semaphore_wait(row_here.at[0], NX - 1)
    for k in far_first(NX, NY):
        px, py, _ = peer(k)
        remote(NOTE.at[0], NOTES.at[me], LABELS, (comp, px, py))

    tab_copy.wait()
    for copy in surface_halo:
        copy.wait_recv()
    kl, kr = hs_l[...], hs_r[...]
    cols = jnp.where(even16, kl, pltpu.roll(kr, 126, 1))
    after = []
    for f in range(NF):
        v = S[f, pl.ds(last, 16), :]
        edge = pltpu.roll(cols, (128 - 2 * f) % 128, 1)
        left = jnp.where(lane16 == 0, edge, pltpu.roll(v, 1, 1))
        right = jnp.where(lane16 == 127, edge, pltpu.roll(v, 127, 1))
        above = jnp.where(row16 == 0, hs_a[pl.ds(f, 1), :], pltpu.roll(v, 1, 0))
        below = jnp.where(row16 == 15, hs_b[pl.ds(f, 1), :], pltpu.roll(v, 15, 0))
        upper = S[f, pl.ds(last - 16, 16), :]
        after.append(v + diff[f] * (above + below + left + right - 4.0 * v) + 0.1 * (upper - v))
    combined = [after[0] - after[4], after[1], after[2], after[3], after[6] + after[7], after[5] + after[8], after[9], after[9]]
    for f in range(8):
        X[pl.ds(16 * f, 16), :] = combined[f]
    for i in range(16):
        piece = quad(split_stack(X[pl.ds(i, 8, stride=16), :]), MAC[i])
        pieces[i] = piece
        shifted[i] = pltpu.roll(piece, 7, 0)

    def pack_pieces(n, carry):
        for m in range(4):
            t = n * 4 + m
            one, two = pieces[tab_s[0, 2 * t]], shifted[tab_s[0, 2 * t + 1]]
            MSG[pl.ds(pl.multiple_of(t * 16, 16), 8), :] = jnp.where(sub8 < 7, one, two)
            MSG[pl.ds(pl.multiple_of(t * 16 + 8, 8), 8), :] = two
        return carry

    lax.fori_loop(0, 16, pack_pieces, 0)

    def exchange(number, rows, sent, src, dst_of):
        def step(k, carry):
            px, py, target = peer(k)
            remote(src.at[pl.ds(pl.multiple_of(target * rows, 8), sent), :], dst_of(me), number, (comp, px, py))
            return carry

        for k in far_first(NX, NY):
            step(k, 0)

    def arrived(number, count_ref):
        pltpu.make_async_copy(count_ref, count_ref, recv.at[number]).wait()

    def departed(number, count_ref):
        pltpu.make_async_copy(count_ref, count_ref, send.at[number]).wait()

    mine16 = pl.ds(pl.multiple_of(me * 16, 16), 16)
    mine8 = pl.ds(pl.multiple_of(me * 8, 8), 8)
    exchange(A1, 16, 14, MSG, lambda m: R1.at[pl.ds(pl.multiple_of(m * 16, 16), 14), :])
    R1[mine16, :] = MSG[mine16, :]

    for copy in ocean_halo:
        copy.wait_recv()
    ol, orr = ho_l[...], ho_r[...]
    even64 = lane64 == pair64 * 2
    ho_l[...] = jnp.where(even64, ol, pltpu.roll(orr, 126, 1))

    def around(v, q, edges):
        edge = pltpu.roll(edges, 128 - 2 * q, 1)
        left = jnp.where(lane64 == 0, edge, pltpu.roll(v, 1, 1))
        right = jnp.where(lane64 == 127, edge, pltpu.roll(v, 127, 1))
        above = jnp.where(row64 == 0, ho_a[pl.ds(q, 1), :], pltpu.roll(v, 1, 0))
        below = jnp.where(row64 == 63, ho_b[pl.ds(q, 1), :], pltpu.roll(v, 63, 0))
        return above, below, left, right

    for n, w in enumerate(around(wet, planes, ho_l[...])):
        WN[1 + n] = w

    def sea(f, carry):
        mix = mixing[f]
        base = f * OLEV
        for lev in range(OLEV):
            q = base + lev
            v = O[pl.ds(pl.multiple_of(q * 64, 64), 64), :]
            total = jnp.zeros((64, 128), F32)
            edges = pltpu.roll(ho_l[...], 128 - 2 * q, 1)
            left = jnp.where(lane64 == 0, edges, pltpu.roll(v, 1, 1))
            right = jnp.where(lane64 == 127, edges, pltpu.roll(v, 127, 1))
            above = jnp.where(row64 == 0, ho_a[pl.ds(q, 1), :], pltpu.roll(v, 1, 0))
            below = jnp.where(row64 == 63, ho_b[pl.ds(q, 1), :], pltpu.roll(v, 63, 0))
            total = WN[1] * (above - v) + WN[2] * (below - v) + WN[3] * (left - v) + WN[4] * (right - v)
            upper = v if lev == 0 else O[pl.ds(pl.multiple_of(q * 64 - 64, 64), 64), :]
            lower = v if lev == OLEV - 1 else O[pl.ds(pl.multiple_of(q * 64 + 64, 64), 64), :]
            w = WN[0]
            ON[pl.ds(pl.multiple_of(q * 64, 64), 64), :] = v + w * (
                mix * w * total + 0.1 * (upper + lower - 2.0 * v)
            )
        return carry

    lax.fori_loop(0, NO, sea, 0)

    loads[5].wait()

    def split_o(i, carry):
        MOC[i] = split_cat(MO[i])
        MOT[i] = split_cat(jnp.transpose(MO[i]))
        MAT[i] = split_cat(jnp.transpose(MA[i]))
        return carry

    lax.fori_loop(0, 16, split_o, 0)

    loads[1].wait()

    def pack_first(f, carry):
        pack_atmos(S, rf_t, rf_b, kf, f)
        return carry

    lax.fori_loop(0, NF, pack_first, 0)
    full_halo = halo(FULL, rf_t, rf_b, kf, hf_a, hf_b, hf_l, hf_r, dev_down, dev_up)

    arrived(LABELS, NOTES.at[pl.ds(0, peers - 1)])
    notes = NOTES[:, 0, :]
    slots = pltpu.roll(notes, 112, 1)
    labels = []
    for c in range(2):
        hit = notes == (2 * me + c).astype(F32)
        of_e = jnp.sum(jnp.where(hit & (lane64 < 16), slots, 0.0), axis=1, keepdims=True) - 1.0
        of_o = jnp.sum(jnp.where(hit & (lane64 >= 32) & (lane64 < 48), slots, 0.0), axis=1, keepdims=True) - 1.0
        labels.append(jnp.where(lane64 < 64, of_o, of_e))
    lane128 = lax.broadcasted_iota(jnp.int32, (128, 128), 1)
    place = (lane128 - jnp.where(lane128 < 64, 0, 64)).astype(F32)
    chosen = (jnp.concatenate(labels, axis=0) == place).astype(F32)
    QM[...] = chosen.astype(BF16)
    PT[...] = jnp.transpose(chosen).astype(BF16)

    arrived(A1, R1.at[pl.ds(0, 14 * (peers - 1)), :])
    fields = [halves(PT[pl.ds(64, 16), :], split_cat(both_ranks(R1, f, 7, 16))) for f in range(7)]
    heat, salt, east, north, gain, fresh, shape = fields
    speed = jnp.sqrt(east * east + north * north + 0.5)
    flux = [
        speed * heat + gain,
        speed * salt + fresh,
        speed * east * (1.0 + 0.2 * jnp.tanh(shape)),
        speed * north,
    ]
    for g in range(8):
        FL[pl.ds(16 * g, 16), :] = flux[g % 4]
    for j in range(16):
        mapped[j] = quad(split_stack(FL[pl.ds(j, 8, stride=16), :]), MOC[j])

    def pack_mapped(n, carry):
        for m in range(8):
            t = n * 8 + m
            MSG2[pl.ds(pl.multiple_of(t * 8, 8), 8), :] = jnp.where(
                sub8 < 4, mapped[tab_s[1, 2 * t]], mapped[tab_s[1, 2 * t + 1]]
            )
        return carry

    lax.fori_loop(0, peers // 8, pack_mapped, 0)
    exchange(A2, 8, 8, MSG2, lambda m: R2.at[pl.ds(pl.multiple_of(m * 8, 8), 8), :])
    R2[mine8, :] = MSG2[mine8, :]

    for copy in full_halo:
        copy.wait_recv()

    def atmos_field(src, dst, from_a, from_b, from_l, from_r, f):
        d = diff[f]
        both = jnp.where(even16, from_l[f], pltpu.roll(from_r[f], 126, 1))
        for lev in range(LEV):
            v = src[f, pl.ds(16 * lev, 16), :]
            edge = pltpu.roll(both, (128 - 2 * lev) % 128, 1)
            left = jnp.where(lane16 == 0, edge, pltpu.roll(v, 1, 1))
            right = jnp.where(lane16 == 127, edge, pltpu.roll(v, 127, 1))
            above = jnp.where(row16 == 0, from_a[f, pl.ds(lev, 1), :], pltpu.roll(v, 1, 0))
            below = jnp.where(row16 == 15, from_b[f, pl.ds(lev, 1), :], pltpu.roll(v, 15, 0))
            upper = v if lev == 0 else src[f, pl.ds(16 * lev - 16, 16), :]
            lower = v if lev == LEV - 1 else src[f, pl.ds(16 * lev + 16, 16), :]
            dst[f, pl.ds(16 * lev, 16), :] = (
                v + d * (above + below + left + right - 4.0 * v) + 0.1 * (upper + lower - 2.0 * v)
            )

    def first_step(f, carry):
        atmos_field(S, A, hf_a, hf_b, hf_l, hf_r, f)
        pack_atmos(A, r2_t, r2_b, k2, f)
        return carry

    lax.fori_loop(0, NF, first_step, 0)

    arrived(A2, R2.at[pl.ds(0, 8 * (peers - 1)), :])
    for g in range(NO):
        FOR[pl.ds(64 * g, 64), :] = halves(PT[pl.ds(0, 64), :], split_cat(both_ranks(R2, g, 4, 8)))
    twin_copy = remote(FOR, FORIN, COMP, twin)
    zero64 = jnp.zeros((64, 256), BF16)
    for g in range(NO):
        TOPC[g, pl.ds(64, 64), :] = zero64
        OEC[g, pl.ds(0, 64), :] = zero64
        OEC[g, pl.ds(64, 64), :] = zero64
    twin_copy.wait_recv()
    for g in range(NO):
        rows = pl.ds(64 * OLEV * g, 64)
        plane = pl.ds(64 * g, 64)
        top = ON[rows, :] + WN[0] * (FORCING_SCALE[g] * (FOR[plane, :] + FORIN[plane, :]))
        ON[rows, :] = top
        TOPC[g, pl.ds(0, 64), :] = split_cat(top)
    for g in range(NO):
        put_ranks(ANS, g, halves(QM[...], TOPC[g]))
    exchange(A3, 8, 8, ANS, lambda m: B3.at[m])
    B3[me] = ANS[mine8, :]
    second_halo = halo(SECOND, r2_t, r2_b, k2, h2_a, h2_b, h2_l, h2_r, dev_down, dev_up)
    ocean_store = pltpu.make_async_copy(ON, ocean_out, out_sem.at[0])
    ocean_store.start()

    b3_all = B3.at[pl.ds(0, peers - 1)]
    arrived(A3, b3_all)
    for j in range(16):
        both = quad(split_stack(B3[o_owner[j]]), MOT[j])
        picked = jnp.where(o_rank[j] == 0, both, pltpu.roll(both, 4, 0))
        OE[pl.ds(j, 4, stride=16), :] = picked[0:4]
    for g in range(NO):
        OEC[g, pl.ds(64, 16), :] = split_cat(OE[pl.ds(16 * g, 16), :])
    for g in range(NO):
        put_ranks(REP, g, halves(QM[...], OEC[g]))
    exchange(A4, 8, 8, REP, lambda m: B4.at[m])
    B4[me] = REP[mine8, :]

    for copy in second_halo:
        copy.wait_recv()

    def second_step(f, carry):
        atmos_field(A, N, h2_a, h2_b, h2_l, h2_r, f)
        return carry

    lax.fori_loop(0, NF, second_step, 0)
    atmos_store = pltpu.make_async_copy(N, atmos_out, out_sem.at[1])
    atmos_store.start()

    arrived(A4, B4.at[pl.ds(0, peers - 1)])
    for i in range(16):
        both = quad(split_stack(B4[e_owner[i]]), MAT[i])
        picked = jnp.where(e_rank[i] == 0, both, pltpu.roll(both, 4, 0))
        OSV[pl.ds(i, 4, stride=16), :] = picked[0:4]
    surf_store = pltpu.make_async_copy(OSV, surf_out, out_sem.at[2])
    surf_store.start()

    for copy in surface_halo + full_halo + ocean_halo + second_halo + [twin_copy]:
        copy.wait_send()
    departed(A1, MSG.at[pl.ds(0, 14 * (peers - 1)), :])
    departed(LABELS, NOTES.at[pl.ds(0, peers - 1)])
    departed(A2, MSG2.at[pl.ds(0, 8 * (peers - 1)), :])
    departed(A3, ANS.at[pl.ds(0, 8 * (peers - 1)), :])
    departed(A4, REP.at[pl.ds(0, 8 * (peers - 1)), :])
    ocean_store.wait()
    atmos_store.wait()
    surf_store.wait()


def hand_out(a, b, c, a_out, b_out, c_out, sem):
    copies = [pltpu.make_async_copy(x, y, sem.at[n]) for n, (x, y) in enumerate([(a, a_out), (b, b_out), (c, c_out)])]
    for copy in copies:
        copy.start()
    for copy in copies:
        copy.wait()


def on_device(
    sizes,
    atmos_state, atmos_diffusion, remap_atmos, exchange_owner, exchange_slot,
    remap_ocean, ocean_owner, ocean_slot, ocean_state, ocean_mixing, wet_mask,
):
    NC, NX, NY, NF, LEV, NO, OLEV = sizes
    peers = NX * NY
    hbm = pl.BlockSpec(memory_space=pltpu.HBM)
    any_ = pl.BlockSpec(memory_space=pl.ANY)

    def vm(*shape, dtype=F32):
        return pltpu.VMEM(shape, dtype)

    halo_atmos = [vm(NF, 24, 128), vm(NF, 24, 128), vm(NF, 16, 128), vm(NF, 24, 128), vm(NF, 24, 128), vm(NF, 16, 128), vm(NF, 16, 128)]
    scratch = (
        [vm(NF, 16 * LEV, 128) for _ in range(3)]
        + [vm(16, 128, 128), vm(16, 128, 128)]
        + [vm(16, 128, 256, dtype=BF16) for _ in range(4)]
        + [vm(NO * OLEV * 64, 128), vm(NO * OLEV * 64, 128), vm(64, 128, dtype=jnp.int32), vm(5, 64, 128)]
        + [vm(16, 128) for _ in range(7)]
        + halo_atmos
        + halo_atmos
        + [vm(40, 128), vm(40, 128), vm(64, 128), vm(40, 128), vm(40, 128), vm(64, 128), vm(64, 128)]
        + [vm(1, 1, 128), vm(peers, 1, 128), vm(128, 128), vm(16, 8, 128), vm(16, 8, 128), vm(16 * peers, 128), vm(16 * peers, 128)]
        + [vm(128, 128, dtype=BF16), vm(128, 128, dtype=BF16), vm(128, 128), vm(16, 8, 128)]
        + [vm(8 * peers, 128), vm(8 * peers, 128), vm(256, 128), vm(256, 128)]
        + [vm(NO, 128, 256, dtype=BF16), vm(8 * peers, 128), vm(peers, 8, 128), vm(64, 128)]
        + [vm(NO, 128, 256, dtype=BF16), vm(8 * peers, 128), vm(peers, 8, 128), vm(64, 128)]
        + [pltpu.SMEM((NF,), F32)] + [pltpu.SMEM((16,), jnp.int32) for _ in range(4)] + [pltpu.SMEM((NO,), F32)]
        + [vm(8, 128, dtype=jnp.int32), pltpu.SMEM((8, 128), jnp.int32)]
        + [
            pltpu.SemaphoreType.DMA((12,)),
            pltpu.SemaphoreType.DMA((3,)),
            pltpu.SemaphoreType.DMA((1,)),
            pltpu.SemaphoreType.DMA((SEMS,)),
            pltpu.SemaphoreType.DMA((SEMS,)),
            pltpu.SemaphoreType.REGULAR((1,)),
        ]
    )
    atmos_next, ocean_next, surface = pl.pallas_call(
        functools.partial(kernel, sizes),
        out_shape=(
            jax.ShapeDtypeStruct((NF, 16 * LEV, 128), F32),
            jax.ShapeDtypeStruct((NO * OLEV * 64, 128), F32),
            jax.ShapeDtypeStruct((64, 128), F32),
        ),
        in_specs=[hbm] * 11,
        out_specs=(any_, any_, any_),
        scratch_shapes=scratch,
        compiler_params=pltpu.CompilerParams(
            collective_id=0, has_side_effects=True, vmem_limit_bytes=40 * 1024 * 1024
        ),
    )(*(pltpu.with_memory_space_constraint(x, pltpu.HBM) for x in (
        atmos_state.reshape(NF, 16 * LEV, 128),
        remap_atmos,
        remap_ocean,
        ocean_state.reshape(NO * OLEV * 64, 128),
        wet_mask,
        atmos_diffusion, exchange_owner.reshape(16), exchange_slot, ocean_owner.reshape(16), ocean_slot, ocean_mixing,
    )))
    results = (atmos_next, ocean_next, surface)
    atmos_next, ocean_next, surface = pl.pallas_call(
        hand_out,
        out_shape=tuple(jax.ShapeDtypeStruct(x.shape, x.dtype) for x in results),
        in_specs=[any_] * 3,
        out_specs=(hbm, hbm, hbm),
        scratch_shapes=[pltpu.SemaphoreType.DMA((3,))],
        compiler_params=pltpu.CompilerParams(vmem_limit_bytes=1024 * 1024),
    )(*results)
    return (
        atmos_next.reshape(NF, LEV, 16, 128),
        ocean_next.reshape(NO, OLEV, 64, 128),
        surface.reshape(NO, 16, 128),
    )


def solution(mesh):
    sizes = (mesh.shape["comp"], mesh.shape["gx"], mesh.shape["gy"], 10, 20, 4, 8)
    in_specs = (
        P(None, None, ("comp", "gx"), "gy"),
        P(),
        P(("comp", "gx", "gy"), None, None),
        P(("comp", "gx", "gy"), None),
        P(("comp", "gx", "gy")),
        P(("comp", "gx", "gy"), None, None),
        P(("comp", "gx", "gy"), None),
        P(("comp", "gx", "gy")),
        P(None, None, "gx", "gy"),
        P(),
        P("gx", "gy"),
    )
    out_specs = (
        P(None, None, ("comp", "gx"), "gy"),
        P(None, None, "gx", "gy"),
        P(None, ("comp", "gx"), "gy"),
    )
    return jax.shard_map(
        functools.partial(on_device, sizes), mesh=mesh, in_specs=in_specs, out_specs=out_specs, check_vma=False
    )
```

```python
import functools

import jax
import jax.numpy as jnp
from jax import lax
from jax.experimental import pallas as pl
from jax.experimental.pallas import tpu as pltpu
from jax.sharding import PartitionSpec as P

MESH = pl.DeviceIdType.MESH
F32 = jnp.float32
BF16 = jnp.bfloat16
FORCING_SCALE = (0.1, -0.1, 0.1, 0.1)

SURF, FULL, SECOND, OCEAN, COMP, A1, A2, A3, A4, LABELS = 0, 4, 8, 12, 16, 17, 18, 19, 20, 21
SEMS = 22


def far_first(nx, ny):
    def way(n, offset, flip):
        total = 0
        for at in range(n):
            to = (at + offset) % n
            ahead = (to - at) % 4
            total = max(total, min(ahead, 4 - ahead) + flip * (to // 4 != at // 4))
        return total

    return sorted(range(1, nx * ny), key=lambda k: (-way(nx, k // ny, 2), -way(ny, k % ny, 1), k))


def split_cat(x):
    hi = x.astype(BF16)
    lo = (x - hi.astype(F32)).astype(BF16)
    return jnp.concatenate([hi, lo], axis=1)


def split_stack(x):
    hi = x.astype(BF16).astype(F32)
    return jnp.concatenate([hi, x - hi], axis=0).astype(BF16)


def dot(a, b):
    return jnp.dot(a, b, preferred_element_type=F32)


def quad(lhs, cat):
    full = dot(lhs, cat)
    return (full[:8, :128] + full[8:, :128]) + (full[:8, 128:] + full[8:, 128:])


def both_ranks(ref, first, apart, stride):
    return jnp.concatenate([ref[pl.ds(first + apart * c, 64, stride=stride), :] for c in range(2)], axis=0)


def put_ranks(ref, g, rows):
    for c in range(2):
        ref[pl.ds(g + 4 * c, 64, stride=8), :] = rows[64 * c : 64 * c + 64]


def halves(lhs, cat):
    full = dot(lhs, cat)
    return full[:, :128] + full[:, 128:]


def kernel(
    sizes,
    state, remap_a, remap_o, ocean, wet_in,
    diff_in, e_owner_in, e_slot_in, o_owner_in, o_slot_in, mixing_in,
    atmos_out, ocean_out, surf_out,
    S, A, N, MA, MO, MAC, MOC, MAT, MOT, O, ON, W, WN,
    rs_t, rs_b, ks, hs_a, hs_b, hs_l, hs_r,
    rf_t, rf_b, kf, hf_a, hf_b, hf_l, hf_r,
    r2_t, r2_b, k2, h2_a, h2_b, h2_l, h2_r,
    ro_t, ro_b, ko, ho_a, ho_b, ho_l, ho_r,
    NOTE, NOTES, X, pieces, shifted, MSG, R1, QM, PT, FL, mapped, MSG2, R2, FOR, FORIN,
    TOPC, ANS, B3, OE, OEC, REP, B4,
    diff, e_owner, e_slot, o_owner, o_slot, mixing,
    tab_v, tab_s,
    in_sem, out_sem, tab_sem, send, recv, row_here,
):
    NC, NX, NY, NF, LEV, NO, OLEV = sizes
    peers = NX * NY
    comp, gx, gy = lax.axis_index("comp"), lax.axis_index("gx"), lax.axis_index("gy")
    me = gx * NY + gy
    pos = comp * NX + gx
    ring = NC * NX
    down, up = lax.rem(pos + 1, ring), lax.rem(pos + ring - 1, ring)
    dev_down = (down // NX, lax.rem(down, NX), gy)
    dev_up = (up // NX, lax.rem(up, NX), gy)
    dev_right = (comp, gx, lax.rem(gy + 1, NY))
    dev_left = (comp, gx, lax.rem(gy + NY - 1, NY))
    sea_down = (comp, lax.rem(gx + 1, NX), gy)
    sea_up = (comp, lax.rem(gx + NX - 1, NX), gy)
    twin = (lax.rem(comp + 1, NC), gx, gy)

    def peer(k):
        px = lax.rem(gx + k // NY, NX)
        py = lax.rem(gy + lax.rem(k, NY), NY)
        return px, py, px * NY + py

    top_rows = 16 * (LEV - 2)
    loads = [
        pltpu.make_async_copy(state.at[:, pl.ds(top_rows, 32), :], S.at[:, pl.ds(top_rows, 32), :], in_sem.at[0]),
        pltpu.make_async_copy(state.at[:, pl.ds(0, top_rows), :], S.at[:, pl.ds(0, top_rows), :], in_sem.at[1]),
        pltpu.make_async_copy(ocean, O, in_sem.at[2]),
        pltpu.make_async_copy(wet_in, W, in_sem.at[3]),
        pltpu.make_async_copy(remap_a, MA, in_sem.at[4]),
        pltpu.make_async_copy(remap_o, MO, in_sem.at[5]),
    ]
    small = [
        pltpu.make_async_copy(src, dst, in_sem.at[6 + n])
        for n, (src, dst) in enumerate([
            (e_owner_in, e_owner), (o_owner_in, o_owner), (e_slot_in, e_slot), (o_slot_in, o_slot),
            (diff_in, diff), (mixing_in, mixing),
        ])
    ]
    loads[0].start()

    barrier = pltpu.get_barrier_semaphore()

    row_peers = [(comp, gx, lax.rem(gy + b, NY)) for b in range(1, NY)]
    column_peers = [(comp, lax.rem(gx + a, NX), gy) for a in range(1, NX)]
    greeted = row_peers + column_peers + [dev_down, dev_up, twin]
    for other in greeted:
        pl.semaphore_signal(barrier, inc=1, device_id=other, device_id_type=MESH)

    for load in small + loads[1:]:
        load.start()

    lane16 = lax.broadcasted_iota(jnp.int32, (16, 128), 1)
    row16 = lax.broadcasted_iota(jnp.int32, (16, 128), 0)
    pair16 = lane16 // 2
    even16 = lane16 == pair16 * 2
    sub8 = lax.broadcasted_iota(jnp.int32, (8, 128), 0)

    def remote(src, dst, number, device):
        copy = pltpu.make_async_remote_copy(
            src_ref=src, dst_ref=dst, send_sem=send.at[number], recv_sem=recv.at[number],
            device_id=device, device_id_type=MESH,
        )
        copy.start()
        return copy

    def halo(number, rows_t, rows_b, cols, from_a, from_b, from_l, from_r, below, above):
        if len(rows_b.shape) == 3:
            used = pl.ds(0, LEV)
            rows_t, rows_b, from_a, from_b = (ref.at[:, used, :] for ref in (rows_t, rows_b, from_a, from_b))
        return [
            remote(rows_b, from_a, number, below),
            remote(rows_t, from_b, number + 1, above),
            remote(cols, from_l, number + 2, dev_right),
            remote(cols, from_r, number + 3, dev_left),
        ]

    loads[0].wait()
    last = 16 * (LEV - 1)
    packed = jnp.zeros((16, 128), F32)
    for f in range(NF):
        v = S[f, pl.ds(last, 16), :]
        packed = jnp.where(pair16 == f, pltpu.roll(v, 2 * f + 1, 1), packed)
        rs_t[pl.ds(f, 1), :] = v[0:1]
        rs_b[pl.ds(f, 1), :] = v[15:16]
    ks[...] = packed
    pl.semaphore_wait(barrier, len(greeted))
    surface_halo = halo(SURF, rs_t, rs_b, ks, hs_a, hs_b, hs_l, hs_r, dev_down, dev_up)
    for other in column_peers:
        pl.semaphore_signal(row_here.at[0], inc=1, device_id=other, device_id_type=MESH)

    def places(owner):
        ranks, keys = [], []
        for i in range(16):
            rank = jnp.int32(0)
            for j in range(i):
                rank = rank + (owner[j] == owner[i]).astype(jnp.int32)
            ranks.append(rank)
            keys.append(2 * owner[i] + rank)
        return ranks, keys

    for load in small:
        load.wait()
    e_rank, e_key = places(e_owner)
    o_rank, o_key = places(o_owner)
    lane8 = lax.broadcasted_iota(jnp.int32, (8, 128), 1)
    table = jnp.zeros((8, 128), jnp.int32)
    for i in range(16):
        table = jnp.where(lane8 == jnp.where(sub8 == 0, e_key[i], o_key[i]), i, table)
    tab_v[...] = table
    tab_copy = pltpu.make_async_copy(tab_v, tab_s, tab_sem.at[0])
    tab_copy.start()

    def pack_atmos(src, rows_t, rows_b, cols, f):
        kept = jnp.zeros((16, 128), F32)
        for lev in range(LEV):
            v = src[f, pl.ds(16 * lev, 16), :]
            kept = jnp.where(pair16 == lev, pltpu.roll(v, 2 * lev + 1, 1), kept)
        cols[f] = kept
        rows_t[f, pl.ds(0, LEV), :] = src[f, pl.ds(0, LEV, stride=16), :]
        rows_b[f, pl.ds(0, LEV), :] = src[f, pl.ds(15, LEV, stride=16), :]

    loads[2].wait()
    loads[3].wait()
    planes = NO * OLEV
    lane64 = lax.broadcasted_iota(jnp.int32, (64, 128), 1)
    row64 = lax.broadcasted_iota(jnp.int32, (64, 128), 0)
    pair64 = lane64 // 2
    wet = W[...].astype(F32)
    WN[0] = wet
    kept = jnp.where(pair64 == planes, pltpu.roll(wet, 2 * planes + 1, 1), 0.0)
    ko[...] = kept
    ro_t[pl.ds(planes, 1), :] = wet[0:1]
    ro_b[pl.ds(planes, 1), :] = wet[63:64]

    def pack_ocean(f, carry):
        kept = ko[...]
        for lev in range(OLEV):
            q = f * OLEV + lev
            v = O[pl.ds(pl.multiple_of(q * 64, 64), 64), :]
            kept = jnp.where(pair64 == q, pltpu.roll(v, 2 * q + 1, 1), kept)
        ko[...] = kept
        return carry

    lax.fori_loop(0, NO, pack_ocean, 0)
    ro_t[pl.ds(0, planes), :] = O[pl.ds(0, planes, stride=64), :]
    ro_b[pl.ds(0, planes), :] = O[pl.ds(63, planes, stride=64), :]
    ocean_halo = halo(OCEAN, ro_t, ro_b, ko, ho_a, ho_b, ho_l, ho_r, sea_down, sea_up)

    loads[4].wait()

    def split_a(i, carry):
        MAC[i] = split_cat(MA[i])
        return carry

    lax.fori_loop(0, 16, split_a, 0)

    lane1 = lax.broadcasted_iota(jnp.int32, (1, 128), 1)
    row = jnp.zeros((1, 128), jnp.int32)
    for i in range(16):
        for at, value in ((0, e_key[i]), (16, e_slot[i] + 1), (32, o_key[i]), (48, o_slot[i] + 1)):
            row = jnp.where(lane1 == at + i, value, row)
    NOTE[0] = row.astype(F32)
    NOTES[me] = row.astype(F32)
    pl.semaphore_wait(row_here.at[0], NX - 1)
    for k in far_first(NX, NY):
        px, py, _ = peer(k)
        remote(NOTE.at[0], NOTES.at[me], LABELS, (comp, px, py))

    tab_copy.wait()
    for copy in surface_halo:
        copy.wait_recv()
    kl, kr = hs_l[...], hs_r[...]
    cols = jnp.where(even16, kl, pltpu.roll(kr, 126, 1))
    after = []
    for f in range(NF):
        v = S[f, pl.ds(last, 16), :]
        edge = pltpu.roll(cols, (128 - 2 * f) % 128, 1)
        left = jnp.where(lane16 == 0, edge, pltpu.roll(v, 1, 1))
        right = jnp.where(lane16 == 127, edge, pltpu.roll(v, 127, 1))
        above = jnp.where(row16 == 0, hs_a[pl.ds(f, 1), :], pltpu.roll(v, 1, 0))
        below = jnp.where(row16 == 15, hs_b[pl.ds(f, 1), :], pltpu.roll(v, 15, 0))
        upper = S[f, pl.ds(last - 16, 16), :]
        after.append(v + diff[f] * (above + below + left + right - 4.0 * v) + 0.1 * (upper - v))
    combined = [after[0] - after[4], after[1], after[2], after[3], after[6] + after[7], after[5] + after[8], after[9], after[9]]
    for f in range(8):
        X[pl.ds(16 * f, 16), :] = combined[f]
    for i in range(16):
        piece = quad(split_stack(X[pl.ds(i, 8, stride=16), :]), MAC[i])
        pieces[i] = piece
        shifted[i] = pltpu.roll(piece, 7, 0)

    def pack_pieces(n, carry):
        for m in range(4):
            t = n * 4 + m
            one, two = pieces[tab_s[0, 2 * t]], shifted[tab_s[0, 2 * t + 1]]
            MSG[pl.ds(pl.multiple_of(t * 16, 16), 8), :] = jnp.where(sub8 < 7, one, two)
            MSG[pl.ds(pl.multiple_of(t * 16 + 8, 8), 8), :] = two
        return carry

    lax.fori_loop(0, 16, pack_pieces, 0)

    def exchange(number, rows, sent, src, dst_of):
        def step(k, carry):
            px, py, target = peer(k)
            remote(src.at[pl.ds(pl.multiple_of(target * rows, 8), sent), :], dst_of(me), number, (comp, px, py))
            return carry

        for k in far_first(NX, NY):
            step(k, 0)

    def arrived(number, count_ref):
        pltpu.make_async_copy(count_ref, count_ref, recv.at[number]).wait()

    def departed(number, count_ref):
        pltpu.make_async_copy(count_ref, count_ref, send.at[number]).wait()

    mine16 = pl.ds(pl.multiple_of(me * 16, 16), 16)
    mine8 = pl.ds(pl.multiple_of(me * 8, 8), 8)
    exchange(A1, 16, 14, MSG, lambda m: R1.at[pl.ds(pl.multiple_of(m * 16, 16), 14), :])
    R1[mine16, :] = MSG[mine16, :]

    for copy in ocean_halo:
        copy.wait_recv()
    ol, orr = ho_l[...], ho_r[...]
    even64 = lane64 == pair64 * 2
    ho_l[...] = jnp.where(even64, ol, pltpu.roll(orr, 126, 1))

    def around(v, q, edges):
        edge = pltpu.roll(edges, 128 - 2 * q, 1)
        left = jnp.where(lane64 == 0, edge, pltpu.roll(v, 1, 1))
        right = jnp.where(lane64 == 127, edge, pltpu.roll(v, 127, 1))
        above = jnp.where(row64 == 0, ho_a[pl.ds(q, 1), :], pltpu.roll(v, 1, 0))
        below = jnp.where(row64 == 63, ho_b[pl.ds(q, 1), :], pltpu.roll(v, 63, 0))
        return above, below, left, right

    for n, w in enumerate(around(wet, planes, ho_l[...])):
        WN[1 + n] = w

    def sea(f, carry):
        mix = mixing[f]
        base = f * OLEV
        for lev in range(OLEV):
            q = base + lev
            v = O[pl.ds(pl.multiple_of(q * 64, 64), 64), :]
            total = jnp.zeros((64, 128), F32)
            edges = pltpu.roll(ho_l[...], 128 - 2 * q, 1)
            left = jnp.where(lane64 == 0, edges, pltpu.roll(v, 1, 1))
            right = jnp.where(lane64 == 127, edges, pltpu.roll(v, 127, 1))
            above = jnp.where(row64 == 0, ho_a[pl.ds(q, 1), :], pltpu.roll(v, 1, 0))
            below = jnp.where(row64 == 63, ho_b[pl.ds(q, 1), :], pltpu.roll(v, 63, 0))
            total = WN[1] * (above - v) + WN[2] * (below - v) + WN[3] * (left - v) + WN[4] * (right - v)
            upper = v if lev == 0 else O[pl.ds(pl.multiple_of(q * 64 - 64, 64), 64), :]
            lower = v if lev == OLEV - 1 else O[pl.ds(pl.multiple_of(q * 64 + 64, 64), 64), :]
            w = WN[0]
            ON[pl.ds(pl.multiple_of(q * 64, 64), 64), :] = v + w * (
                mix * w * total + 0.1 * (upper + lower - 2.0 * v)
            )
        return carry

    lax.fori_loop(0, NO, sea, 0)

    loads[5].wait()

    def split_o(i, carry):
        MOC[i] = split_cat(MO[i])
        MOT[i] = split_cat(jnp.transpose(MO[i]))
        MAT[i] = split_cat(jnp.transpose(MA[i]))
        return carry

    lax.fori_loop(0, 16, split_o, 0)

    loads[1].wait()

    def pack_first(f, carry):
        pack_atmos(S, rf_t, rf_b, kf, f)
        return carry

    lax.fori_loop(0, NF, pack_first, 0)
    full_halo = halo(FULL, rf_t, rf_b, kf, hf_a, hf_b, hf_l, hf_r, dev_down, dev_up)

    arrived(LABELS, NOTES.at[pl.ds(0, peers - 1)])
    notes = NOTES[:, 0, :]
    slots = pltpu.roll(notes, 112, 1)
    labels = []
    for c in range(2):
        hit = notes == (2 * me + c).astype(F32)
        of_e = jnp.sum(jnp.where(hit & (lane64 < 16), slots, 0.0), axis=1, keepdims=True) - 1.0
        of_o = jnp.sum(jnp.where(hit & (lane64 >= 32) & (lane64 < 48), slots, 0.0), axis=1, keepdims=True) - 1.0
        labels.append(jnp.where(lane64 < 64, of_o, of_e))
    lane128 = lax.broadcasted_iota(jnp.int32, (128, 128), 1)
    place = (lane128 - jnp.where(lane128 < 64, 0, 64)).astype(F32)
    chosen = (jnp.concatenate(labels, axis=0) == place).astype(F32)
    QM[...] = chosen.astype(BF16)
    PT[...] = jnp.transpose(chosen).astype(BF16)

    arrived(A1, R1.at[pl.ds(0, 14 * (peers - 1)), :])
    fields = [halves(PT[pl.ds(64, 16), :], split_cat(both_ranks(R1, f, 7, 16))) for f in range(7)]
    heat, salt, east, north, gain, fresh, shape = fields
    speed = jnp.sqrt(east * east + north * north + 0.5)
    flux = [
        speed * heat + gain,
        speed * salt + fresh,
        speed * east * (1.0 + 0.2 * jnp.tanh(shape)),
        speed * north,
    ]
    for g in range(8):
        FL[pl.ds(16 * g, 16), :] = flux[g % 4]
    for j in range(16):
        mapped[j] = quad(split_stack(FL[pl.ds(j, 8, stride=16), :]), MOC[j])

    def pack_mapped(n, carry):
        for m in range(8):
            t = n * 8 + m
            MSG2[pl.ds(pl.multiple_of(t * 8, 8), 8), :] = jnp.where(
                sub8 < 4, mapped[tab_s[1, 2 * t]], mapped[tab_s[1, 2 * t + 1]]
            )
        return carry

    lax.fori_loop(0, peers // 8, pack_mapped, 0)
    exchange(A2, 8, 8, MSG2, lambda m: R2.at[pl.ds(pl.multiple_of(m * 8, 8), 8), :])
    R2[mine8, :] = MSG2[mine8, :]

    for copy in full_halo:
        copy.wait_recv()

    def atmos_field(src, dst, from_a, from_b, from_l, from_r, f):
        d = diff[f]
        both = jnp.where(even16, from_l[f], pltpu.roll(from_r[f], 126, 1))
        for lev in range(LEV):
            v = src[f, pl.ds(16 * lev, 16), :]
            edge = pltpu.roll(both, (128 - 2 * lev) % 128, 1)
            left = jnp.where(lane16 == 0, edge, pltpu.roll(v, 1, 1))
            right = jnp.where(lane16 == 127, edge, pltpu.roll(v, 127, 1))
            above = jnp.where(row16 == 0, from_a[f, pl.ds(lev, 1), :], pltpu.roll(v, 1, 0))
            below = jnp.where(row16 == 15, from_b[f, pl.ds(lev, 1), :], pltpu.roll(v, 15, 0))
            upper = v if lev == 0 else src[f, pl.ds(16 * lev - 16, 16), :]
            lower = v if lev == LEV - 1 else src[f, pl.ds(16 * lev + 16, 16), :]
            dst[f, pl.ds(16 * lev, 16), :] = (
                v + d * (above + below + left + right - 4.0 * v) + 0.1 * (upper + lower - 2.0 * v)
            )

    def first_step(f, carry):
        atmos_field(S, A, hf_a, hf_b, hf_l, hf_r, f)
        pack_atmos(A, r2_t, r2_b, k2, f)
        return carry

    lax.fori_loop(0, NF, first_step, 0)

    arrived(A2, R2.at[pl.ds(0, 8 * (peers - 1)), :])
    for g in range(NO):
        FOR[pl.ds(64 * g, 64), :] = halves(PT[pl.ds(0, 64), :], split_cat(both_ranks(R2, g, 4, 8)))
    twin_copy = remote(FOR, FORIN, COMP, twin)
    zero64 = jnp.zeros((64, 256), BF16)
    for g in range(NO):
        TOPC[g, pl.ds(64, 64), :] = zero64
        OEC[g, pl.ds(0, 64), :] = zero64
        OEC[g, pl.ds(64, 64), :] = zero64
    twin_copy.wait_recv()
    for g in range(NO):
        rows = pl.ds(64 * OLEV * g, 64)
        plane = pl.ds(64 * g, 64)
        top = ON[rows, :] + WN[0] * (FORCING_SCALE[g] * (FOR[plane, :] + FORIN[plane, :]))
        ON[rows, :] = top
        TOPC[g, pl.ds(0, 64), :] = split_cat(top)
    for g in range(NO):
        put_ranks(ANS, g, halves(QM[...], TOPC[g]))
    exchange(A3, 8, 8, ANS, lambda m: B3.at[m])
    B3[me] = ANS[mine8, :]
    second_halo = halo(SECOND, r2_t, r2_b, k2, h2_a, h2_b, h2_l, h2_r, dev_down, dev_up)
    ocean_store = pltpu.make_async_copy(ON, ocean_out, out_sem.at[0])
    ocean_store.start()

    b3_all = B3.at[pl.ds(0, peers - 1)]
    arrived(A3, b3_all)
    for j in range(16):
        both = quad(split_stack(B3[o_owner[j]]), MOT[j])
        picked = jnp.where(o_rank[j] == 0, both, pltpu.roll(both, 4, 0))
        OE[pl.ds(j, 4, stride=16), :] = picked[0:4]
    for g in range(NO):
        OEC[g, pl.ds(64, 16), :] = split_cat(OE[pl.ds(16 * g, 16), :])
    for g in range(NO):
        put_ranks(REP, g, halves(QM[...], OEC[g]))
    exchange(A4, 8, 8, REP, lambda m: B4.at[m])
    B4[me] = REP[mine8, :]

    for copy in second_halo:
        copy.wait_recv()

    def second_step(f, carry):
        atmos_field(A, N, h2_a, h2_b, h2_l, h2_r, f)
        return carry

    lax.fori_loop(0, NF, second_step, 0)
    atmos_store = pltpu.make_async_copy(N, atmos_out, out_sem.at[1])
    atmos_store.start()

    arrived(A4, B4.at[pl.ds(0, peers - 1)])
    for i in range(16):
        both = quad(split_stack(B4[e_owner[i]]), MAT[i])
        picked = jnp.where(e_rank[i] == 0, both, pltpu.roll(both, 4, 0))
        surf_out[pl.ds(i, 4, stride=16), :] = picked[0:4]

    for copy in surface_halo + full_halo + ocean_halo + second_halo + [twin_copy]:
        copy.wait_send()
    departed(A1, MSG.at[pl.ds(0, 14 * (peers - 1)), :])
    departed(LABELS, NOTES.at[pl.ds(0, peers - 1)])
    departed(A2, MSG2.at[pl.ds(0, 8 * (peers - 1)), :])
    departed(A3, ANS.at[pl.ds(0, 8 * (peers - 1)), :])
    departed(A4, REP.at[pl.ds(0, 8 * (peers - 1)), :])
    ocean_store.wait()
    atmos_store.wait()


def hand_out(a, b, c, a_out, b_out, c_out, sem):
    copies = [pltpu.make_async_copy(x, y, sem.at[n]) for n, (x, y) in enumerate([(a, a_out), (b, b_out), (c, c_out)])]
    for copy in copies:
        copy.start()
    for copy in copies:
        copy.wait()


def on_device(
    sizes,
    atmos_state, atmos_diffusion, remap_atmos, exchange_owner, exchange_slot,
    remap_ocean, ocean_owner, ocean_slot, ocean_state, ocean_mixing, wet_mask,
):
    NC, NX, NY, NF, LEV, NO, OLEV = sizes
    peers = NX * NY
    hbm = pl.BlockSpec(memory_space=pltpu.HBM)
    any_ = pl.BlockSpec(memory_space=pl.ANY)

    def vm(*shape, dtype=F32):
        return pltpu.VMEM(shape, dtype)

    halo_atmos = [vm(NF, 24, 128), vm(NF, 24, 128), vm(NF, 16, 128), vm(NF, 24, 128), vm(NF, 24, 128), vm(NF, 16, 128), vm(NF, 16, 128)]
    scratch = (
        [vm(NF, 16 * LEV, 128) for _ in range(3)]
        + [vm(16, 128, 128), vm(16, 128, 128)]
        + [vm(16, 128, 256, dtype=BF16) for _ in range(4)]
        + [vm(NO * OLEV * 64, 128), vm(NO * OLEV * 64, 128), vm(64, 128, dtype=jnp.int32), vm(5, 64, 128)]
        + [vm(16, 128) for _ in range(7)]
        + halo_atmos
        + halo_atmos
        + [vm(40, 128), vm(40, 128), vm(64, 128), vm(40, 128), vm(40, 128), vm(64, 128), vm(64, 128)]
        + [vm(1, 1, 128), vm(peers, 1, 128), vm(128, 128), vm(16, 8, 128), vm(16, 8, 128), vm(16 * peers, 128), vm(16 * peers, 128)]
        + [vm(128, 128, dtype=BF16), vm(128, 128, dtype=BF16), vm(128, 128), vm(16, 8, 128)]
        + [vm(8 * peers, 128), vm(8 * peers, 128), vm(256, 128), vm(256, 128)]
        + [vm(NO, 128, 256, dtype=BF16), vm(8 * peers, 128), vm(peers, 8, 128), vm(64, 128)]
        + [vm(NO, 128, 256, dtype=BF16), vm(8 * peers, 128), vm(peers, 8, 128)]
        + [pltpu.SMEM((NF,), F32)] + [pltpu.SMEM((16,), jnp.int32) for _ in range(4)] + [pltpu.SMEM((NO,), F32)]
        + [vm(8, 128, dtype=jnp.int32), pltpu.SMEM((8, 128), jnp.int32)]
        + [
            pltpu.SemaphoreType.DMA((12,)),
            pltpu.SemaphoreType.DMA((3,)),
            pltpu.SemaphoreType.DMA((1,)),
            pltpu.SemaphoreType.DMA((SEMS,)),
            pltpu.SemaphoreType.DMA((SEMS,)),
            pltpu.SemaphoreType.REGULAR((1,)),
        ]
    )
    atmos_next, ocean_next, surface = pl.pallas_call(
        functools.partial(kernel, sizes),
        out_shape=(
            jax.ShapeDtypeStruct((NF, 16 * LEV, 128), F32),
            jax.ShapeDtypeStruct((NO * OLEV * 64, 128), F32),
            jax.ShapeDtypeStruct((64, 128), F32),
        ),
        in_specs=[hbm] * 11,
        out_specs=(any_, any_, pl.BlockSpec(memory_space=pltpu.VMEM)),
        scratch_shapes=scratch,
        compiler_params=pltpu.CompilerParams(
            collective_id=0, has_side_effects=True, vmem_limit_bytes=40 * 1024 * 1024
        ),
    )(*(pltpu.with_memory_space_constraint(x, pltpu.HBM) for x in (
        atmos_state.reshape(NF, 16 * LEV, 128),
        remap_atmos,
        remap_ocean,
        ocean_state.reshape(NO * OLEV * 64, 128),
        wet_mask,
        atmos_diffusion, exchange_owner.reshape(16), exchange_slot, ocean_owner.reshape(16), ocean_slot, ocean_mixing,
    )))
    results = (atmos_next, ocean_next, surface)
    atmos_next, ocean_next, surface = pl.pallas_call(
        hand_out,
        out_shape=tuple(jax.ShapeDtypeStruct(x.shape, x.dtype) for x in results),
        in_specs=[any_] * 3,
        out_specs=(hbm, hbm, hbm),
        scratch_shapes=[pltpu.SemaphoreType.DMA((3,))],
        compiler_params=pltpu.CompilerParams(vmem_limit_bytes=1024 * 1024),
    )(*results)
    return (
        atmos_next.reshape(NF, LEV, 16, 128),
        ocean_next.reshape(NO, OLEV, 64, 128),
        surface.reshape(NO, 16, 128),
    )


def solution(mesh):
    sizes = (mesh.shape["comp"], mesh.shape["gx"], mesh.shape["gy"], 10, 20, 4, 8)
    in_specs = (
        P(None, None, ("comp", "gx"), "gy"),
        P(),
        P(("comp", "gx", "gy"), None, None),
        P(("comp", "gx", "gy"), None),
        P(("comp", "gx", "gy")),
        P(("comp", "gx", "gy"), None, None),
        P(("comp", "gx", "gy"), None),
        P(("comp", "gx", "gy")),
        P(None, None, "gx", "gy"),
        P(),
        P("gx", "gy"),
    )
    out_specs = (
        P(None, None, ("comp", "gx"), "gy"),
        P(None, None, "gx", "gy"),
        P(None, ("comp", "gx"), "gy"),
    )
    return jax.shard_map(
        functools.partial(on_device, sizes), mesh=mesh, in_specs=in_specs, out_specs=out_specs, check_vma=False
    )
```
